32 devices in a mesh: layer: 8 (over y, x, core), dp: 4 (over z).
Axes of the slice: x: 2, y: 2, z: 4, core: 2. Of those that a mesh axis runs over, the one named last changes fastest.
Arguments:
- activations: bfloat16 [8, 1024, 2048], P('layer', 'dp')
- factor_old: float32 [8, 2048, 2048], P('layer', 'dp'), as said below
- cross_old: float32 [8, 2048, 2048], P('layer', 'dp')
- gradients: bfloat16 [8, 2048, 1024], P('layer', 'dp'), may hold values from -6 to 6
- moments: bfloat16 [8, 2048, 1024], P('layer', 'dp'), may hold values from -6 to 6
- exponents: int32 [8, 16], P('layer', 'dp'), may hold values from -3 to 2
- master: float32 [8, 2048, 1024], P('layer', 'dp'), may hold values from -6 to 6
Outputs:
- factor_new: float32 [8, 2048, 2048], P('layer', 'dp')
- cross_new: float32 [8, 2048, 2048], P('layer', 'dp')
- moments_new: bfloat16 [8, 2048, 1024], P('layer', 'dp')
- master_new: float32 [8, 2048, 1024], P('layer', 'dp')
- replicas: bfloat16 [8, 2048, 1024], P('layer')
The draws below stay inside these ranges and needn't reach their ends.
Inputs may be any that keep to these rules, and one draw needn't show every extreme that they name: factor_old is symmetric in its last two dimensions, and its diagonal entries lie between 0.6 and 1.4.
All inputs are finite; a program needn't handle non-finite values.
Results may differ from the reference program's by a relative error of at most 0.0025.
Values may be sent and summed in bfloat16 or wider, within the bound.
A program may use at most 128 MiB of HBM per device.

```python
import jax
import jax.numpy as jnp
from jax import lax

FEATURES = 2048
OUTPUTS = 1024
SCALE_BLOCK = 128
LAYERS = 8
TOKENS = 1024


def draw_activations(key, part):
    subkeys = jax.random.split(jax.random.fold_in(key, 101), 2)
    persist = jax.random.uniform(subkeys[0], (FEATURES,), jnp.float32, 0.3, 0.95)
    noise = jax.random.normal(subkeys[1], (LAYERS, TOKENS, FEATURES), jnp.float32)
    renewal = jnp.sqrt(1.0 - persist * persist)

    def advance(previous, layer_noise):
        following = persist * previous + renewal * layer_noise
        return (following, following)
    _, stacked = lax.scan(advance, noise[0], noise[1:])
    result = jnp.concatenate([noise[0][None], stacked], 0)
    return result.astype(jnp.bfloat16)


def draw_factor_old(key, part):
    subkeys = jax.random.split(jax.random.fold_in(key, 202), 2)
    diagonal_values = jax.random.uniform(subkeys[0], (LAYERS, FEATURES), jnp.float32, 0.6, 1.4)
    raw = jax.random.normal(subkeys[1], (LAYERS, FEATURES, FEATURES), jnp.float32)
    raw = raw * (0.3 / jnp.sqrt(jnp.float32(FEATURES)))
    symmetric = (raw + jnp.swapaxes(raw, 1, 2)) * 0.70710678
    identity = jnp.eye(FEATURES, dtype=jnp.float32)
    return symmetric * (1.0 - identity) + diagonal_values[:, :, None] * identity


def draw_cross_old(key, part):
    subkeys = jax.random.split(jax.random.fold_in(key, 303), 2)
    diagonal_values = jax.random.uniform(subkeys[0], (LAYERS, FEATURES), jnp.float32, 0.2, 0.9)
    raw = jax.random.normal(subkeys[1], (LAYERS, FEATURES, FEATURES), jnp.float32)
    raw = raw * (0.3 / jnp.sqrt(jnp.float32(FEATURES)))
    identity = jnp.eye(FEATURES, dtype=jnp.float32)
    return raw * (1.0 - identity) + diagonal_values[:, :, None] * identity


def touch_ends(drawn, own_key, least, largest):
    spot = [jax.random.randint(jax.random.fold_in(own_key, axis), (), 0, length) for axis, length in enumerate(drawn.shape)]
    longest = drawn.shape.index(max(drawn.shape))
    beside = spot[:longest] + [(spot[longest] + 1) % drawn.shape[longest]] + spot[longest + 1:]
    return drawn.at[tuple(spot)].set(least).at[tuple(beside)].set(largest)


def block_levels(key, extent, cuts, low, largest):
    def one(dim, blocks):
        draws = jax.random.uniform(jax.random.fold_in(jax.random.fold_in(key, 6), dim), (blocks,), jnp.float32, low / len(cuts), largest / len(cuts))
        return jnp.repeat(jnp.exp(draws), extent[dim] // blocks).reshape((-1,) + (1,) * (len(extent) - dim - 1))

    gain = one(*cuts[0])
    for cut in cuts[1:]:
        gain = gain * one(*cut)
    return gain


def centred(stream_key, extent, deviation, most, shards=(), kind=jnp.bfloat16):
    values = deviation * jax.random.normal(stream_key, extent, jnp.float32)
    if shards:
        values = values * block_levels(stream_key, extent, shards, -0.22, 0.18)
    return jnp.clip(values, -most, most).astype(kind)


def setup_inputs(seed: int = 0) -> dict:
    arg_keys = jax.random.split(jax.random.key(seed), 8)
    activations = draw_activations(jax.random.fold_in(arg_keys[7], 71), 0)
    factor_old = draw_factor_old(jax.random.fold_in(arg_keys[7], 71), 0)
    cross_old = draw_cross_old(jax.random.fold_in(arg_keys[7], 71), 0)
    gradients = centred(arg_keys[3], (LAYERS, FEATURES, OUTPUTS), 1.0, 6.0, ((0, 8), (1, 4)))
    moments = centred(arg_keys[4], (LAYERS, FEATURES, OUTPUTS), 1.0, 6.0, ((0, 8), (1, 4)))
    exponents = touch_ends(jax.random.randint(arg_keys[5], (LAYERS, FEATURES // SCALE_BLOCK), -3, 3), jax.random.fold_in(arg_keys[5], 1), -3, 2).astype(jnp.int32)
    master = centred(arg_keys[6], (LAYERS, FEATURES, OUTPUTS), 1.0, 6.0, ((0, 8), (1, 4)), jnp.float32)
    return dict(activations=activations, factor_old=factor_old, cross_old=cross_old, gradients=gradients, moments=moments, exponents=exponents, master=master)


FACTOR_DECAY = 0.9
DAMPING = 0.5
MOMENTUM = 0.8
STEP_SIZE = 0.05


def chain_solve(target, pivots, coupling):
    coupling_ratio = coupling / pivots

    def forward_step(passed, slices):
        target_layer, pivot_layer, coupled = slices
        scaled = (target_layer - passed) / pivot_layer[:, None]
        return coupled[:, None] * scaled, scaled

    zero_block = jnp.zeros(target.shape[1:], jnp.float32)
    _, scaled_all = lax.scan(forward_step, zero_block, (target, pivots, coupling))

    def backward_step(nearer, slices):
        scaled, ratio_layer = slices
        solved = scaled - ratio_layer[:, None] * nearer
        return solved, solved

    _, solved_all = lax.scan(backward_step, zero_block, (scaled_all, coupling_ratio), reverse=True)
    return solved_all


def reference(activations, factor_old, cross_old, gradients, moments, exponents, master):
    fresh_weight = (1.0 - FACTOR_DECAY) / TOKENS
    next_acts = jnp.concatenate([activations[1:], jnp.zeros_like(activations[:1])], 0)

    def refresh(slices):
        own_layer, next_layer, factor_prev, cross_prev = slices
        batch_factor = jnp.dot(own_layer.T, own_layer, preferred_element_type=jnp.float32)
        batch_cross = jnp.dot(own_layer.T, next_layer, preferred_element_type=jnp.float32)
        return (FACTOR_DECAY * factor_prev + fresh_weight * batch_factor,
                FACTOR_DECAY * cross_prev + fresh_weight * batch_cross)

    factor_new, cross_new = lax.map(refresh, (activations, next_acts, factor_old, cross_old))
    diag_index = jnp.arange(FEATURES)
    pivots = DAMPING + factor_new[:, diag_index, diag_index]
    coupling = cross_new[:, diag_index, diag_index]
    grad_wide = gradients.astype(jnp.float32)
    initial = chain_solve(grad_wide, pivots, coupling).astype(jnp.bfloat16)
    initial_wide = initial.astype(jnp.float32)
    zero_sol = jnp.zeros_like(initial_wide[:1])
    upper_sol = jnp.concatenate([initial_wide[1:], zero_sol], 0)
    lower_sol = jnp.concatenate([zero_sol, initial_wide[:-1]], 0)
    cross_lower = jnp.concatenate([jnp.zeros_like(cross_new[:1]), cross_new[:-1]], 0)

    def apply_blocks(slices):
        factor_layer, cross_layer, cross_prev, own_block, upper_block, lower_block = slices
        result = jnp.dot(factor_layer, own_block, precision=lax.Precision.HIGHEST, preferred_element_type=jnp.float32)
        result = result + DAMPING * own_block
        result = result + jnp.dot(cross_layer, upper_block, precision=lax.Precision.HIGHEST, preferred_element_type=jnp.float32)
        result = result + jnp.dot(cross_prev.T, lower_block, precision=lax.Precision.HIGHEST, preferred_element_type=jnp.float32)
        return result

    applied = lax.map(apply_blocks, (factor_new, cross_new, cross_lower, initial_wide, upper_sol, lower_sol))
    update = initial_wide + chain_solve(grad_wide - applied, pivots, coupling)
    dequant = jnp.repeat(jnp.exp2(exponents.astype(jnp.float32)), SCALE_BLOCK, axis=1)[:, :, None]
    requant = jnp.repeat(jnp.exp2(-exponents.astype(jnp.float32)), SCALE_BLOCK, axis=1)[:, :, None]
    moment = MOMENTUM * moments.astype(jnp.float32) * dequant + (1.0 - MOMENTUM) * update
    moments_new = (moment * requant).astype(jnp.bfloat16)
    master_new = master - STEP_SIZE * moment
    replicas = master_new.astype(jnp.bfloat16)
    return factor_new, cross_new, moments_new, master_new, replicas
```

```python
import functools

import jax
import jax.numpy as jnp
from jax import lax
from jax.experimental import pallas as pl
from jax.experimental.pallas import tpu as pltpu
from jax.sharding import PartitionSpec as P

SCALE_BLOCK = 128


FACTOR_DECAY = 0.9
DAMPING = 0.5
MOMENTUM = 0.8
STEP_SIZE = 0.05


MESH = pl.DeviceIdType.MESH


def exchange_kernel(axis, count, modes, *refs):
    items = len(modes)
    sources, targets = refs[:items], refs[items : 2 * items]
    send_sem, recv_sem, local_sem = refs[2 * items :]
    mine = lax.axis_index(axis)
    barrier = pltpu.get_barrier_semaphore()
    for step in range(1, count):
        peer = lax.rem(mine + step, count)
        pl.semaphore_signal(barrier, inc=1, device_id={axis: peer}, device_id_type=MESH)
    pl.semaphore_wait(barrier, count - 1)
    remote, local = [], []
    for step in range(count - 1, 0, -1):
        peer = lax.rem(mine + step, count)
        for item, mode in enumerate(modes):
            if mode == "down" and step != count - 1:
                continue
            source = sources[item].at[peer] if mode == "swap" else sources[item]
            target = targets[item] if mode == "down" else targets[item].at[mine]
            remote.append(
                pltpu.make_async_remote_copy(
                    src_ref=source,
                    dst_ref=target,
                    send_sem=send_sem.at[item, step - 1],
                    recv_sem=recv_sem.at[item, step - 1],
                    device_id={axis: peer},
                    device_id_type=MESH,
                )
            )
            remote[-1].start()
    for item, mode in enumerate(modes):
        if mode != "down":
            source = sources[item].at[mine] if mode == "swap" else sources[item]
            local.append(
                pltpu.make_async_copy(source, targets[item].at[mine], local_sem.at[item])
            )
            local[-1].start()
    for copy in local + remote:
        copy.wait()


def exchange(axis, call_id, *pairs):
    count = lax.axis_size(axis)
    modes = tuple(mode for mode, _ in pairs)
    arrays = [array for _, array in pairs]
    shapes = [
        jax.ShapeDtypeStruct(
            (count,) + array.shape if mode == "gather" else array.shape, array.dtype
        )
        for mode, array in pairs
    ]
    sent = sum(array.size * array.dtype.itemsize for array in arrays)
    return pl.pallas_call(
        functools.partial(exchange_kernel, axis, count, modes),
        out_shape=shapes,
        in_specs=[pl.BlockSpec(memory_space=pltpu.VMEM)] * len(arrays),
        out_specs=[pl.BlockSpec(memory_space=pl.ANY)] * len(arrays),
        scratch_shapes=[
            pltpu.SemaphoreType.DMA((len(arrays), count - 1)),
            pltpu.SemaphoreType.DMA((len(arrays), count - 1)),
            pltpu.SemaphoreType.DMA((len(arrays),)),
        ],
        compiler_params=pltpu.CompilerParams(collective_id=call_id, has_side_effects=True),
        cost_estimate=pl.CostEstimate(flops=0, bytes_accessed=20 * sent, transcendentals=0),
    )(*arrays)


def first_kernel(layers, target_ref, pivot_ref, coupling_ref, out_ref, scaled_ref):
    def target_of(layer):
        return target_ref[layer].astype(jnp.float32)

    sweep(layers, target_of, pivot_ref, coupling_ref, out_ref, scaled_ref)


def second_kernel(
    layers, target_ref, initial_ref, away_ref, lower_ref, pivot_ref, coupling_ref, out_ref, scaled_ref
):
    def target_of(layer):
        target = target_ref[layer].astype(jnp.float32)
        target = target - pivot_ref[layer] * initial_ref[layer].astype(jnp.float32)
        if layer < layers - 1:
            target = target - coupling_ref[layer] * initial_ref[layer + 1].astype(jnp.float32)
        target = target - away_ref[layer].astype(jnp.float32)
        if layer:
            target = target - coupling_ref[layer - 1] * initial_ref[layer - 1].astype(jnp.float32)
            target = target - lower_ref[layer - 1].astype(jnp.float32)
        return target

    sweep(layers, target_of, pivot_ref, coupling_ref, out_ref, scaled_ref)


def sweep(layers, target_of, pivot_ref, coupling_ref, out_ref, scaled_ref):
    passed = None
    for layer in range(layers):
        target = target_of(layer)
        if layer:
            target = target - passed
        scaled = target / pivot_ref[layer]
        scaled_ref[layer] = scaled
        passed = coupling_ref[layer] * scaled
    solved = scaled
    out_ref[layers - 1] = solved.astype(out_ref.dtype)
    for layer in range(layers - 2, -1, -1):
        ratio = coupling_ref[layer] / pivot_ref[layer]
        solved = scaled_ref[layer] - ratio * solved
        out_ref[layer] = solved.astype(out_ref.dtype)


def chain_solve(pivots, coupling, *arrays):
    layers, rows, columns = arrays[0].shape
    width = 256 if columns % 256 == 0 else columns
    wide = pl.BlockSpec((layers, rows, width), lambda i: (0, 0, i))
    narrow = pl.BlockSpec((layers, rows, 1), lambda i: (0, 0, 0))
    size = arrays[0].size
    return pl.pallas_call(
        functools.partial(first_kernel if len(arrays) == 1 else second_kernel, layers),
        out_shape=jax.ShapeDtypeStruct(arrays[0].shape, jnp.bfloat16),
        grid=(columns // width,),
        in_specs=[wide] * len(arrays) + [narrow] * 2,
        out_specs=wide,
        scratch_shapes=[pltpu.VMEM((layers, rows, width), jnp.float32)],
        cost_estimate=pl.CostEstimate(
            flops=10 * size, bytes_accessed=8 * size, transcendentals=0
        ),
        name="solve",
    )(*arrays, pivots, coupling)


def shifted(value, axis, steps):
    count = lax.axis_size(axis)
    leading, last = (max(0, -steps), min(count, count - steps))
    return lax.ppermute(value, axis, [(source, source + steps) for source in range(leading, last)])


def product(left, right):
    return jnp.dot(left, right, preferred_element_type=jnp.float32)


CHUNKS = 4


def column_of(row, eye):
    return jnp.sum(jnp.where(eye, jnp.broadcast_to(row, eye.shape), 0.0), axis=1, keepdims=True)


def identity(size):
    return lax.broadcasted_iota(jnp.int32, (size, size), 0) == lax.broadcasted_iota(
        jnp.int32, (size, size), 1
    )


def greet():
    barrier = pltpu.get_barrier_semaphore()
    total = 0
    for axis in ("layer", "dp"):
        count, mine = lax.axis_size(axis), lax.axis_index(axis)
        for step in range(1, count):
            pl.semaphore_signal(
                barrier, inc=1, device_id={axis: lax.rem(mine + step, count)}, device_id_type=MESH
            )
        total += count - 1
    pl.semaphore_wait(barrier, total)


def remote(source, target, send_sem, recv_sem, axis, step):
    count, mine = lax.axis_size(axis), lax.axis_index(axis)
    return pltpu.make_async_remote_copy(
        src_ref=source,
        dst_ref=target,
        send_sem=send_sem,
        recv_sem=recv_sem,
        device_id={axis: lax.rem(mine + step + count, count)},
        device_id_type=MESH,
    )


class Line:
    def __init__(self, axis, source, target, send_sem, recv_sem, pieces):
        self.axis, self.count, self.mine = axis, lax.axis_size(axis), lax.axis_index(axis)
        self.source, self.target, self.pieces = source, target, pieces
        self.send_sem, self.recv_sem = send_sem, recv_sem

    def copy(self, way, hop, piece):
        sign = 1 if way == 0 else -1
        block = jnp.clip(self.mine - sign * hop, 0, self.count - 1)
        landing = self.target(block, piece)
        return remote(
            self.source(piece) if hop == 0 else landing,
            landing,
            self.send_sem.at[way, hop, piece],
            self.recv_sem.at[way, hop, piece],
            self.axis,
            sign,
        )

    def has_next(self, way):
        return self.mine < self.count - 1 if way == 0 else self.mine > 0

    def has_block(self, way, hop):
        return self.mine >= hop if way == 0 else self.mine + hop <= self.count - 1

    def begin(self, pieces):
        for piece in pieces:
            for way in (0, 1):

                @pl.when(self.has_next(way))
                def _():
                    self.copy(way, 0, piece).start()

    def arrive(self, hop, pieces, then=None):
        for piece in pieces:
            for way in (0, 1):

                @pl.when(self.has_block(way, hop))
                def _():
                    self.copy(way, hop - 1, piece).wait_recv()
                    if hop < self.count - 1:

                        @pl.when(self.has_next(way))
                        def _():
                            self.copy(way, hop, piece).start()

                    if then is not None:
                        sign = 1 if way == 0 else -1
                        then(jnp.clip(self.mine - sign * hop, 0, self.count - 1), piece)

    def finish(self):
        for hop in range(self.count - 1):
            for piece in range(self.pieces):
                for way in (0, 1):

                    @pl.when(self.has_next(way) & self.has_block(way, hop))
                    def _():
                        self.copy(way, hop, piece).wait_send()


def front_kernel(
    fresh_weight,
    acts, grads, factor_old, cross_old,
    factor_high_out, factor_low_out, cross_high_out, cross_low_out, turned_out,
    initial_out, grads_out, solved_out, scales_out, own_scales_out,
    tokens, upper, factor, cross, cross_cut, blocks, grads_in, solved, scaled,
    sums_away, sums_in, own_scales, scales, own_turned, upper_turned,
    factor_high, factor_low, cross_high, cross_low, turned,
    line_send, line_recv, lift_send, lift_recv, grad_send, grad_recv, sum_send, sum_recv,
    scale_send, scale_recv, start_send, start_recv, block_send, block_recv, local_sem,
):
    layers, groups = lax.axis_size("layer"), lax.axis_size("dp")
    layer, group = lax.axis_index("layer"), lax.axis_index("dp")
    rows, features = factor.shape
    count = acts.shape[0]
    part = count // CHUNKS
    chunk = rows // layers
    columns = grads.shape[2]
    own = pl.ds(pl.multiple_of(group * rows, rows), rows)

    def span(piece):
        return pl.ds(piece * part, part)

    load_acts = pltpu.make_async_copy(acts, tokens.at[group], local_sem.at[0])
    load_factor = pltpu.make_async_copy(factor_old, factor, local_sem.at[1])
    load_cross = pltpu.make_async_copy(cross_old, cross, local_sem.at[2])
    load_grads = pltpu.make_async_copy(grads.at[layer], grads_in.at[layer], local_sem.at[3])
    load_acts.start()
    load_cross.start()
    load_factor.start()
    load_grads.start()
    greet()

    line = Line(
        "dp",
        lambda piece: acts.at[span(piece)],
        lambda block, piece: tokens.at[block, span(piece)],
        line_send,
        line_recv,
        CHUNKS,
    )

    def lift_copy(source, block, piece):
        return remote(
            source,
            upper.at[block, span(piece)],
            lift_send.at[block, piece],
            lift_recv.at[block, piece],
            "layer",
            -1,
        )

    def lift(block, piece):
        @pl.when(layer > 0)
        def _():
            lift_copy(tokens.at[block, span(piece)], block, piece).start()

    @pl.when(layer > 0)
    def _():
        for piece in range(CHUNKS):
            lift_copy(acts.at[span(piece)], group, piece).start()

    def grad_copy(step):
        peer = lax.rem(layer + step, layers)
        return remote(
            grads.at[peer], grads_in.at[layer], grad_send.at[step - 1], grad_recv.at[step - 1],
            "layer", step,
        )

    for step in range(layers - 1, 0, -1):
        grad_copy(step).start()
    line.begin(range(CHUNKS // 2))

    load_acts.wait()
    sums_away[...] = jnp.zeros_like(sums_away)
    for place in range(groups):
        wide = tokens[group, :, place * rows : (place + 1) * rows].astype(jnp.float32)
        sums_away[place, 0:1, :] = jnp.sum(wide * wide, axis=0, keepdims=True)
    load_cross.wait()
    load_factor.wait()
    eye = identity(rows)
    factor_diagonal = jnp.sum(jnp.where(eye, factor[:, own], 0.0), axis=1, keepdims=True)
    cross_diagonal = jnp.sum(jnp.where(eye, cross[:, own], 0.0), axis=1, keepdims=True)

    @pl.when(layer < layers - 1)
    def _():
        for piece in range(CHUNKS):
            lift_copy(acts.at[span(piece)], group, piece).wait_recv()
        for place in range(groups):
            cut = slice(place * rows, (place + 1) * rows)
            wide = tokens[group, :, cut].astype(jnp.float32)
            above = upper[group, :, cut].astype(jnp.float32)
            sums_away[place, 1:2, :] = jnp.sum(wide * above, axis=0, keepdims=True)

    @pl.when(layer == layers - 1)
    def _():
        upper[...] = jnp.zeros_like(upper)

    def sum_copy(step):
        peer = lax.rem(group + step, groups)
        return remote(
            sums_away.at[peer], sums_in.at[group], sum_send.at[step - 1], sum_recv.at[step - 1],
            "dp", step,
        )

    for step in range(groups - 1, 0, -1):
        sum_copy(step).start()
    line.begin(range(CHUNKS // 2, CHUNKS))
    sums_in[group] = sums_away[group]
    line.arrive(1, range(CHUNKS // 2))

    for step in range(groups - 1, 0, -1):
        sum_copy(step).wait_recv()
    sums = fresh_weight * jnp.sum(sums_in[...], axis=0)
    own_sum = column_of(sums[0:1], eye)
    next_sum = column_of(sums[1:2], eye)
    own_diagonal = FACTOR_DECAY * factor_diagonal + own_sum
    own_coupling = FACTOR_DECAY * cross_diagonal + next_sum
    lane = lax.broadcasted_iota(jnp.int32, (rows, 128), 1)
    own_scales[...] = jnp.where(
        lane == 0,
        DAMPING + own_diagonal,
        jnp.where(lane == 1, own_coupling, jnp.where(lane == 2, own_diagonal, next_sum)),
    )

    def scale_copy(step):
        peer = lax.rem(layer + step, layers)
        return remote(
            own_scales.at[pl.ds(pl.multiple_of(peer * chunk, chunk), chunk)],
            scales.at[layer], scale_send.at[step - 1], scale_recv.at[step - 1], "layer", step,
        )

    for step in range(layers - 1, 0, -1):
        scale_copy(step).start()
    scales[layer] = own_scales[pl.ds(pl.multiple_of(layer * chunk, chunk), chunk), :]
    line.arrive(1, range(CHUNKS // 2, CHUNKS))
    load_grads.wait()
    for step in range(layers - 1, 0, -1):
        scale_copy(step).wait_recv()
        grad_copy(step).wait_recv()

    width = scaled.shape[2]

    def solve(tile, carry):
        cut = pl.ds(pl.multiple_of(tile * width, width), width)
        passed = None
        for place in range(layers):
            target = grads_in[place, :, cut].astype(jnp.float32)
            if place:
                target = target - passed
            value = target / scales[place, :, 0:1]
            scaled[place] = value
            passed = scales[place, :, 1:2] * value
        result = value
        solved[layers - 1, :, cut] = result.astype(jnp.bfloat16)
        for place in range(layers - 2, -1, -1):
            ratio = scales[place, :, 1:2] / scales[place, :, 0:1]
            result = scaled[place] - ratio * result
            solved[place, :, cut] = result.astype(jnp.bfloat16)
        return carry

    lax.fori_loop(0, columns // width, solve, 0)

    def start_copy(step):
        peer = lax.rem(layer + step, layers)
        return remote(
            solved.at[peer], initial_out.at[layer], start_send.at[step - 1],
            start_recv.at[step - 1], "layer", step,
        )

    for step in range(layers - 1, 0, -1):
        start_copy(step).start()
    stores = [
        pltpu.make_async_copy(solved.at[layer], initial_out.at[layer], local_sem.at[0]),
        pltpu.make_async_copy(grads_in, grads_out, local_sem.at[1]),
        pltpu.make_async_copy(solved, solved_out, local_sem.at[2]),
        pltpu.make_async_copy(scales, scales_out, local_sem.at[3]),
        pltpu.make_async_copy(own_scales, own_scales_out, local_sem.at[4]),
    ]
    for store in stores:
        store.start()

    def narrow(tile, carry):
        cut = pl.ds(pl.multiple_of(tile * rows, rows), rows)
        cross_cut[:, cut] = cross[:, cut].astype(jnp.bfloat16)
        return carry

    lax.fori_loop(0, groups, narrow, 0)
    blocks[group] = jnp.where(eye, 0.0, cross[:, own]).astype(jnp.bfloat16)

    for way in (0, 1):

        @pl.when(line.has_block(way, 1))
        def _():
            for piece in range(CHUNKS):
                lift(jnp.clip(group - (1 if way == 0 else -1), 0, groups - 1), piece)

    for hop in range(2, groups - 1):
        line.arrive(hop, range(CHUNKS), lift)

    def block_copy(step):
        peer = lax.rem(group + step, groups)
        return remote(
            cross_cut.at[:, pl.ds(pl.multiple_of(peer * rows, rows), rows)],
            blocks.at[group], block_send.at[step - 1], block_recv.at[step - 1], "dp", step,
        )

    for step in range(groups - 1, 0, -1):
        block_copy(step).start()
    line.arrive(groups - 1, range(CHUNKS), lift)

    tile = 256
    every = count * groups

    def gather(ref, cut):
        return ref[:, :, cut].reshape(every, cut.size)

    own_turned[...] = gather(tokens, own).astype(jnp.float32).T.astype(jnp.bfloat16)

    def refresh_factor(place, carry):
        cut = pl.ds(pl.multiple_of(place * tile, tile), tile)
        fresh = product(own_turned[...], gather(tokens, cut))
        value = FACTOR_DECAY * factor[:, cut] + fresh_weight * fresh
        high = value.astype(jnp.bfloat16)
        factor_high[:, cut] = high
        factor_low[:, cut] = (value - high.astype(jnp.float32)).astype(jnp.bfloat16)
        return carry

    lax.fori_loop(0, features // tile, refresh_factor, 0)
    more = [
        pltpu.make_async_copy(factor_high, factor_high_out, local_sem.at[5]),
        pltpu.make_async_copy(factor_low, factor_low_out, local_sem.at[6]),
    ]
    for store in more:
        store.start()
    stores += more

    @pl.when(layer < layers - 1)
    def _():
        for step in range(1, groups):
            block = lax.rem(group + step, groups)
            for piece in range(CHUNKS):
                lift_copy(acts.at[span(piece)], block, piece).wait_recv()

    upper_turned[...] = gather(upper, own).astype(jnp.float32).T.astype(jnp.bfloat16)

    def refresh_cross(place, carry):
        cut = pl.ds(pl.multiple_of(place * tile, tile), tile)
        fresh = product(own_turned[...], gather(upper, cut))
        value = FACTOR_DECAY * cross[:, cut] + fresh_weight * fresh
        high = value.astype(jnp.bfloat16)
        cross_high[:, cut] = high
        cross_low[:, cut] = (value - high.astype(jnp.float32)).astype(jnp.bfloat16)
        factor[:, cut] = fresh_weight * product(upper_turned[...], gather(tokens, cut))
        return carry

    lax.fori_loop(0, features // tile, refresh_cross, 0)
    more = [
        pltpu.make_async_copy(cross_high, cross_high_out, local_sem.at[7]),
        pltpu.make_async_copy(cross_low, cross_low_out, local_sem.at[8]),
    ]
    for store in more:
        store.start()
    stores += more

    factor[:, own] = jnp.where(eye, 0.0, factor[:, own])
    for step in range(groups - 1, 0, -1):
        block_copy(step).wait_recv()

    def join(place, carry):
        cut = pl.ds(pl.multiple_of(place * rows, rows), rows)
        old = blocks[place].astype(jnp.float32).T
        turned[:, cut] = (FACTOR_DECAY * old + factor[:, cut]).astype(jnp.bfloat16)
        return carry

    lax.fori_loop(0, groups, join, 0)
    last = pltpu.make_async_copy(turned, turned_out, local_sem.at[9])
    last.start()
    stores.append(last)

    for step in range(1, layers):
        start_copy(step).wait()
        grad_copy(step).wait_send()
        scale_copy(step).wait_send()
    for step in range(1, groups):
        sum_copy(step).wait_send()
        block_copy(step).wait_send()

    @pl.when(layer > 0)
    def _():
        for block in range(groups):
            for piece in range(CHUNKS):
                lift_copy(acts.at[span(piece)], block, piece).wait_send()

    line.finish()
    for store in stores:
        store.wait()


def front(fresh_weight, acts, grads, factor_old, cross_old):
    layers, groups = lax.axis_size("layer"), lax.axis_size("dp")
    rows, features = factor_old.shape
    count = acts.shape[0]
    chunk, columns = grads.shape[1:]
    every = count * groups
    half, full = jnp.bfloat16, jnp.float32
    dma = pltpu.SemaphoreType.DMA
    shape = jax.ShapeDtypeStruct
    return pl.pallas_call(
        functools.partial(front_kernel, fresh_weight),
        out_shape=[shape((rows, features), half)] * 5
        + [shape((layers, chunk, columns), half)] * 3
        + [shape((layers, chunk, 128), full), shape((rows, 128), full)],
        in_specs=[pl.BlockSpec(memory_space=pl.ANY)] * 4,
        out_specs=[pl.BlockSpec(memory_space=pl.ANY)] * 10,
        scratch_shapes=[
            pltpu.VMEM((groups, count, features), half),
            pltpu.VMEM((groups, count, features), half),
            pltpu.VMEM((rows, features), full),
            pltpu.VMEM((rows, features), full),
            pltpu.VMEM((rows, features), half),
            pltpu.VMEM((groups, rows, rows), half),
            pltpu.VMEM((layers, chunk, columns), half),
            pltpu.VMEM((layers, chunk, columns), half),
            pltpu.VMEM((layers, chunk, 256), full),
            pltpu.VMEM((groups, 8, rows), full),
            pltpu.VMEM((groups, 8, rows), full),
            pltpu.VMEM((rows, 128), full),
            pltpu.VMEM((layers, chunk, 128), full),
            pltpu.VMEM((rows, every), half),
            pltpu.VMEM((rows, every), half),
        ]
        + [pltpu.VMEM((rows, features), half)] * 5
        + [dma((2, groups - 1, CHUNKS))] * 2
        + [dma((groups, CHUNKS))] * 2
        + [dma((layers - 1,))] * 2
        + [dma((groups - 1,))] * 2
        + [dma((layers - 1,))] * 4
        + [dma((groups - 1,))] * 2
        + [dma((10,))],
        compiler_params=pltpu.CompilerParams(
            collective_id=0, has_side_effects=True, vmem_limit_bytes=63 << 20
        ),
        cost_estimate=pl.CostEstimate(
            flops=6 * every * rows * features, bytes_accessed=200_000_000, transcendentals=0
        ),
        name="front",
    )(acts, grads, factor_old, cross_old)


def body(activations, factor_old, cross_old, gradients, moments, exponents, master):
    layers, groups = lax.axis_size("layer"), lax.axis_size("dp")
    group = lax.axis_index("dp")
    row_count, _ = factor_old.shape[1:]
    columns = gradients.shape[2]
    chunk = row_count // layers
    row_start = group * row_count
    fresh_weight = (1.0 - FACTOR_DECAY) / (activations.shape[1] * groups)
    factor_high, factor_low, cross_high, cross_low, turned, initial, grad_swapped, initial_swapped, scales, own_scales = front(
        fresh_weight,
        activations[0],
        gradients[0].reshape(layers, chunk, columns),
        factor_old[0],
        cross_old[0],
    )
    pivots, coupling = scales[:, :, 0:1], scales[:, :, 1:2]
    own_coupling, own_diagonal = own_scales[:, 1:2], own_scales[:, 2:3]
    initial = initial.reshape(row_count, columns)

    pieces = 2
    width = columns // pieces
    parts = [slice(piece * width, (piece + 1) * width) for piece in range(pieces)]
    own_full = [lax.all_gather(initial[:, parts[0]], "dp", axis=0, tiled=True)]

    later = [initial[:, part] for part in parts[1:]]
    own_full += [lax.all_gather(value, "dp", axis=0, tiled=True) for value in later]

    def leave(piece):
        full, near = own_full[piece], initial[:, parts[piece]].astype(jnp.float32)
        upper = shifted(full, "layer", -1)
        transposed = product(turned, full).astype(jnp.bfloat16)
        away = product(factor_high, full) + product(factor_low, full) - own_diagonal * near
        upper_rows = lax.dynamic_slice_in_dim(upper, row_start, row_count, 0)
        away = away + product(cross_high, upper) + product(cross_low, upper)
        away = (away - own_coupling * upper_rows.astype(jnp.float32)).astype(jnp.bfloat16)
        return [value.reshape(layers, chunk, width) for value in (away, transposed)]

    dequant = jnp.repeat(jnp.exp2(exponents[0].astype(jnp.float32)), SCALE_BLOCK)[:, None]
    requant = jnp.repeat(jnp.exp2(-exponents[0].astype(jnp.float32)), SCALE_BLOCK)[:, None]
    results, sent = [], None
    for piece, part in enumerate(parts):
        away, lowered = leave(piece)
        if piece:
            gathered = lax.all_gather(sent, "dp", axis=0, tiled=True)
            away, lowered, held = lax.optimization_barrier((away, lowered, results[-1]))
            results[-1] = held + (gathered,)
        away, lowered = exchange("layer", 4 + 2 * piece, ("swap", away), ("swap", lowered))
        if piece + 1 < pieces:
            away, lowered, own_full[piece + 1] = lax.optimization_barrier(
                (away, lowered, own_full[piece + 1])
            )
        correction = chain_solve(
            pivots, coupling, grad_swapped[:, :, part], initial_swapped[:, :, part], away, lowered
        )
        (correction,) = exchange("layer", 5 + 2 * piece, ("swap", correction))
        correction = correction.reshape(row_count, width)
        update = initial[:, part].astype(jnp.float32) + correction.astype(jnp.float32)
        moment = MOMENTUM * moments[0][:, part].astype(jnp.float32) * dequant
        moment = moment + (1.0 - MOMENTUM) * update
        fresh_moments = (moment * requant).astype(jnp.bfloat16)
        fresh_master = master[0][:, part] - STEP_SIZE * moment
        sent = fresh_master.astype(jnp.bfloat16)
        results.append((fresh_moments, fresh_master))
    results[-1] += (lax.all_gather(sent, "dp", axis=0, tiled=True),)
    moments_new, master_new, replicas = [jnp.concatenate(values, 1) for values in zip(*results)]
    factor_new = factor_high.astype(jnp.float32) + factor_low.astype(jnp.float32)
    cross_new = cross_high.astype(jnp.float32) + cross_low.astype(jnp.float32)
    return (factor_new[None], cross_new[None], moments_new[None], master_new[None], replicas[None])


def solution(mesh):
    return jax.shard_map(
        body,
        mesh=mesh,
        in_specs=(
            P("layer", "dp", None),
            P("layer", "dp", None),
            P("layer", "dp", None),
            P("layer", "dp", None),
            P("layer", "dp", None),
            P("layer", "dp"),
            P("layer", "dp", None),
        ),
        out_specs=(
            P("layer", "dp", None),
            P("layer", "dp", None),
            P("layer", "dp", None),
            P("layer", "dp", None),
            P("layer", None, None),
        ),
        check_vma=False,
    )
```

```python
import functools

import jax
import jax.numpy as jnp
from jax import lax
from jax.experimental import pallas as pl
from jax.experimental.pallas import tpu as pltpu
from jax.sharding import PartitionSpec as P

SCALE_BLOCK = 128


FACTOR_DECAY = 0.9
DAMPING = 0.5
MOMENTUM = 0.8
STEP_SIZE = 0.05

MESH = pl.DeviceIdType.MESH


def product(left, right):
    return jnp.dot(left, right, preferred_element_type=jnp.float32)


CHUNKS = 4


def column_of(row, eye):
    return jnp.sum(jnp.where(eye, jnp.broadcast_to(row, eye.shape), 0.0), axis=1, keepdims=True)


def identity(size):
    return lax.broadcasted_iota(jnp.int32, (size, size), 0) == lax.broadcasted_iota(
        jnp.int32, (size, size), 1
    )


def greet():
    barrier = pltpu.get_barrier_semaphore()
    total = 0
    for axis in ("layer", "dp"):
        count, mine = lax.axis_size(axis), lax.axis_index(axis)
        for step in range(1, count):
            pl.semaphore_signal(
                barrier, inc=1, device_id={axis: lax.rem(mine + step, count)}, device_id_type=MESH
            )
        total += count - 1
    pl.semaphore_wait(barrier, total)


def remote(source, target, send_sem, recv_sem, axis, step):
    count, mine = lax.axis_size(axis), lax.axis_index(axis)
    return pltpu.make_async_remote_copy(
        src_ref=source,
        dst_ref=target,
        send_sem=send_sem,
        recv_sem=recv_sem,
        device_id={axis: lax.rem(mine + step + count, count)},
        device_id_type=MESH,
    )


class Line:
    def __init__(self, axis, source, target, send_sem, recv_sem, pieces):
        self.axis, self.count, self.mine = axis, lax.axis_size(axis), lax.axis_index(axis)
        self.source, self.target, self.pieces = source, target, pieces
        self.send_sem, self.recv_sem = send_sem, recv_sem

    def copy(self, way, hop, piece):
        sign = 1 if way == 0 else -1
        block = jnp.clip(self.mine - sign * hop, 0, self.count - 1)
        landing = self.target(block, piece)
        return remote(
            self.source(piece) if hop == 0 else landing,
            landing,
            self.send_sem.at[way, hop, piece],
            self.recv_sem.at[way, hop, piece],
            self.axis,
            sign,
        )

    def has_next(self, way):
        return self.mine < self.count - 1 if way == 0 else self.mine > 0

    def has_block(self, way, hop):
        return self.mine >= hop if way == 0 else self.mine + hop <= self.count - 1

    def begin(self, pieces):
        for piece in pieces:
            for way in (0, 1):

                @pl.when(self.has_next(way))
                def _():
                    self.copy(way, 0, piece).start()

    def arrive(self, hop, pieces, then=None):
        for piece in pieces:
            for way in (0, 1):

                @pl.when(self.has_block(way, hop))
                def _():
                    self.copy(way, hop - 1, piece).wait_recv()
                    if hop < self.count - 1:

                        @pl.when(self.has_next(way))
                        def _():
                            self.copy(way, hop, piece).start()

                    if then is not None:
                        sign = 1 if way == 0 else -1
                        then(jnp.clip(self.mine - sign * hop, 0, self.count - 1), piece)

    def finish(self):
        for hop in range(self.count - 1):
            for piece in range(self.pieces):
                for way in (0, 1):

                    @pl.when(self.has_next(way) & self.has_block(way, hop))
                    def _():
                        self.copy(way, hop, piece).wait_send()


def front_kernel(
    fresh_weight,
    acts, grads, factor_old, cross_old,
    factor_high_out, factor_low_out, cross_high_out, cross_low_out, turned_out,
    initial_out, grads_out, solved_out, scales_out, own_scales_out,
    tokens, upper, factor, cross, cross_cut, blocks, grads_in, solved, scaled,
    sums_away, sums_in, own_scales, scales, own_turned, upper_turned,
    factor_high, factor_low, cross_high, cross_low, turned,
    line_send, line_recv, lift_send, lift_recv, grad_send, grad_recv, sum_send, sum_recv,
    scale_send, scale_recv, start_send, start_recv, block_send, block_recv, local_sem,
):
    layers, groups = lax.axis_size("layer"), lax.axis_size("dp")
    layer, group = lax.axis_index("layer"), lax.axis_index("dp")
    rows, features = factor.shape
    count = acts.shape[0]
    part = count // CHUNKS
    chunk = rows // layers
    columns = grads.shape[2]
    own = pl.ds(pl.multiple_of(group * rows, rows), rows)

    def span(piece):
        return pl.ds(piece * part, part)

    load_acts = pltpu.make_async_copy(acts, tokens.at[group], local_sem.at[0])
    load_factor = pltpu.make_async_copy(factor_old, factor, local_sem.at[1])
    load_cross = pltpu.make_async_copy(cross_old, cross, local_sem.at[2])
    load_grads = pltpu.make_async_copy(grads.at[layer], grads_in.at[layer], local_sem.at[3])
    load_acts.start()
    load_cross.start()
    load_factor.start()
    load_grads.start()
    greet()

    line = Line(
        "dp",
        lambda piece: acts.at[span(piece)],
        lambda block, piece: tokens.at[block, span(piece)],
        line_send,
        line_recv,
        CHUNKS,
    )

    def lift_copy(source, block, piece):
        return remote(
            source,
            upper.at[block, span(piece)],
            lift_send.at[block, piece],
            lift_recv.at[block, piece],
            "layer",
            -1,
        )

    def lift(block, piece):
        @pl.when(layer > 0)
        def _():
            lift_copy(tokens.at[block, span(piece)], block, piece).start()

    @pl.when(layer > 0)
    def _():
        for piece in range(CHUNKS):
            lift_copy(acts.at[span(piece)], group, piece).start()

    def grad_copy(step):
        peer = lax.rem(layer + step, layers)
        return remote(
            grads.at[peer], grads_in.at[layer], grad_send.at[step - 1], grad_recv.at[step - 1],
            "layer", step,
        )

    for step in range(layers - 1, 0, -1):
        grad_copy(step).start()
    line.begin(range(CHUNKS // 2))

    load_acts.wait()
    sums_away[...] = jnp.zeros_like(sums_away)
    for place in range(groups):
        wide = tokens[group, :, place * rows : (place + 1) * rows].astype(jnp.float32)
        sums_away[place, 0:1, :] = jnp.sum(wide * wide, axis=0, keepdims=True)
    load_cross.wait()
    load_factor.wait()
    eye = identity(rows)
    factor_diagonal = jnp.sum(jnp.where(eye, factor[:, own], 0.0), axis=1, keepdims=True)
    cross_diagonal = jnp.sum(jnp.where(eye, cross[:, own], 0.0), axis=1, keepdims=True)

    @pl.when(layer < layers - 1)
    def _():
        for piece in range(CHUNKS):
            lift_copy(acts.at[span(piece)], group, piece).wait_recv()
        for place in range(groups):
            cut = slice(place * rows, (place + 1) * rows)
            wide = tokens[group, :, cut].astype(jnp.float32)
            above = upper[group, :, cut].astype(jnp.float32)
            sums_away[place, 1:2, :] = jnp.sum(wide * above, axis=0, keepdims=True)

    @pl.when(layer == layers - 1)
    def _():
        upper[...] = jnp.zeros_like(upper)

    def sum_copy(step):
        peer = lax.rem(group + step, groups)
        return remote(
            sums_away.at[peer], sums_in.at[group], sum_send.at[step - 1], sum_recv.at[step - 1],
            "dp", step,
        )

    for step in range(groups - 1, 0, -1):
        sum_copy(step).start()
    line.begin(range(CHUNKS // 2, CHUNKS))
    sums_in[group] = sums_away[group]
    line.arrive(1, range(CHUNKS // 2))

    for step in range(groups - 1, 0, -1):
        sum_copy(step).wait_recv()
    sums = fresh_weight * jnp.sum(sums_in[...], axis=0)
    own_sum = column_of(sums[0:1], eye)
    next_sum = column_of(sums[1:2], eye)
    own_diagonal = FACTOR_DECAY * factor_diagonal + own_sum
    own_coupling = FACTOR_DECAY * cross_diagonal + next_sum
    lane = lax.broadcasted_iota(jnp.int32, (rows, 128), 1)
    own_scales[...] = jnp.where(
        lane == 0,
        DAMPING + own_diagonal,
        jnp.where(lane == 1, own_coupling, jnp.where(lane == 2, own_diagonal, next_sum)),
    )

    def scale_copy(step):
        peer = lax.rem(layer + step, layers)
        return remote(
            own_scales.at[pl.ds(pl.multiple_of(peer * chunk, chunk), chunk)],
            scales.at[layer], scale_send.at[step - 1], scale_recv.at[step - 1], "layer", step,
        )

    for step in range(layers - 1, 0, -1):
        scale_copy(step).start()
    scales[layer] = own_scales[pl.ds(pl.multiple_of(layer * chunk, chunk), chunk), :]
    line.arrive(1, range(CHUNKS // 2, CHUNKS))
    load_grads.wait()
    for step in range(layers - 1, 0, -1):
        scale_copy(step).wait_recv()
        grad_copy(step).wait_recv()

    width = scaled.shape[2]

    def solve(tile, carry):
        cut = pl.ds(pl.multiple_of(tile * width, width), width)
        passed = None
        for place in range(layers):
            target = grads_in[place, :, cut].astype(jnp.float32)
            if place:
                target = target - passed
            value = target / scales[place, :, 0:1]
            scaled[place] = value
            passed = scales[place, :, 1:2] * value
        result = value
        solved[layers - 1, :, cut] = result.astype(jnp.bfloat16)
        for place in range(layers - 2, -1, -1):
            ratio = scales[place, :, 1:2] / scales[place, :, 0:1]
            result = scaled[place] - ratio * result
            solved[place, :, cut] = result.astype(jnp.bfloat16)
        return carry

    lax.fori_loop(0, columns // width, solve, 0)

    def start_copy(step):
        peer = lax.rem(layer + step, layers)
        return remote(
            solved.at[peer], initial_out.at[layer], start_send.at[step - 1],
            start_recv.at[step - 1], "layer", step,
        )

    for step in range(layers - 1, 0, -1):
        start_copy(step).start()
    stores = [
        pltpu.make_async_copy(solved.at[layer], initial_out.at[layer], local_sem.at[0]),
        pltpu.make_async_copy(grads_in, grads_out, local_sem.at[1]),
        pltpu.make_async_copy(solved, solved_out, local_sem.at[2]),
        pltpu.make_async_copy(scales, scales_out, local_sem.at[3]),
        pltpu.make_async_copy(own_scales, own_scales_out, local_sem.at[4]),
    ]
    for store in stores:
        store.start()

    def narrow(tile, carry):
        cut = pl.ds(pl.multiple_of(tile * rows, rows), rows)
        cross_cut[:, cut] = cross[:, cut].astype(jnp.bfloat16)
        return carry

    lax.fori_loop(0, groups, narrow, 0)
    blocks[group] = jnp.where(eye, 0.0, cross[:, own]).astype(jnp.bfloat16)

    for way in (0, 1):

        @pl.when(line.has_block(way, 1))
        def _():
            for piece in range(CHUNKS):
                lift(jnp.clip(group - (1 if way == 0 else -1), 0, groups - 1), piece)

    for hop in range(2, groups - 1):
        line.arrive(hop, range(CHUNKS), lift)

    def block_copy(step):
        peer = lax.rem(group + step, groups)
        return remote(
            cross_cut.at[:, pl.ds(pl.multiple_of(peer * rows, rows), rows)],
            blocks.at[group], block_send.at[step - 1], block_recv.at[step - 1], "dp", step,
        )

    for step in range(groups - 1, 0, -1):
        block_copy(step).start()
    line.arrive(groups - 1, range(CHUNKS), lift)

    tile = 256
    every = count * groups

    def gather(ref, cut):
        return ref[:, :, cut].reshape(every, cut.size)

    own_turned[...] = gather(tokens, own).astype(jnp.float32).T.astype(jnp.bfloat16)

    def refresh_factor(place, carry):
        cut = pl.ds(pl.multiple_of(place * tile, tile), tile)
        fresh = product(own_turned[...], gather(tokens, cut))
        value = FACTOR_DECAY * factor[:, cut] + fresh_weight * fresh
        high = value.astype(jnp.bfloat16)
        factor_high[:, cut] = high
        factor_low[:, cut] = (value - high.astype(jnp.float32)).astype(jnp.bfloat16)
        return carry

    lax.fori_loop(0, features // tile, refresh_factor, 0)
    more = [
        pltpu.make_async_copy(factor_high, factor_high_out, local_sem.at[5]),
        pltpu.make_async_copy(factor_low, factor_low_out, local_sem.at[6]),
    ]
    for store in more:
        store.start()
    stores += more

    @pl.when(layer < layers - 1)
    def _():
        for step in range(1, groups):
            block = lax.rem(group + step, groups)
            for piece in range(CHUNKS):
                lift_copy(acts.at[span(piece)], block, piece).wait_recv()

    upper_turned[...] = gather(upper, own).astype(jnp.float32).T.astype(jnp.bfloat16)

    def refresh_cross(place, carry):
        cut = pl.ds(pl.multiple_of(place * tile, tile), tile)
        fresh = product(own_turned[...], gather(upper, cut))
        value = FACTOR_DECAY * cross[:, cut] + fresh_weight * fresh
        high = value.astype(jnp.bfloat16)
        cross_high[:, cut] = high
        cross_low[:, cut] = (value - high.astype(jnp.float32)).astype(jnp.bfloat16)
        factor[:, cut] = fresh_weight * product(upper_turned[...], gather(tokens, cut))
        return carry

    lax.fori_loop(0, features // tile, refresh_cross, 0)
    more = [
        pltpu.make_async_copy(cross_high, cross_high_out, local_sem.at[7]),
        pltpu.make_async_copy(cross_low, cross_low_out, local_sem.at[8]),
    ]
    for store in more:
        store.start()
    stores += more

    factor[:, own] = jnp.where(eye, 0.0, factor[:, own])
    for step in range(groups - 1, 0, -1):
        block_copy(step).wait_recv()

    def join(place, carry):
        cut = pl.ds(pl.multiple_of(place * rows, rows), rows)
        old = blocks[place].astype(jnp.float32).T
        turned[:, cut] = (FACTOR_DECAY * old + factor[:, cut]).astype(jnp.bfloat16)
        return carry

    lax.fori_loop(0, groups, join, 0)
    last = pltpu.make_async_copy(turned, turned_out, local_sem.at[9])
    last.start()
    stores.append(last)

    for step in range(1, layers):
        start_copy(step).wait()
        grad_copy(step).wait_send()
        scale_copy(step).wait_send()
    for step in range(1, groups):
        sum_copy(step).wait_send()
        block_copy(step).wait_send()

    @pl.when(layer > 0)
    def _():
        for block in range(groups):
            for piece in range(CHUNKS):
                lift_copy(acts.at[span(piece)], block, piece).wait_send()

    line.finish()
    for store in stores:
        store.wait()


def front(fresh_weight, acts, grads, factor_old, cross_old):
    layers, groups = lax.axis_size("layer"), lax.axis_size("dp")
    rows, features = factor_old.shape
    count = acts.shape[0]
    chunk, columns = grads.shape[1:]
    every = count * groups
    half, full = jnp.bfloat16, jnp.float32
    dma = pltpu.SemaphoreType.DMA
    shape = jax.ShapeDtypeStruct
    return pl.pallas_call(
        functools.partial(front_kernel, fresh_weight),
        out_shape=[shape((rows, features), half)] * 5
        + [shape((layers, chunk, columns), half)] * 3
        + [shape((layers, chunk, 128), full), shape((rows, 128), full)],
        in_specs=[pl.BlockSpec(memory_space=pl.ANY)] * 4,
        out_specs=[pl.BlockSpec(memory_space=pl.ANY)] * 10,
        scratch_shapes=[
            pltpu.VMEM((groups, count, features), half),
            pltpu.VMEM((groups, count, features), half),
            pltpu.VMEM((rows, features), full),
            pltpu.VMEM((rows, features), full),
            pltpu.VMEM((rows, features), half),
            pltpu.VMEM((groups, rows, rows), half),
            pltpu.VMEM((layers, chunk, columns), half),
            pltpu.VMEM((layers, chunk, columns), half),
            pltpu.VMEM((layers, chunk, 256), full),
            pltpu.VMEM((groups, 8, rows), full),
            pltpu.VMEM((groups, 8, rows), full),
            pltpu.VMEM((rows, 128), full),
            pltpu.VMEM((layers, chunk, 128), full),
            pltpu.VMEM((rows, every), half),
            pltpu.VMEM((rows, every), half),
        ]
        + [pltpu.VMEM((rows, features), half)] * 5
        + [dma((2, groups - 1, CHUNKS))] * 2
        + [dma((groups, CHUNKS))] * 2
        + [dma((layers - 1,))] * 2
        + [dma((groups - 1,))] * 2
        + [dma((layers - 1,))] * 4
        + [dma((groups - 1,))] * 2
        + [dma((10,))],
        compiler_params=pltpu.CompilerParams(
            collective_id=0, has_side_effects=True, vmem_limit_bytes=63 << 20
        ),
        cost_estimate=pl.CostEstimate(
            flops=6 * every * rows * features, bytes_accessed=200_000_000, transcendentals=0
        ),
        name="front",
    )(acts, grads, factor_old, cross_old)


PIECES = 4


def back_kernel(
    factor_high_in, factor_low_in, cross_high_in, cross_low_in, turned_in,
    initial_in, grads_in, solved_in, scales_in, own_scales_in, moments_in, exponents_in, master_in,
    moments_out, master_out, replicas_out,
    factor_high, factor_low, cross_high, cross_low, turned,
    initial, grads, solved, scales, own_scales, moments, powers, master,
    full, upper, away, lowered, away_in, lowered_in, scaled, fixed, fixed_in,
    moments_new, master_new, replicas,
    first_send, first_recv, last_send, last_recv, lift_send, lift_recv,
    away_send, away_recv, lowered_send, lowered_recv, fixed_send, fixed_recv, load_sem, store_sem,
):
    layers, groups = lax.axis_size("layer"), lax.axis_size("dp")
    layer, group = lax.axis_index("layer"), lax.axis_index("dp")
    rows, columns = initial.shape
    chunk = rows // layers
    width = columns // PIECES
    features = rows * groups

    def cut(piece):
        return slice(piece * width, (piece + 1) * width)

    pairs = (
        (initial_in, initial),
        (factor_high_in, factor_high),
        (factor_low_in, factor_low),
        (cross_high_in, cross_high),
        (cross_low_in, cross_low),
        (turned_in, turned),
        (own_scales_in, own_scales),
        (grads_in, grads),
        (solved_in, solved),
        (scales_in, scales),
        (moments_in, moments),
        (exponents_in, powers),
        (master_in, master),
    )
    loads = [
        pltpu.make_async_copy(source, target, load_sem.at[place])
        for place, (source, target) in enumerate(pairs)
    ]
    for load in loads:
        load.start()
    greet()

    first = Line(
        "dp",
        lambda piece: initial_in.at[:, cut(piece)],
        lambda block, piece: full.at[piece, block],
        first_send,
        first_recv,
        PIECES,
    )
    last = Line(
        "dp",
        lambda piece: replicas.at[piece],
        lambda block, piece: replicas_out.at[block, :, cut(piece)],
        last_send,
        last_recv,
        PIECES,
    )

    def lift_copy(source, block, piece):
        return remote(
            source, upper.at[piece, block], lift_send.at[piece, block], lift_recv.at[piece, block],
            "layer", -1,
        )

    def lift(block, piece):
        @pl.when(layer > 0)
        def _():
            lift_copy(full.at[piece, block], block, piece).start()

    def begin(piece):
        first.begin([piece])

        @pl.when(layer > 0)
        def _():
            lift_copy(initial_in.at[:, cut(piece)], group, piece).start()

    begin(0)
    begin(1)

    @pl.when(layer == layers - 1)
    def _():
        upper[...] = jnp.zeros_like(upper)

    loads[0].wait()
    for piece in range(PIECES):
        full[piece, group] = initial[:, cut(piece)]

    def relay_copy(which, piece, step):
        source, target, send_sem, recv_sem = (
            (away, away_in, away_send, away_recv),
            (lowered, lowered_in, lowered_send, lowered_recv),
            (fixed, fixed_in, fixed_send, fixed_recv),
        )[which]
        peer = lax.rem(layer + step, layers)
        return remote(
            source.at[piece, peer], target.at[piece, layer],
            send_sem.at[step - 1, piece], recv_sem.at[step - 1, piece], "layer", step,
        )

    def multiply(piece):
        @pl.when(layer < layers - 1)
        def _():
            for block in range(groups):
                lift_copy(full.at[piece, block], block, piece).wait_recv()

        def some(place, carry):
            part = pl.ds(pl.multiple_of(place * chunk * 2, chunk * 2), chunk * 2)
            mine = full[piece].reshape(features, width)
            theirs = upper[piece].reshape(features, width)
            low = product(turned[part, :], mine)
            value = product(factor_high[part, :], mine) + product(factor_low[part, :], mine)
            value = value - own_scales[part, 2:3] * full[piece, group, part, :].astype(jnp.float32)
            value = value + product(cross_high[part, :], theirs) + product(cross_low[part, :], theirs)
            value = value - own_scales[part, 1:2] * upper[piece, group, part, :].astype(jnp.float32)
            for side in range(2):
                inner = slice(side * chunk, (side + 1) * chunk)
                away[piece, 2 * place + side] = value[inner].astype(jnp.bfloat16)
                lowered[piece, 2 * place + side] = low[inner].astype(jnp.bfloat16)
            return carry

        lax.fori_loop(0, layers // 2, some, 0)
        for step in range(layers - 1, 0, -1):
            relay_copy(0, piece, step).start()
            relay_copy(1, piece, step).start()
        away_in[piece, layer] = away[piece, layer]
        lowered_in[piece, layer] = lowered[piece, layer]

    def correct(piece):
        for step in range(layers - 1, 0, -1):
            relay_copy(0, piece, step).wait_recv()
            relay_copy(1, piece, step).wait_recv()
        part = cut(piece)

        def wide(ref, place):
            return ref[place, :, part].astype(jnp.float32)

        passed = None
        for place in range(layers):
            target = wide(grads, place) - scales[place, :, 0:1] * wide(solved, place)
            if place < layers - 1:
                target = target - scales[place, :, 1:2] * wide(solved, place + 1)
            target = target - away_in[piece, place].astype(jnp.float32)
            if place:
                target = target - scales[place - 1, :, 1:2] * wide(solved, place - 1)
                target = target - lowered_in[piece, place - 1].astype(jnp.float32)
                target = target - passed
            value = target / scales[place, :, 0:1]
            scaled[place] = value
            passed = scales[place, :, 1:2] * value
        result = value
        fixed[piece, layers - 1] = result.astype(jnp.bfloat16)
        for place in range(layers - 2, -1, -1):
            ratio = scales[place, :, 1:2] / scales[place, :, 0:1]
            result = scaled[place] - ratio * result
            fixed[piece, place] = result.astype(jnp.bfloat16)
        for step in range(layers - 1, 0, -1):
            relay_copy(2, piece, step).start()
        fixed_in[piece, layer] = fixed[piece, layer]

    stores = []

    def update(piece):
        for step in range(layers - 1, 0, -1):
            relay_copy(2, piece, step).wait_recv()
        part = cut(piece)

        def some(place, carry):
            inner = pl.ds(pl.multiple_of(place * chunk, chunk), chunk)
            change = initial[inner, part].astype(jnp.float32) + fixed_in[piece, place].astype(
                jnp.float32
            )
            moment = MOMENTUM * moments[inner, part].astype(jnp.float32) * powers[inner, 0:1]
            moment = moment + (1.0 - MOMENTUM) * change
            moments_new[inner, part] = (moment * powers[inner, 1:2]).astype(jnp.bfloat16)
            weights = master[inner, part] - STEP_SIZE * moment
            master_new[inner, part] = weights
            replicas[piece, inner, :] = weights.astype(jnp.bfloat16)
            return carry

        lax.fori_loop(0, layers, some, 0)
        last.begin([piece])
        for place, (source, target) in enumerate(
            (
                (replicas.at[piece], replicas_out.at[group, :, part]),
                (master_new.at[:, part], master_out.at[:, part]),
                (moments_new.at[:, part], moments_out.at[:, part]),
            )
        ):
            stores.append(pltpu.make_async_copy(source, target, store_sem.at[place, piece]))
            stores[-1].start()

    far = groups - 1
    for hop in range(1, far):
        first.arrive(hop, [0], lift)
    for load in loads[1:]:
        load.wait()
    if PIECES > 2:
        begin(2)
    first.arrive(1, [1], lift)
    for piece in range(PIECES):
        first.arrive(far, [piece], lift)
        if piece + 1 < PIECES:
            for hop in range(2, far):
                first.arrive(hop, [piece + 1], lift)
        if piece + 3 < PIECES:
            begin(piece + 3)
        multiply(piece)
        if piece + 2 < PIECES:
            first.arrive(1, [piece + 2], lift)
        if piece:
            update(piece - 1)
        if piece > 1:
            for hop in range(1, far):
                last.arrive(hop, [piece - 2])
        correct(piece)
    last.arrive(far, [0])
    for hop in range(1, far):
        last.arrive(hop, [PIECES - 2])
    update(PIECES - 1)
    for piece in range(1, PIECES - 1):
        last.arrive(far, [piece])
    for hop in range(1, groups):
        last.arrive(hop, [PIECES - 1])

    for piece in range(PIECES):
        for step in range(1, layers):
            for which in range(3):
                relay_copy(which, piece, step).wait_send()

        @pl.when(layer > 0)
        def _():
            for block in range(groups):
                lift_copy(full.at[piece, block], block, piece).wait_send()

    first.finish()
    last.finish()
    for store in stores:
        store.wait()


def back(matrices, initial, grads, solved, scales, own_scales, moments, powers, master):
    layers, groups = lax.axis_size("layer"), lax.axis_size("dp")
    rows, columns = initial.shape
    features = matrices[0].shape[1]
    chunk, width = rows // layers, columns // PIECES
    half, full = jnp.bfloat16, jnp.float32
    dma = pltpu.SemaphoreType.DMA
    shape = jax.ShapeDtypeStruct
    swapped = pltpu.VMEM((PIECES, layers, chunk, width), half)
    return pl.pallas_call(
        back_kernel,
        out_shape=[
            shape((rows, columns), half),
            shape((rows, columns), full),
            shape((groups, rows, columns), half),
        ],
        in_specs=[pl.BlockSpec(memory_space=pl.ANY)] * 13,
        out_specs=[pl.BlockSpec(memory_space=pl.ANY)] * 3,
        scratch_shapes=[pltpu.VMEM((rows, features), half)] * 5
        + [
            pltpu.VMEM((rows, columns), half),
            pltpu.VMEM((layers, chunk, columns), half),
            pltpu.VMEM((layers, chunk, columns), half),
            pltpu.VMEM((layers, chunk, 128), full),
            pltpu.VMEM((rows, 128), full),
            pltpu.VMEM((rows, columns), half),
            pltpu.VMEM((rows, 128), full),
            pltpu.VMEM((rows, columns), full),
            pltpu.VMEM((PIECES, groups, rows, width), half),
            pltpu.VMEM((PIECES, groups, rows, width), half),
        ]
        + [swapped] * 4
        + [pltpu.VMEM((layers, chunk, width), full)]
        + [swapped] * 2
        + [
            pltpu.VMEM((rows, columns), half),
            pltpu.VMEM((rows, columns), full),
            pltpu.VMEM((PIECES, rows, width), half),
        ]
        + [dma((2, groups - 1, PIECES))] * 4
        + [dma((PIECES, groups))] * 2
        + [dma((layers - 1, PIECES))] * 6
        + [dma((13,)), dma((3, PIECES))],
        compiler_params=pltpu.CompilerParams(
            collective_id=1, has_side_effects=True, vmem_limit_bytes=63 << 20
        ),
        cost_estimate=pl.CostEstimate(
            flops=10 * features * rows * columns, bytes_accessed=300_000_000, transcendentals=0
        ),
        name="back",
    )(*matrices, initial, grads, solved, scales, own_scales, moments, powers, master)


def body(activations, factor_old, cross_old, gradients, moments, exponents, master):
    layers, groups = lax.axis_size("layer"), lax.axis_size("dp")
    row_count, features = factor_old.shape[1:]
    columns = gradients.shape[2]
    chunk = row_count // layers
    fresh_weight = (1.0 - FACTOR_DECAY) / (activations.shape[1] * groups)
    powers = jnp.repeat(exponents[0].astype(jnp.float32), SCALE_BLOCK)[:, None]
    lane = lax.broadcasted_iota(jnp.int32, (row_count, 128), 1)
    powers = jnp.exp2(jnp.where(lane == 0, powers, -powers))
    *matrices, initial, grad_swapped, initial_swapped, scales, own_scales = front(
        fresh_weight,
        activations[0],
        gradients[0].reshape(layers, chunk, columns),
        factor_old[0],
        cross_old[0],
    )
    moments_new, master_new, replicas = back(
        matrices,
        initial.reshape(row_count, columns),
        grad_swapped,
        initial_swapped,
        scales,
        own_scales,
        moments[0],
        powers,
        master[0],
    )
    factor_high, factor_low, cross_high, cross_low, _ = matrices
    factor_new = factor_high.astype(jnp.float32) + factor_low.astype(jnp.float32)
    cross_new = cross_high.astype(jnp.float32) + cross_low.astype(jnp.float32)
    replicas = replicas.reshape(features, columns)
    return (factor_new[None], cross_new[None], moments_new[None], master_new[None], replicas[None])


def solution(mesh):
    return jax.shard_map(
        body,
        mesh=mesh,
        in_specs=(
            P("layer", "dp", None),
            P("layer", "dp", None),
            P("layer", "dp", None),
            P("layer", "dp", None),
            P("layer", "dp", None),
            P("layer", "dp"),
            P("layer", "dp", None),
        ),
        out_specs=(
            P("layer", "dp", None),
            P("layer", "dp", None),
            P("layer", "dp", None),
            P("layer", "dp", None),
            P("layer", None, None),
        ),
        check_vma=False,
    )
```

```python
import functools

import jax
import jax.numpy as jnp
from jax import lax
from jax.experimental import pallas as pl
from jax.experimental.pallas import tpu as pltpu
from jax.sharding import PartitionSpec as P

SCALE_BLOCK = 128


FACTOR_DECAY = 0.9
DAMPING = 0.5
MOMENTUM = 0.8
STEP_SIZE = 0.05

MESH = pl.DeviceIdType.MESH


def product(left, right):
    return jnp.dot(left, right, preferred_element_type=jnp.float32)


CHUNKS = 4


def column_of(row, eye):
    return jnp.sum(jnp.where(eye, jnp.broadcast_to(row, eye.shape), 0.0), axis=1, keepdims=True)


def identity(size):
    return lax.broadcasted_iota(jnp.int32, (size, size), 0) == lax.broadcasted_iota(
        jnp.int32, (size, size), 1
    )


def greet():
    barrier = pltpu.get_barrier_semaphore()
    total = 0
    for axis in ("layer", "dp"):
        count, mine = lax.axis_size(axis), lax.axis_index(axis)
        for step in range(1, count):
            pl.semaphore_signal(
                barrier, inc=1, device_id={axis: lax.rem(mine + step, count)}, device_id_type=MESH
            )
        total += count - 1
    pl.semaphore_wait(barrier, total)


def remote(source, target, send_sem, recv_sem, axis, step):
    count, mine = lax.axis_size(axis), lax.axis_index(axis)
    return pltpu.make_async_remote_copy(
        src_ref=source,
        dst_ref=target,
        send_sem=send_sem,
        recv_sem=recv_sem,
        device_id={axis: lax.rem(mine + step + count, count)},
        device_id_type=MESH,
    )


class Line:
    def __init__(self, axis, source, target, send_sem, recv_sem, pieces):
        self.axis, self.count, self.mine = axis, lax.axis_size(axis), lax.axis_index(axis)
        self.source, self.target, self.pieces = source, target, pieces
        self.send_sem, self.recv_sem = send_sem, recv_sem

    def copy(self, way, hop, piece):
        sign = 1 if way == 0 else -1
        block = jnp.clip(self.mine - sign * hop, 0, self.count - 1)
        landing = self.target(block, piece)
        return remote(
            self.source(piece) if hop == 0 else landing,
            landing,
            self.send_sem.at[way, hop, piece],
            self.recv_sem.at[way, hop, piece],
            self.axis,
            sign,
        )

    def has_next(self, way):
        return self.mine < self.count - 1 if way == 0 else self.mine > 0

    def has_block(self, way, hop):
        return self.mine >= hop if way == 0 else self.mine + hop <= self.count - 1

    def begin(self, pieces):
        for piece in pieces:
            for way in (0, 1):

                @pl.when(self.has_next(way))
                def _():
                    self.copy(way, 0, piece).start()

    def arrive(self, hop, pieces, then=None):
        for piece in pieces:
            for way in (0, 1):

                @pl.when(self.has_block(way, hop))
                def _():
                    self.copy(way, hop - 1, piece).wait_recv()
                    if hop < self.count - 1:

                        @pl.when(self.has_next(way))
                        def _():
                            self.copy(way, hop, piece).start()

                    if then is not None:
                        sign = 1 if way == 0 else -1
                        then(jnp.clip(self.mine - sign * hop, 0, self.count - 1), piece)

    def finish(self):
        for hop in range(self.count - 1):
            for piece in range(self.pieces):
                for way in (0, 1):

                    @pl.when(self.has_next(way) & self.has_block(way, hop))
                    def _():
                        self.copy(way, hop, piece).wait_send()


def front_kernel(
    fresh_weight,
    acts, grads, factor_old, cross_old,
    factor_out, cross_out, factor_high_out, factor_low_out, cross_high_out, cross_low_out, mixed_out,
    initial_out, above_out, grads_out, solved_out, scales_out, own_scales_out,
    tokens, upper, factor, cross, cross_cut, blocks, grads_in, solved, scaled,
    sums_away, sums_in, own_scales, scales, own_turned, upper_turned,
    factor_high, factor_low, cross_high, cross_low, mixed, fresh,
    line_send, line_recv, lift_send, lift_recv, grad_send, grad_recv, sum_send, sum_recv,
    scale_send, scale_recv, start_send, start_recv, block_send, block_recv, above_send, above_recv,
    local_sem,
):
    layers, groups = lax.axis_size("layer"), lax.axis_size("dp")
    layer, group = lax.axis_index("layer"), lax.axis_index("dp")
    rows, features = factor.shape
    count = acts.shape[0]
    part = count // CHUNKS
    chunk = rows // layers
    columns = grads.shape[2]
    own = pl.ds(pl.multiple_of(group * rows, rows), rows)

    def span(piece):
        return pl.ds(piece * part, part)

    load_acts = pltpu.make_async_copy(acts, tokens.at[group], local_sem.at[0])
    load_factor = pltpu.make_async_copy(factor_old, factor, local_sem.at[1])
    load_cross = pltpu.make_async_copy(cross_old, cross, local_sem.at[2])
    load_grads = pltpu.make_async_copy(grads.at[layer], grads_in.at[layer], local_sem.at[3])
    load_acts.start()
    load_cross.start()
    load_factor.start()
    load_grads.start()
    greet()

    line = Line(
        "dp",
        lambda piece: acts.at[span(piece)],
        lambda block, piece: tokens.at[block, span(piece)],
        line_send,
        line_recv,
        CHUNKS,
    )

    def lift_copy(source, block, piece):
        return remote(
            source,
            upper.at[block, span(piece)],
            lift_send.at[block, piece],
            lift_recv.at[block, piece],
            "layer",
            -1,
        )

    def lift(block, piece):
        @pl.when(layer > 0)
        def _():
            lift_copy(tokens.at[block, span(piece)], block, piece).start()

    @pl.when(layer > 0)
    def _():
        for piece in range(CHUNKS):
            lift_copy(acts.at[span(piece)], group, piece).start()

    def grad_copy(step):
        peer = lax.rem(layer + step, layers)
        return remote(
            grads.at[peer], grads_in.at[layer], grad_send.at[step - 1], grad_recv.at[step - 1],
            "layer", step,
        )

    for step in range(layers - 1, 0, -1):
        grad_copy(step).start()
    line.begin(range(CHUNKS // 2))

    load_acts.wait()
    sums_away[...] = jnp.zeros_like(sums_away)
    for place in range(groups):
        wide = tokens[group, :, place * rows : (place + 1) * rows].astype(jnp.float32)
        sums_away[place, 0:1, :] = jnp.sum(wide * wide, axis=0, keepdims=True)
    load_cross.wait()
    load_factor.wait()
    eye = identity(rows)
    factor_diagonal = jnp.sum(jnp.where(eye, factor[:, own], 0.0), axis=1, keepdims=True)
    cross_diagonal = jnp.sum(jnp.where(eye, cross[:, own], 0.0), axis=1, keepdims=True)

    @pl.when(layer < layers - 1)
    def _():
        for piece in range(CHUNKS):
            lift_copy(acts.at[span(piece)], group, piece).wait_recv()
        for place in range(groups):
            cut = slice(place * rows, (place + 1) * rows)
            wide = tokens[group, :, cut].astype(jnp.float32)
            above = upper[group, :, cut].astype(jnp.float32)
            sums_away[place, 1:2, :] = jnp.sum(wide * above, axis=0, keepdims=True)

    @pl.when(layer == layers - 1)
    def _():
        upper[...] = jnp.zeros_like(upper)

    def sum_copy(step):
        peer = lax.rem(group + step, groups)
        return remote(
            sums_away.at[peer], sums_in.at[group], sum_send.at[step - 1], sum_recv.at[step - 1],
            "dp", step,
        )

    for step in range(groups - 1, 0, -1):
        sum_copy(step).start()
    line.begin(range(CHUNKS // 2, CHUNKS))
    sums_in[group] = sums_away[group]
    line.arrive(1, range(CHUNKS // 2))

    for step in range(groups - 1, 0, -1):
        sum_copy(step).wait_recv()
    sums = fresh_weight * jnp.sum(sums_in[...], axis=0)
    own_sum = column_of(sums[0:1], eye)
    next_sum = column_of(sums[1:2], eye)
    own_diagonal = FACTOR_DECAY * factor_diagonal + own_sum
    own_coupling = FACTOR_DECAY * cross_diagonal + next_sum
    lane = lax.broadcasted_iota(jnp.int32, (rows, 128), 1)
    own_scales[...] = jnp.where(
        lane == 0,
        DAMPING + own_diagonal,
        jnp.where(lane == 1, own_coupling, jnp.where(lane == 2, own_diagonal, next_sum)),
    )

    def scale_copy(step):
        peer = lax.rem(layer + step, layers)
        return remote(
            own_scales.at[pl.ds(pl.multiple_of(peer * chunk, chunk), chunk)],
            scales.at[layer], scale_send.at[step - 1], scale_recv.at[step - 1], "layer", step,
        )

    for step in range(layers - 1, 0, -1):
        scale_copy(step).start()
    scales[layer] = own_scales[pl.ds(pl.multiple_of(layer * chunk, chunk), chunk), :]
    line.arrive(1, range(CHUNKS // 2, CHUNKS))
    load_grads.wait()
    for step in range(layers - 1, 0, -1):
        scale_copy(step).wait_recv()
        grad_copy(step).wait_recv()

    width = scaled.shape[2]

    def solve(tile, carry):
        cut = pl.ds(pl.multiple_of(tile * width, width), width)
        passed = None
        for place in range(layers):
            target = grads_in[place, :, cut].astype(jnp.float32)
            if place:
                target = target - passed
            value = target / scales[place, :, 0:1]
            scaled[place] = value
            passed = scales[place, :, 1:2] * value
        result = value
        solved[layers - 1, :, cut] = result.astype(jnp.bfloat16)
        for place in range(layers - 2, -1, -1):
            ratio = scales[place, :, 1:2] / scales[place, :, 0:1]
            result = scaled[place] - ratio * result
            solved[place, :, cut] = result.astype(jnp.bfloat16)
        return carry

    lax.fori_loop(0, columns // width, solve, 0)

    def start_copy(step):
        peer = lax.rem(layer + step, layers)
        return remote(
            solved.at[peer], initial_out.at[layer], start_send.at[step - 1],
            start_recv.at[step - 1], "layer", step,
        )

    for step in range(layers - 1, 0, -1):
        start_copy(step).start()
    stores = [
        pltpu.make_async_copy(solved.at[layer], initial_out.at[layer], local_sem.at[0]),
        pltpu.make_async_copy(grads_in, grads_out, local_sem.at[1]),
        pltpu.make_async_copy(solved, solved_out, local_sem.at[2]),
        pltpu.make_async_copy(scales, scales_out, local_sem.at[3]),
        pltpu.make_async_copy(own_scales, own_scales_out, local_sem.at[4]),
    ]
    for copy in stores:
        copy.start()

    def narrow(tile, carry):
        cut = pl.ds(pl.multiple_of(tile * rows, rows), rows)
        cross_cut[:, cut] = cross[:, cut].astype(jnp.bfloat16)
        return carry

    lax.fori_loop(0, groups, narrow, 0)
    blocks[group] = jnp.where(eye, 0.0, cross[:, own]).astype(jnp.bfloat16)

    for way in (0, 1):

        @pl.when(line.has_block(way, 1))
        def _():
            for piece in range(CHUNKS):
                lift(jnp.clip(group - (1 if way == 0 else -1), 0, groups - 1), piece)

    for hop in range(2, groups - 1):
        line.arrive(hop, range(CHUNKS), lift)

    def block_copy(step):
        peer = lax.rem(group + step, groups)
        return remote(
            cross_cut.at[:, pl.ds(pl.multiple_of(peer * rows, rows), rows)],
            blocks.at[group], block_send.at[step - 1], block_recv.at[step - 1], "dp", step,
        )

    for step in range(groups - 1, 0, -1):
        block_copy(step).start()
    for step in range(1, layers):
        start_copy(step).wait_recv()
    stores[0].wait()
    above_copy = remote(initial_out, above_out, above_send, above_recv, "layer", -1)

    @pl.when(layer > 0)
    def _():
        above_copy.start()

    line.arrive(groups - 1, range(CHUNKS), lift)

    tile = 256
    every = count * groups

    def gather(ref, cut):
        return ref[:, :, cut].reshape(every, cut.size)

    def place_halves(value, high, low, cut):
        value = value.T
        first = value.astype(jnp.bfloat16)
        high[cut, :] = first
        low[cut, :] = (value - first.astype(jnp.float32)).astype(jnp.bfloat16)

    own_turned[...] = gather(tokens, own).astype(jnp.float32).T.astype(jnp.bfloat16)

    def refresh_factor(place, carry):
        cut = pl.ds(pl.multiple_of(place * tile, tile), tile)
        value = product(own_turned[...], gather(tokens, cut))
        value = FACTOR_DECAY * factor[:, cut] + fresh_weight * value
        factor[:, cut] = value
        place_halves(value, factor_high, factor_low, cut)
        return carry

    lax.fori_loop(0, features // tile, refresh_factor, 0)

    def store(*pairs):
        for source, target in pairs:
            stores.append(pltpu.make_async_copy(source, target, local_sem.at[len(stores)]))
            stores[-1].start()

    store((factor, factor_out), (factor_high, factor_high_out), (factor_low, factor_low_out))

    @pl.when(layer < layers - 1)
    def _():
        for step in range(1, groups):
            block = lax.rem(group + step, groups)
            for piece in range(CHUNKS):
                lift_copy(acts.at[span(piece)], block, piece).wait_recv()

    upper_turned[...] = gather(upper, own).astype(jnp.float32).T.astype(jnp.bfloat16)

    def refresh_cross(place, carry):
        cut = pl.ds(pl.multiple_of(place * tile, tile), tile)
        value = product(own_turned[...], gather(upper, cut))
        value = FACTOR_DECAY * cross[:, cut] + fresh_weight * value
        cross[:, cut] = value
        place_halves(value, cross_high, cross_low, cut)
        fresh[cut, :] = fresh_weight * product(upper_turned[...], gather(tokens, cut)).T
        return carry

    lax.fori_loop(0, features // tile, refresh_cross, 0)
    store((cross, cross_out), (cross_high, cross_high_out), (cross_low, cross_low_out))

    fresh[own, :] = jnp.where(eye, 0.0, fresh[own, :])
    for step in range(groups - 1, 0, -1):
        block_copy(step).wait_recv()

    def join(place, carry):
        cut = pl.ds(pl.multiple_of(place * rows, rows), rows)
        old = FACTOR_DECAY * blocks[place].astype(jnp.float32)
        mixed[cut, :] = (old + fresh[cut, :]).astype(jnp.bfloat16)
        return carry

    lax.fori_loop(0, groups, join, 0)
    store((mixed, mixed_out))

    @pl.when(layer > 0)
    def _():
        above_copy.wait_send()

    @pl.when(layer < layers - 1)
    def _():
        above_copy.wait_recv()

    for step in range(1, layers):
        start_copy(step).wait_send()
        grad_copy(step).wait_send()
        scale_copy(step).wait_send()
    for step in range(1, groups):
        sum_copy(step).wait_send()
        block_copy(step).wait_send()

    @pl.when(layer > 0)
    def _():
        for block in range(groups):
            for piece in range(CHUNKS):
                lift_copy(acts.at[span(piece)], block, piece).wait_send()

    line.finish()
    for copy in stores[1:]:
        copy.wait()


def front(fresh_weight, acts, grads, factor_old, cross_old):
    layers, groups = lax.axis_size("layer"), lax.axis_size("dp")
    rows, features = factor_old.shape
    count = acts.shape[0]
    chunk, columns = grads.shape[1:]
    every = count * groups
    half, full = jnp.bfloat16, jnp.float32
    dma = pltpu.SemaphoreType.DMA
    shape = jax.ShapeDtypeStruct
    return pl.pallas_call(
        functools.partial(front_kernel, fresh_weight),
        out_shape=[shape((rows, features), full)] * 2
        + [shape((features, rows), half)] * 5
        + [shape((layers, chunk, columns), half)] * 4
        + [shape((layers, chunk, 128), full), shape((rows, 128), full)],
        in_specs=[pl.BlockSpec(memory_space=pl.ANY)] * 4,
        out_specs=[pl.BlockSpec(memory_space=pl.ANY)] * 13,
        scratch_shapes=[
            pltpu.VMEM((groups, count, features), half),
            pltpu.VMEM((groups, count, features), half),
            pltpu.VMEM((rows, features), full),
            pltpu.VMEM((rows, features), full),
            pltpu.VMEM((rows, features), half),
            pltpu.VMEM((groups, rows, rows), half),
            pltpu.VMEM((layers, chunk, columns), half),
            pltpu.VMEM((layers, chunk, columns), half),
            pltpu.VMEM((layers, chunk, 256), full),
            pltpu.VMEM((groups, 8, rows), full),
            pltpu.VMEM((groups, 8, rows), full),
            pltpu.VMEM((rows, 128), full),
            pltpu.VMEM((layers, chunk, 128), full),
            pltpu.VMEM((rows, every), half),
            pltpu.VMEM((rows, every), half),
        ]
        + [pltpu.VMEM((features, rows), half)] * 5
        + [pltpu.VMEM((features, rows), full)]
        + [dma((2, groups - 1, CHUNKS))] * 2
        + [dma((groups, CHUNKS))] * 2
        + [dma((layers - 1,))] * 2
        + [dma((groups - 1,))] * 2
        + [dma((layers - 1,))] * 4
        + [dma((groups - 1,))] * 2
        + [dma] * 2
        + [dma((12,))],
        compiler_params=pltpu.CompilerParams(
            collective_id=0, has_side_effects=True, vmem_limit_bytes=63 << 20
        ),
        cost_estimate=pl.CostEstimate(
            flops=6 * every * rows * features, bytes_accessed=200_000_000, transcendentals=0
        ),
        name="front",
    )(acts, grads, factor_old, cross_old)


PIECES = 4


class Sums:
    def __init__(self, axis, source, target, send_sem, recv_sem):
        self.axis, self.count, self.mine = axis, lax.axis_size(axis), lax.axis_index(axis)
        self.source, self.target = source, target
        self.send_sem, self.recv_sem = send_sem, recv_sem

    def copy(self, way, piece, owner):
        return remote(
            self.source(piece, owner),
            self.target(way, piece, owner),
            self.send_sem.at[way, piece, owner],
            self.recv_sem.at[way, piece, owner],
            self.axis,
            1 if way == 0 else -1,
        )

    def has_before(self, way):
        return self.mine > 0 if way == 0 else self.mine < self.count - 1

    def step(self, piece, distance, add):
        for way in (0, 1):
            sign = 1 if way == 0 else -1
            owner = self.mine + sign * distance

            @pl.when((owner >= 0) & (owner < self.count))
            def _():
                place = jnp.clip(owner, 0, self.count - 1)

                @pl.when(self.has_before(way))
                def _():
                    self.copy(way, piece, place).wait_recv()

                add(way, piece, place)
                self.copy(way, piece, place).start()

    def close(self, piece):
        for way in (0, 1):

            @pl.when(self.has_before(way))
            def _():
                self.copy(way, piece, self.mine).wait_recv()

    def finish(self, pieces):
        for piece in range(pieces):
            for distance in range(1, self.count):
                for way in (0, 1):
                    owner = self.mine + (distance if way == 0 else -distance)

                    @pl.when((owner >= 0) & (owner < self.count))
                    def _():
                        self.copy(way, piece, jnp.clip(owner, 0, self.count - 1)).wait_send()


def back_kernel(
    exponents,
    factor_high_in, factor_low_in, cross_high_in, cross_low_in, mixed_in,
    initial_in, above_in, grads_in, solved_in, scales_in, own_scales_in, moments_in, master_in,
    moments_out, master_out, replicas_out,
    factor_high, factor_low, cross_high, cross_low, mixed,
    initial, above, grads, solved, scales, own_scales, moments, master, powers,
    below, below_in, shares, sums, sums_in, applied, applied_in, scaled, fixed, fixed_in,
    moments_new, master_new, replicas,
    last_send, last_recv, below_send, below_recv, sum_send, sum_recv,
    applied_send, applied_recv, fixed_send, fixed_recv, load_sem, store_sem,
):
    layers, groups = lax.axis_size("layer"), lax.axis_size("dp")
    layer, group = lax.axis_index("layer"), lax.axis_index("dp")
    rows, columns = initial.shape
    chunk = rows // layers
    width = columns // PIECES

    def cut(piece):
        return slice(piece * width, (piece + 1) * width)

    def block(place):
        return pl.ds(pl.multiple_of(place * rows, rows), rows)

    pairs = (
        (initial_in, initial),
        (cross_high_in, cross_high),
        (cross_low_in, cross_low),
        (own_scales_in, own_scales),
        (factor_high_in, factor_high),
        (factor_low_in, factor_low),
        (mixed_in, mixed),
        (grads_in, grads),
        (solved_in, solved),
        (scales_in, scales),
        (moments_in, moments),
        (master_in, master),
    )
    loads = [
        pltpu.make_async_copy(source, target, load_sem.at[place])
        for place, (source, target) in enumerate(pairs)
    ]
    load_above = pltpu.make_async_copy(above_in, above, load_sem.at[len(pairs)])

    for load in loads[:7]:
        load.start()

    @pl.when(layer < layers - 1)
    def _():
        load_above.start()

    for load in loads[7:]:
        load.start()

    greet()

    line = Sums(
        "dp",
        lambda piece, owner: sums.at[piece, owner],
        lambda way, piece, owner: sums_in.at[way, piece, owner],
        sum_send,
        sum_recv,
    )
    last = Line(
        "dp",
        lambda piece: replicas.at[piece],
        lambda place, piece: replicas_out.at[place, :, cut(piece)],
        last_send,
        last_recv,
        PIECES,
    )

    def below_copy(piece, owner):
        return remote(
            below.at[piece, owner], below_in.at[piece, owner],
            below_send.at[piece, owner], below_recv.at[piece, owner], "layer", 1,
        )

    @pl.when(layer == layers - 1)
    def _():
        above[...] = jnp.zeros_like(above)

    @pl.when(layer == 0)
    def _():
        below_in[...] = jnp.zeros_like(below_in)

    for load in loads[:4]:
        load.wait()

    def lend(piece):
        part = cut(piece)

        @pl.when(layer < layers - 1)
        def _():
            mine = initial[:, part]

            def some(turn, carry):
                place = jnp.where(2 * group < groups, groups - 1 - turn, turn)
                value = product(cross_high[block(place), :], mine)
                value = value + product(cross_low[block(place), :], mine)
                below[piece, place] = value.astype(jnp.bfloat16)

                @pl.when(place == group)
                def _():
                    near = value - own_scales[:, 1:2] * mine.astype(jnp.float32)
                    below[piece, place] = near.astype(jnp.bfloat16)

                below_copy(piece, place).start()
                return carry

            lax.fori_loop(0, groups, some, 0)

    def share(piece):
        part = cut(piece)
        mine, theirs = initial[:, part], above[:, part]

        def some(place, carry):
            value = product(factor_high[block(place), :], mine)
            value = value + product(factor_low[block(place), :], mine)
            shares[piece, place] = value + product(mixed[block(place), :], theirs)
            return carry

        lax.fori_loop(0, groups, some, 0)
        shares[piece, group] = shares[piece, group] - own_scales[:, 2:3] * mine.astype(jnp.float32)

    def add(way, piece, place):
        @pl.when(layer > 0)
        def _():
            below_copy(piece, place).wait_recv()

        value = shares[piece, place] + below_in[piece, place].astype(jnp.float32)
        value = value + sums_in[way, piece, place].astype(jnp.float32)
        sums[piece, place] = value.astype(jnp.bfloat16)

    def swap_copy(which, piece, step):
        source, target, send_sem, recv_sem = (
            (applied, applied_in, applied_send, applied_recv),
            (fixed, fixed_in, fixed_send, fixed_recv),
        )[which]
        peer = lax.rem(layer + step, layers)
        return remote(
            source.at[piece, peer], target.at[piece, layer],
            send_sem.at[step - 1, piece], recv_sem.at[step - 1, piece], "layer", step,
        )

    def swap(which, piece):
        for step in range(layers - 1, 0, -1):
            swap_copy(which, piece, step).start()

    def join(piece):
        line.close(piece)

        @pl.when(layer > 0)
        def _():
            below_copy(piece, group).wait_recv()

        def some(place, carry):
            inner = pl.ds(pl.multiple_of(place * chunk, chunk), chunk)
            value = shares[piece, group, inner, :]
            value = value + below_in[piece, group, inner, :].astype(jnp.float32)
            for way in (0, 1):
                value = value + sums_in[way, piece, group, inner, :].astype(jnp.float32)
            applied[piece, place] = value.astype(jnp.bfloat16)
            return carry

        lax.fori_loop(0, layers, some, 0)
        swap(0, piece)
        applied_in[piece, layer] = applied[piece, layer]

    def correct(piece):
        for step in range(layers - 1, 0, -1):
            swap_copy(0, piece, step).wait_recv()
        part = cut(piece)

        def wide(ref, place):
            return ref[place, :, part].astype(jnp.float32)

        passed = None
        for place in range(layers):
            target = wide(grads, place) - scales[place, :, 0:1] * wide(solved, place)
            if place < layers - 1:
                target = target - scales[place, :, 1:2] * wide(solved, place + 1)
            target = target - applied_in[piece, place].astype(jnp.float32)
            if place:
                target = target - scales[place - 1, :, 1:2] * wide(solved, place - 1)
                target = target - passed
            value = target / scales[place, :, 0:1]
            scaled[place] = value
            passed = scales[place, :, 1:2] * value
        result = value
        fixed[piece, layers - 1] = result.astype(jnp.bfloat16)
        for place in range(layers - 2, -1, -1):
            ratio = scales[place, :, 1:2] / scales[place, :, 0:1]
            result = scaled[place] - ratio * result
            fixed[piece, place] = result.astype(jnp.bfloat16)
        swap(1, piece)
        fixed_in[piece, layer] = fixed[piece, layer]

    stores = []

    def update(piece):
        for step in range(layers - 1, 0, -1):
            swap_copy(1, piece, step).wait_recv()
        part = cut(piece)

        def some(place, carry):
            inner = pl.ds(pl.multiple_of(place * chunk, chunk), chunk)
            change = initial[inner, part].astype(jnp.float32) + fixed_in[piece, place].astype(
                jnp.float32
            )
            moment = MOMENTUM * moments[inner, part].astype(jnp.float32) * powers[inner, 0:1]
            moment = moment + (1.0 - MOMENTUM) * change
            moments_new[inner, part] = (moment * powers[inner, 1:2]).astype(jnp.bfloat16)
            weights = master[inner, part] - STEP_SIZE * moment
            master_new[inner, part] = weights
            replicas[piece, inner, :] = weights.astype(jnp.bfloat16)
            return carry

        lax.fori_loop(0, layers, some, 0)
        last.begin([piece])
        for place, (source, target) in enumerate(
            (
                (replicas.at[piece], replicas_out.at[group, :, part]),
                (master_new.at[:, part], master_out.at[:, part]),
                (moments_new.at[:, part], moments_out.at[:, part]),
            )
        ):
            stores.append(pltpu.make_async_copy(source, target, store_sem.at[place, piece]))
            stores[-1].start()

    far = groups - 1
    lend(0)
    for load in loads[4:7]:
        load.wait()

    @pl.when(layer < layers - 1)
    def _():
        load_above.wait()

    @pl.when(group == 0)
    def _():
        sums_in[0] = jnp.zeros_like(sums_in[0])

    @pl.when(group == groups - 1)
    def _():
        sums_in[1] = jnp.zeros_like(sums_in[1])

    share(0)
    lend(1)
    lane = lax.broadcasted_iota(jnp.int32, (SCALE_BLOCK, 128), 1)
    for place in range(rows // SCALE_BLOCK):
        power = jnp.full((SCALE_BLOCK, 128), exponents[0, place].astype(jnp.float32))
        powers[place * SCALE_BLOCK : (place + 1) * SCALE_BLOCK, :] = jnp.exp2(
            jnp.where(lane == 0, power, -power)
        )
    for load in loads[7:]:
        load.wait()
    for piece in range(PIECES):
        for distance in range(far, 0, -1):
            line.step(piece, distance, add)
        if piece + 1 < PIECES:
            share(piece + 1)
        if piece + 2 < PIECES:
            lend(piece + 2)
        if piece:
            correct(piece - 1)
        join(piece)
        if piece:
            update(piece - 1)
        if piece > 1:
            for hop in range(1, far):
                last.arrive(hop, [piece - 2])
    correct(PIECES - 1)
    last.arrive(far, [0])
    for hop in range(1, far):
        last.arrive(hop, [PIECES - 2])
    update(PIECES - 1)
    for piece in range(1, PIECES - 1):
        last.arrive(far, [piece])
    for hop in range(1, groups):
        last.arrive(hop, [PIECES - 1])

    for piece in range(PIECES):
        for step in range(1, layers):
            for which in range(2):
                swap_copy(which, piece, step).wait_send()

        @pl.when(layer < layers - 1)
        def _():
            for place in range(groups):
                below_copy(piece, place).wait_send()

    line.finish(PIECES)
    last.finish()
    for store in stores:
        store.wait()


def back(exponents, matrices, initial, above, grads, solved, scales, own_scales, moments, master):
    layers, groups = lax.axis_size("layer"), lax.axis_size("dp")
    rows, columns = initial.shape
    features = matrices[0].shape[0]
    chunk, width = rows // layers, columns // PIECES
    half, full = jnp.bfloat16, jnp.float32
    dma = pltpu.SemaphoreType.DMA
    shape = jax.ShapeDtypeStruct
    swapped = pltpu.VMEM((PIECES, layers, chunk, width), half)
    return pl.pallas_call(
        back_kernel,
        out_shape=[
            shape((rows, columns), half),
            shape((rows, columns), full),
            shape((groups, rows, columns), half),
        ],
        in_specs=[pl.BlockSpec(memory_space=pltpu.SMEM)]
        + [pl.BlockSpec(memory_space=pl.ANY)] * 13,
        out_specs=[pl.BlockSpec(memory_space=pl.ANY)] * 3,
        scratch_shapes=[pltpu.VMEM((features, rows), half)] * 5
        + [
            pltpu.VMEM((rows, columns), half),
            pltpu.VMEM((rows, columns), half),
            pltpu.VMEM((layers, chunk, columns), half),
            pltpu.VMEM((layers, chunk, columns), half),
            pltpu.VMEM((layers, chunk, 128), full),
            pltpu.VMEM((rows, 128), full),
            pltpu.VMEM((rows, columns), half),
            pltpu.VMEM((rows, columns), full),
            pltpu.VMEM((rows, 128), full),
            pltpu.VMEM((PIECES, groups, rows, width), half),
            pltpu.VMEM((PIECES, groups, rows, width), half),
            pltpu.VMEM((PIECES, groups, rows, width), full),
            pltpu.VMEM((PIECES, groups, rows, width), half),
            pltpu.VMEM((2, PIECES, groups, rows, width), half),
        ]
        + [swapped] * 2
        + [pltpu.VMEM((layers, chunk, width), full)]
        + [swapped] * 2
        + [
            pltpu.VMEM((rows, columns), half),
            pltpu.VMEM((rows, columns), full),
            pltpu.VMEM((PIECES, rows, width), half),
        ]
        + [dma((2, groups - 1, PIECES))] * 2
        + [dma((PIECES, groups))] * 2
        + [dma((2, PIECES, groups))] * 2
        + [dma((layers - 1, PIECES))] * 4
        + [dma((13,)), dma((3, PIECES))],
        compiler_params=pltpu.CompilerParams(
            collective_id=1, has_side_effects=True, vmem_limit_bytes=63 << 20
        ),
        cost_estimate=pl.CostEstimate(
            flops=10 * features * rows * columns, bytes_accessed=300_000_000, transcendentals=0
        ),
        name="back",
    )(exponents, *matrices, initial, above, grads, solved, scales, own_scales, moments, master)


def body(activations, factor_old, cross_old, gradients, moments, exponents, master):
    layers, groups = lax.axis_size("layer"), lax.axis_size("dp")
    row_count, features = factor_old.shape[1:]
    columns = gradients.shape[2]
    chunk = row_count // layers
    fresh_weight = (1.0 - FACTOR_DECAY) / (activations.shape[1] * groups)
    factor_new, cross_new, *rest = front(
        fresh_weight,
        activations[0],
        gradients[0].reshape(layers, chunk, columns),
        factor_old[0],
        cross_old[0],
    )
    *matrices, initial, above, grad_swapped, initial_swapped, scales, own_scales = rest
    moments_new, master_new, replicas = back(
        exponents,
        matrices,
        initial.reshape(row_count, columns),
        above.reshape(row_count, columns),
        grad_swapped,
        initial_swapped,
        scales,
        own_scales,
        moments[0],
        master[0],
    )
    replicas = replicas.reshape(features, columns)
    return (factor_new[None], cross_new[None], moments_new[None], master_new[None], replicas[None])


def solution(mesh):
    return jax.shard_map(
        body,
        mesh=mesh,
        in_specs=(
            P("layer", "dp", None),
            P("layer", "dp", None),
            P("layer", "dp", None),
            P("layer", "dp", None),
            P("layer", "dp", None),
            P("layer", "dp"),
            P("layer", "dp", None),
        ),
        out_specs=(
            P("layer", "dp", None),
            P("layer", "dp", None),
            P("layer", "dp", None),
            P("layer", "dp", None),
            P("layer", None, None),
        ),
        check_vma=False,
    )
```

```python
import functools

import jax
import jax.numpy as jnp
from jax import lax
from jax.experimental import pallas as pl
from jax.experimental.pallas import tpu as pltpu
from jax.sharding import PartitionSpec as P

SCALE_BLOCK = 128


FACTOR_DECAY = 0.9
DAMPING = 0.5
MOMENTUM = 0.8
STEP_SIZE = 0.05

MESH = pl.DeviceIdType.MESH


def product(left, right):
    return jnp.dot(left, right, preferred_element_type=jnp.float32)


CHUNKS = 4


def column_of(row, eye):
    return jnp.sum(jnp.where(eye, jnp.broadcast_to(row, eye.shape), 0.0), axis=1, keepdims=True)


def identity(size):
    return lax.broadcasted_iota(jnp.int32, (size, size), 0) == lax.broadcasted_iota(
        jnp.int32, (size, size), 1
    )


def greet():
    barrier = pltpu.get_barrier_semaphore()
    total = 0
    for axis in ("layer", "dp"):
        count, mine = lax.axis_size(axis), lax.axis_index(axis)
        for step in range(1, count):
            pl.semaphore_signal(
                barrier, inc=1, device_id={axis: lax.rem(mine + step, count)}, device_id_type=MESH
            )
        total += count - 1
    pl.semaphore_wait(barrier, total)


def remote(source, target, send_sem, recv_sem, axis, step):
    count, mine = lax.axis_size(axis), lax.axis_index(axis)
    return pltpu.make_async_remote_copy(
        src_ref=source,
        dst_ref=target,
        send_sem=send_sem,
        recv_sem=recv_sem,
        device_id={axis: lax.rem(mine + step + count, count)},
        device_id_type=MESH,
    )


class Line:
    def __init__(self, axis, source, target, send_sem, recv_sem, pieces):
        self.axis, self.count, self.mine = axis, lax.axis_size(axis), lax.axis_index(axis)
        self.source, self.target, self.pieces = source, target, pieces
        self.send_sem, self.recv_sem = send_sem, recv_sem

    def copy(self, way, hop, piece):
        sign = 1 if way == 0 else -1
        block = jnp.clip(self.mine - sign * hop, 0, self.count - 1)
        landing = self.target(block, piece)
        return remote(
            self.source(piece) if hop == 0 else landing,
            landing,
            self.send_sem.at[way, hop, piece],
            self.recv_sem.at[way, hop, piece],
            self.axis,
            sign,
        )

    def has_next(self, way):
        return self.mine < self.count - 1 if way == 0 else self.mine > 0

    def has_block(self, way, hop):
        return self.mine >= hop if way == 0 else self.mine + hop <= self.count - 1

    def begin(self, pieces):
        for piece in pieces:
            for way in (0, 1):

                @pl.when(self.has_next(way))
                def _():
                    self.copy(way, 0, piece).start()

    def arrive(self, hop, pieces, then=None):
        for piece in pieces:
            for way in (0, 1):

                @pl.when(self.has_block(way, hop))
                def _():
                    self.copy(way, hop - 1, piece).wait_recv()
                    if hop < self.count - 1:

                        @pl.when(self.has_next(way))
                        def _():
                            self.copy(way, hop, piece).start()

                    if then is not None:
                        sign = 1 if way == 0 else -1
                        then(jnp.clip(self.mine - sign * hop, 0, self.count - 1), piece)

    def finish(self, pieces=None):
        for hop in range(self.count - 1):
            for piece in pieces or range(self.pieces):
                for way in (0, 1):

                    @pl.when(self.has_next(way) & self.has_block(way, hop))
                    def _():
                        self.copy(way, hop, piece).wait_send()


def front_kernel(
    fresh_weight,
    acts, grads, factor_old, cross_old,
    factor_out, cross_out, factor_high_out, factor_low_out, cross_high_out, cross_low_out, lent_out,
    initial_out, full_out, upper_out, grads_out, solved_out, scales_out, own_scales_out,
    tokens, upper, factor, cross, grads_in, solved, scaled,
    sums_away, sums_in, own_scales, scales, own_turned,
    factor_high, factor_low, cross_high, cross_low, lent,
    line_send, line_recv, lift_send, lift_recv, grad_send, grad_recv, sum_send, sum_recv,
    scale_send, scale_recv, start_send, start_recv, first_send, first_recv, rise_send, rise_recv, local_sem,
):
    layers, groups = lax.axis_size("layer"), lax.axis_size("dp")
    layer, group = lax.axis_index("layer"), lax.axis_index("dp")
    rows, features = factor.shape
    count = acts.shape[0]
    part = count // CHUNKS
    chunk = rows // layers
    columns = grads.shape[2]
    own = pl.ds(pl.multiple_of(group * rows, rows), rows)

    def span(piece):
        return pl.ds(piece * part, part)

    load_acts = pltpu.make_async_copy(acts, tokens.at[group], local_sem.at[0])
    load_factor = pltpu.make_async_copy(factor_old, factor, local_sem.at[1])
    load_cross = pltpu.make_async_copy(cross_old, cross, local_sem.at[2])
    load_grads = pltpu.make_async_copy(grads.at[layer], grads_in.at[layer], local_sem.at[3])
    load_acts.start()
    load_cross.start()
    load_factor.start()
    load_grads.start()
    greet()

    line = Line(
        "dp",
        lambda piece: acts.at[span(piece)],
        lambda block, piece: tokens.at[block, span(piece)],
        line_send,
        line_recv,
        CHUNKS,
    )

    def lift_copy(source, block, piece):
        return remote(
            source,
            upper.at[block, span(piece)],
            lift_send.at[block, piece],
            lift_recv.at[block, piece],
            "layer",
            -1,
        )

    def lift(block, piece):
        @pl.when(layer > 0)
        def _():
            lift_copy(tokens.at[block, span(piece)], block, piece).start()

    @pl.when(layer > 0)
    def _():
        for piece in range(CHUNKS):
            lift_copy(acts.at[span(piece)], group, piece).start()

    def grad_copy(step):
        peer = lax.rem(layer + step, layers)
        return remote(
            grads.at[peer], grads_in.at[layer], grad_send.at[step - 1], grad_recv.at[step - 1],
            "layer", step,
        )

    for step in range(layers - 1, 0, -1):
        grad_copy(step).start()
    line.begin(range(CHUNKS // 2))

    load_acts.wait()
    sums_away[...] = jnp.zeros_like(sums_away)
    for place in range(groups):
        wide = tokens[group, :, place * rows : (place + 1) * rows].astype(jnp.float32)
        sums_away[place, 0:1, :] = jnp.sum(wide * wide, axis=0, keepdims=True)
    load_cross.wait()
    load_factor.wait()
    eye = identity(rows)
    factor_diagonal = jnp.sum(jnp.where(eye, factor[:, own], 0.0), axis=1, keepdims=True)
    cross_diagonal = jnp.sum(jnp.where(eye, cross[:, own], 0.0), axis=1, keepdims=True)

    @pl.when(layer < layers - 1)
    def _():
        for piece in range(CHUNKS):
            lift_copy(acts.at[span(piece)], group, piece).wait_recv()
        for place in range(groups):
            cut = slice(place * rows, (place + 1) * rows)
            wide = tokens[group, :, cut].astype(jnp.float32)
            above = upper[group, :, cut].astype(jnp.float32)
            sums_away[place, 1:2, :] = jnp.sum(wide * above, axis=0, keepdims=True)

    @pl.when(layer == layers - 1)
    def _():
        upper[...] = jnp.zeros_like(upper)

    def sum_copy(step):
        peer = lax.rem(group + step, groups)
        return remote(
            sums_away.at[peer], sums_in.at[group], sum_send.at[step - 1], sum_recv.at[step - 1],
            "dp", step,
        )

    for step in range(groups - 1, 0, -1):
        sum_copy(step).start()
    line.begin(range(CHUNKS // 2, CHUNKS))
    sums_in[group] = sums_away[group]
    line.arrive(1, range(CHUNKS // 2))

    for step in range(groups - 1, 0, -1):
        sum_copy(step).wait_recv()
    sums = fresh_weight * jnp.sum(sums_in[...], axis=0)
    own_sum = column_of(sums[0:1], eye)
    next_sum = column_of(sums[1:2], eye)
    own_diagonal = FACTOR_DECAY * factor_diagonal + own_sum
    own_coupling = FACTOR_DECAY * cross_diagonal + next_sum
    lane = lax.broadcasted_iota(jnp.int32, (rows, 128), 1)
    own_scales[...] = jnp.where(
        lane == 0,
        DAMPING + own_diagonal,
        jnp.where(lane == 1, own_coupling, jnp.where(lane == 2, own_diagonal, next_sum)),
    )

    def scale_copy(step):
        peer = lax.rem(layer + step, layers)
        return remote(
            own_scales.at[pl.ds(pl.multiple_of(peer * chunk, chunk), chunk)],
            scales.at[layer], scale_send.at[step - 1], scale_recv.at[step - 1], "layer", step,
        )

    for step in range(layers - 1, 0, -1):
        scale_copy(step).start()
    scales[layer] = own_scales[pl.ds(pl.multiple_of(layer * chunk, chunk), chunk), :]
    line.arrive(1, range(CHUNKS // 2, CHUNKS))
    for way in (0, 1):

        @pl.when(line.has_block(way, 1))
        def _():
            for piece in range(CHUNKS):
                lift(jnp.clip(group - (1 if way == 0 else -1), 0, groups - 1), piece)

    load_grads.wait()
    for step in range(layers - 1, 0, -1):
        scale_copy(step).wait_recv()
        grad_copy(step).wait_recv()

    width = scaled.shape[2]

    def solve(tile, carry):
        cut = pl.ds(pl.multiple_of(tile * width, width), width)
        passed = None
        for place in range(layers):
            target = grads_in[place, :, cut].astype(jnp.float32)
            if place:
                target = target - passed
            value = target / scales[place, :, 0:1]
            scaled[place] = value
            passed = scales[place, :, 1:2] * value
        result = value
        solved[layers - 1, :, cut] = result.astype(jnp.bfloat16)
        for place in range(layers - 2, -1, -1):
            ratio = scales[place, :, 1:2] / scales[place, :, 0:1]
            result = scaled[place] - ratio * result
            solved[place, :, cut] = result.astype(jnp.bfloat16)
        return carry

    lax.fori_loop(0, columns // width, solve, 0)

    def start_copy(step):
        peer = lax.rem(layer + step, layers)
        return remote(
            solved.at[peer], initial_out.at[layer], start_send.at[step - 1],
            start_recv.at[step - 1], "layer", step,
        )

    for step in range(layers - 1, 0, -1):
        start_copy(step).start()
    stores = [
        pltpu.make_async_copy(solved.at[layer], initial_out.at[layer], local_sem.at[0]),
        pltpu.make_async_copy(grads_in, grads_out, local_sem.at[1]),
        pltpu.make_async_copy(solved, solved_out, local_sem.at[2]),
        pltpu.make_async_copy(scales, scales_out, local_sem.at[3]),
        pltpu.make_async_copy(own_scales, own_scales_out, local_sem.at[4]),
    ]
    for store in stores:
        store.start()

    for hop in range(2, groups - 1):
        line.arrive(hop, range(CHUNKS), lift)

    line.arrive(groups - 1, [0], lift)
    for step in range(1, layers):
        start_copy(step).wait_recv()
    stores[0].wait()

    piece_width = columns // PIECES
    begun = initial_out.at[:, :, 0:piece_width]
    first = Line(
        "dp",
        lambda piece: begun,
        lambda block, piece: full_out.at[block],
        first_send,
        first_recv,
        1,
    )

    def rise_copy(source, block):
        return remote(
            source, upper_out.at[block], rise_send.at[block], rise_recv.at[block], "layer", -1
        )

    def rise(block, piece):
        @pl.when(layer > 0)
        def _():
            rise_copy(full_out.at[block], block).start()

    first.begin([0])

    @pl.when(layer > 0)
    def _():
        rise_copy(begun, group).start()

    line.arrive(groups - 1, range(1, CHUNKS), lift)

    tile = 256
    every = count * groups

    def gather(ref, cut):
        return ref[:, :, cut].reshape(every, cut.size)

    own_turned[...] = gather(tokens, own).astype(jnp.float32).T.astype(jnp.bfloat16)

    def refresh_factor(place, carry):
        cut = pl.ds(pl.multiple_of(place * tile, tile), tile)
        value = product(own_turned[...], gather(tokens, cut))
        value = FACTOR_DECAY * factor[:, cut] + fresh_weight * value
        factor[:, cut] = value
        high = value.astype(jnp.bfloat16)
        factor_high[:, cut] = high
        factor_low[:, cut] = (value - high.astype(jnp.float32)).astype(jnp.bfloat16)
        return carry

    tiles = features // tile
    lax.fori_loop(0, tiles // 2, refresh_factor, 0)
    first.arrive(1, [0], rise)
    lax.fori_loop(tiles // 2, tiles, refresh_factor, 0)
    for hop in range(2, groups - 1):
        first.arrive(hop, [0], rise)
    more = [
        pltpu.make_async_copy(factor, factor_out, local_sem.at[10]),
        pltpu.make_async_copy(factor_high, factor_high_out, local_sem.at[5]),
        pltpu.make_async_copy(factor_low, factor_low_out, local_sem.at[6]),
    ]
    for store in more:
        store.start()
    stores += more

    @pl.when(layer < layers - 1)
    def _():
        for step in range(1, groups):
            block = lax.rem(group + step, groups)
            for piece in range(CHUNKS):
                lift_copy(acts.at[span(piece)], block, piece).wait_recv()

    def refresh_cross(place, carry):
        cut = pl.ds(pl.multiple_of(place * tile, tile), tile)
        value = product(own_turned[...], gather(upper, cut))
        value = FACTOR_DECAY * cross[:, cut] + fresh_weight * value
        cross[:, cut] = value
        high = value.astype(jnp.bfloat16)
        cross_high[:, cut] = high
        cross_low[:, cut] = (value - high.astype(jnp.float32)).astype(jnp.bfloat16)
        lent[cut, :] = value.T.astype(jnp.bfloat16)
        return carry

    lax.fori_loop(0, tiles, refresh_cross, 0)
    more = [
        pltpu.make_async_copy(cross, cross_out, local_sem.at[11]),
        pltpu.make_async_copy(cross_high, cross_high_out, local_sem.at[7]),
        pltpu.make_async_copy(cross_low, cross_low_out, local_sem.at[8]),
    ]
    for store in more:
        store.start()
    stores += more

    lent[own, :] = jnp.where(eye, 0.0, lent[own, :].astype(jnp.float32)).astype(jnp.bfloat16)
    last = pltpu.make_async_copy(lent, lent_out, local_sem.at[9])
    last.start()
    stores.append(last)

    first.arrive(groups - 1, [0], rise)

    @pl.when(layer < layers - 1)
    def _():
        for block in range(groups):
            rise_copy(begun, block).wait_recv()

    @pl.when(layer > 0)
    def _():
        for block in range(groups):
            rise_copy(begun, block).wait_send()

    for step in range(1, layers):
        start_copy(step).wait_send()
        grad_copy(step).wait_send()
        scale_copy(step).wait_send()
    for step in range(1, groups):
        sum_copy(step).wait_send()

    @pl.when(layer > 0)
    def _():
        for block in range(groups):
            for piece in range(CHUNKS):
                lift_copy(acts.at[span(piece)], block, piece).wait_send()

    line.finish()
    first.finish()
    for store in stores[1:]:
        store.wait()


def front(fresh_weight, acts, grads, factor_old, cross_old):
    layers, groups = lax.axis_size("layer"), lax.axis_size("dp")
    rows, features = factor_old.shape
    count = acts.shape[0]
    chunk, columns = grads.shape[1:]
    every = count * groups
    half, full = jnp.bfloat16, jnp.float32
    dma = pltpu.SemaphoreType.DMA
    shape = jax.ShapeDtypeStruct
    return pl.pallas_call(
        functools.partial(front_kernel, fresh_weight),
        out_shape=[shape((rows, features), full)] * 2
        + [shape((rows, features), half)] * 4
        + [shape((features, rows), half)]
        + [shape((layers, chunk, columns), half)]
        + [shape((groups, layers, chunk, columns // PIECES), half)] * 2
        + [shape((layers, chunk, columns), half)] * 2
        + [shape((layers, chunk, 128), full), shape((rows, 128), full)],
        in_specs=[pl.BlockSpec(memory_space=pl.ANY)] * 4,
        out_specs=[pl.BlockSpec(memory_space=pl.ANY)] * 14,
        scratch_shapes=[
            pltpu.VMEM((groups, count, features), half),
            pltpu.VMEM((groups, count, features), half),
            pltpu.VMEM((rows, features), full),
            pltpu.VMEM((rows, features), full),
            pltpu.VMEM((layers, chunk, columns), half),
            pltpu.VMEM((layers, chunk, columns), half),
            pltpu.VMEM((layers, chunk, 256), full),
            pltpu.VMEM((groups, 8, rows), full),
            pltpu.VMEM((groups, 8, rows), full),
            pltpu.VMEM((rows, 128), full),
            pltpu.VMEM((layers, chunk, 128), full),
            pltpu.VMEM((rows, every), half),
        ]
        + [pltpu.VMEM((rows, features), half)] * 4
        + [pltpu.VMEM((features, rows), half)]
        + [dma((2, groups - 1, CHUNKS))] * 2
        + [dma((groups, CHUNKS))] * 2
        + [dma((layers - 1,))] * 2
        + [dma((groups - 1,))] * 2
        + [dma((layers - 1,))] * 4
        + [dma((2, groups - 1, 1))] * 2
        + [dma((groups,))] * 2
        + [dma((12,))],
        compiler_params=pltpu.CompilerParams(
            collective_id=0, has_side_effects=True, vmem_limit_bytes=63 << 20
        ),
        cost_estimate=pl.CostEstimate(
            flops=6 * every * rows * features, bytes_accessed=200_000_000, transcendentals=0
        ),
        name="front",
    )(acts, grads, factor_old, cross_old)


PIECES = 4
ORDER = (
    "begin 3", "multiply 0", "lend 0", "meet 1", "begin 2", "away 0",
    "meet 3", "lend 1", "near 0", "carry 3", "lend 2", "meet 2",
    "join 0", "carry 1", "away 1", "end 1", "correct 0", "near 1",
    "carry 2", "away 2", "update 0", "join 1", "lend 3", "end 3",
    "multiply 1", "end 2", "multiply 2", "near 2", "correct 1", "multiply 3",
    "first 0", "update 1", "join 2", "middle 0", "away 3", "correct 2",
    "final 0", "update 2", "near 3", "first 1", "join 3", "first 2",
    "correct 3", "middle 1", "update 3", "final 1", "first 3", "final 2 3",
    "middle 2 3",
)


class Sums:
    def __init__(self, axis, source, target, send_sem, recv_sem):
        self.axis, self.count, self.mine = axis, lax.axis_size(axis), lax.axis_index(axis)
        self.source, self.target = source, target
        self.send_sem, self.recv_sem = send_sem, recv_sem

    def copy(self, way, piece, owner):
        return remote(
            self.source(piece, owner),
            self.target(way, piece, owner),
            self.send_sem.at[way, piece, owner],
            self.recv_sem.at[way, piece, owner],
            self.axis,
            1 if way == 0 else -1,
        )

    def has_before(self, way):
        return self.mine > 0 if way == 0 else self.mine < self.count - 1

    def begin(self, piece, add):
        for way in (0, 1):

            @pl.when(jnp.logical_not(self.has_before(way)))
            def _():
                for distance in range(self.count - 1, 0, -1):
                    place = distance if way == 0 else self.count - 1 - distance
                    add(way, piece, place, False)
                    self.copy(way, piece, place).start()

    def step(self, piece, distance, add):
        for way in (0, 1):
            owner = self.mine + (distance if way == 0 else -distance)

            @pl.when((owner >= 0) & (owner < self.count) & self.has_before(way))
            def _():
                place = jnp.clip(owner, 0, self.count - 1)
                self.copy(way, piece, place).wait_recv()
                add(way, piece, place, True)
                self.copy(way, piece, place).start()

    def close(self, piece):
        for way in (0, 1):

            @pl.when(self.has_before(way))
            def _():
                self.copy(way, piece, self.mine).wait_recv()

    def finish(self, pieces):
        for piece in range(pieces):
            for distance in range(1, self.count):
                for way in (0, 1):
                    owner = self.mine + (distance if way == 0 else -distance)

                    @pl.when((owner >= 0) & (owner < self.count))
                    def _():
                        self.copy(way, piece, jnp.clip(owner, 0, self.count - 1)).wait_send()


def back_kernel(
    exponents,
    factor_high_in, factor_low_in, cross_high_in, cross_low_in, lent_in,
    initial_in, full_in, upper_in, grads_in, solved_in, scales_in, own_scales_in, moments_in, master_in,
    moments_out, master_out, replicas_out,
    factor_high, factor_low, cross_high, cross_low, lent,
    initial, grads, solved, scales, own_scales, moments, powers, master,
    full, upper, sums, sums_in, away, lowered, away_in, lowered_in, scaled, fixed, fixed_in,
    moments_new, master_new, replicas,
    first_send, first_recv, sum_send, sum_recv, last_send, last_recv, lift_send, lift_recv,
    away_send, away_recv, lowered_send, lowered_recv, fixed_send, fixed_recv, load_sem, store_sem,
):
    layers, groups = lax.axis_size("layer"), lax.axis_size("dp")
    layer, group = lax.axis_index("layer"), lax.axis_index("dp")
    rows, columns = initial.shape
    chunk = rows // layers
    width = columns // PIECES
    features = rows * groups

    def cut(piece):
        return slice(piece * width, (piece + 1) * width)

    pairs = (
        (initial_in, initial),
        (factor_high_in, factor_high),
        (factor_low_in, factor_low),
        (cross_high_in, cross_high),
        (cross_low_in, cross_low),
        (lent_in, lent),
        (own_scales_in, own_scales),
        (grads_in, grads),
        (solved_in, solved),
        (scales_in, scales),
        (moments_in, moments),
        (master_in, master),
    )
    loads = [
        pltpu.make_async_copy(source, target, load_sem.at[place])
        for place, (source, target) in enumerate(pairs)
    ]
    for load in loads:
        load.start()
    greet()

    first = Line(
        "dp",
        lambda piece: initial_in.at[:, cut(piece)],
        lambda block, piece: full.at[piece, block],
        first_send,
        first_recv,
        PIECES,
    )
    last = Line(
        "dp",
        lambda piece: replicas.at[piece],
        lambda block, piece: replicas_out.at[block, :, cut(piece)],
        last_send,
        last_recv,
        PIECES,
    )

    def lift_copy(source, block, piece):
        return remote(
            source, upper.at[piece, block], lift_send.at[piece, block], lift_recv.at[piece, block],
            "layer", -1,
        )

    def lift(block, piece):
        @pl.when(layer > 0)
        def _():
            lift_copy(full.at[piece, block], block, piece).start()

    def begin(piece):
        first.begin([piece])

        @pl.when(layer > 0)
        def _():
            lift_copy(initial_in.at[:, cut(piece)], group, piece).start()

    begin(1)
    ready = [
        pltpu.make_async_copy(
            full_in.at[lax.rem(group + step, groups)],
            full.at[0, lax.rem(group + step, groups)],
            load_sem.at[len(pairs) + step],
        )
        for step in range(1, groups)
    ]
    ready_upper = pltpu.make_async_copy(upper_in, upper.at[0], load_sem.at[len(pairs)])
    for load in ready:
        load.start()

    @pl.when(layer < layers - 1)
    def _():
        ready_upper.start()

    @pl.when(layer == layers - 1)
    def _():
        upper[...] = jnp.zeros_like(upper)

    loads[0].wait()
    for piece in range(PIECES):
        full[piece, group] = initial[:, cut(piece)]

    def relay_copy(which, piece, step):
        source, target, send_sem, recv_sem = (
            (away, away_in, away_send, away_recv),
            (lowered, lowered_in, lowered_send, lowered_recv),
            (fixed, fixed_in, fixed_send, fixed_recv),
        )[which]
        peer = lax.rem(layer + step, layers)
        return remote(
            source.at[piece, peer], target.at[piece, layer],
            send_sem.at[step - 1, piece], recv_sem.at[step - 1, piece], "layer", step,
        )

    def multiply(piece):
        @pl.when(layer < layers - 1)
        def _():
            if piece == 0:
                ready_upper.wait()
            else:
                for block in range(groups):
                    lift_copy(full.at[piece, block], block, piece).wait_recv()

        def some(place, carry):
            part = pl.ds(pl.multiple_of(place * chunk * 2, chunk * 2), chunk * 2)
            mine = full[piece].reshape(features, width)
            theirs = upper[piece].reshape(features, width)
            value = product(factor_high[part, :], mine) + product(factor_low[part, :], mine)
            value = value - own_scales[part, 2:3] * full[piece, group, part, :].astype(jnp.float32)
            value = value + product(cross_high[part, :], theirs) + product(cross_low[part, :], theirs)
            value = value - own_scales[part, 1:2] * upper[piece, group, part, :].astype(jnp.float32)
            for side in range(2):
                inner = slice(side * chunk, (side + 1) * chunk)
                away[piece, 2 * place + side] = value[inner].astype(jnp.bfloat16)
            return carry

        lax.fori_loop(0, layers // 2, some, 0)
        for step in range(layers - 1, 0, -1):
            relay_copy(0, piece, step).start()
        away_in[piece, layer] = away[piece, layer]

    def block_of(place):
        return pl.ds(pl.multiple_of(place * rows, rows), rows)

    def add(way, piece, place, more):
        value = product(lent[block_of(place), :], initial[:, cut(piece)])
        if more:
            value = value + sums_in[way, piece, place].astype(jnp.float32)
        sums[piece, place] = value.astype(jnp.bfloat16)

    lower = Sums(
        "dp",
        lambda piece, owner: sums.at[piece, owner],
        lambda way, piece, owner: sums_in.at[way, piece, owner],
        sum_send,
        sum_recv,
    )

    def join(piece):
        lower.close(piece)
        value = product(lent[block_of(group), :], initial[:, cut(piece)])
        for way in (0, 1):
            value = value + sums_in[way, piece, group].astype(jnp.float32)
        for place in range(layers):
            part = value[place * chunk : (place + 1) * chunk]
            lowered[piece, place] = part.astype(jnp.bfloat16)
        for step in range(layers - 1, 0, -1):
            relay_copy(1, piece, step).start()
        lowered_in[piece, layer] = lowered[piece, layer]

    def correct(piece):
        for step in range(layers - 1, 0, -1):
            relay_copy(0, piece, step).wait_recv()
            relay_copy(1, piece, step).wait_recv()
        part = cut(piece)

        def wide(ref, place):
            return ref[place, :, part].astype(jnp.float32)

        passed = None
        for place in range(layers):
            target = wide(grads, place) - scales[place, :, 0:1] * wide(solved, place)
            if place < layers - 1:
                target = target - scales[place, :, 1:2] * wide(solved, place + 1)
            target = target - away_in[piece, place].astype(jnp.float32)
            if place:
                target = target - scales[place - 1, :, 1:2] * wide(solved, place - 1)
                target = target - lowered_in[piece, place - 1].astype(jnp.float32)
                target = target - passed
            value = target / scales[place, :, 0:1]
            scaled[place] = value
            passed = scales[place, :, 1:2] * value
        result = value
        fixed[piece, layers - 1] = result.astype(jnp.bfloat16)
        for place in range(layers - 2, -1, -1):
            ratio = scales[place, :, 1:2] / scales[place, :, 0:1]
            result = scaled[place] - ratio * result
            fixed[piece, place] = result.astype(jnp.bfloat16)
        for step in range(layers - 1, 0, -1):
            relay_copy(2, piece, step).start()
        fixed_in[piece, layer] = fixed[piece, layer]

    stores = []

    def update(piece):
        for step in range(layers - 1, 0, -1):
            relay_copy(2, piece, step).wait_recv()
        part = cut(piece)

        def some(place, carry):
            inner = pl.ds(pl.multiple_of(place * chunk, chunk), chunk)
            change = initial[inner, part].astype(jnp.float32) + fixed_in[piece, place].astype(
                jnp.float32
            )
            moment = MOMENTUM * moments[inner, part].astype(jnp.float32) * powers[inner, 0:1]
            moment = moment + (1.0 - MOMENTUM) * change
            moments_new[inner, part] = (moment * powers[inner, 1:2]).astype(jnp.bfloat16)
            weights = master[inner, part] - STEP_SIZE * moment
            master_new[inner, part] = weights
            replicas[piece, inner, :] = weights.astype(jnp.bfloat16)
            return carry

        lax.fori_loop(0, layers, some, 0)
        last.begin([piece])
        for place, (source, target) in enumerate(
            (
                (replicas.at[piece], replicas_out.at[group, :, part]),
                (master_new.at[:, part], master_out.at[:, part]),
                (moments_new.at[:, part], moments_out.at[:, part]),
            )
        ):
            stores.append(pltpu.make_async_copy(source, target, store_sem.at[place, piece]))
            stores[-1].start()

    far = groups - 1
    lane = lax.broadcasted_iota(jnp.int32, (SCALE_BLOCK, 128), 1)
    for place in range(rows // SCALE_BLOCK):
        power = jnp.full((SCALE_BLOCK, 128), exponents[0, place].astype(jnp.float32))
        powers[place * SCALE_BLOCK : (place + 1) * SCALE_BLOCK, :] = jnp.exp2(
            jnp.where(lane == 0, power, -power)
        )
    for way, end in ((0, 0), (1, groups - 1)):

        @pl.when(group == end)
        def _():
            for piece in range(PIECES):
                sums_in[way, piece, end] = jnp.zeros_like(sums_in[way, piece, end])

    for load in loads[1:] + ready:
        load.wait()
    tasks = dict(
        begin=begin,
        meet=lambda piece: first.arrive(1, [piece], lift),
        carry=lambda piece: [first.arrive(hop, [piece], lift) for hop in range(2, far)],
        end=lambda piece: first.arrive(far, [piece], lift),
        lend=lambda piece: lower.begin(piece, add),
        away=lambda piece: [lower.step(piece, distance, add) for distance in range(far - 1, 1, -1)],
        near=lambda piece: lower.step(piece, 1, add),
        multiply=multiply,
        join=join,
        correct=correct,
        update=update,
        first=lambda piece: last.arrive(1, [piece]),
        middle=lambda piece: [last.arrive(hop, [piece]) for hop in range(2, far)],
        final=lambda piece: last.arrive(far, [piece]),
    )
    for entry in ORDER:
        name, *pieces = entry.split()
        for piece in pieces:
            tasks[name](int(piece))

    for piece in range(PIECES):
        for step in range(1, layers):
            for which in range(3):
                relay_copy(which, piece, step).wait_send()

        if piece:

            @pl.when(layer > 0)
            def _():
                for block in range(groups):
                    lift_copy(full.at[piece, block], block, piece).wait_send()

    first.finish(range(1, PIECES))
    lower.finish(PIECES)
    last.finish()
    for store in stores:
        store.wait()


def back(exponents, matrices, initial, full_first, upper_first, grads, solved, scales, own_scales, moments, master):
    layers, groups = lax.axis_size("layer"), lax.axis_size("dp")
    rows, columns = initial.shape
    features = matrices[0].shape[1]
    chunk, width = rows // layers, columns // PIECES
    half, full = jnp.bfloat16, jnp.float32
    dma = pltpu.SemaphoreType.DMA
    shape = jax.ShapeDtypeStruct
    swapped = pltpu.VMEM((PIECES, layers, chunk, width), half)
    return pl.pallas_call(
        back_kernel,
        out_shape=[
            shape((rows, columns), half),
            shape((rows, columns), full),
            shape((groups, rows, columns), half),
        ],
        in_specs=[pl.BlockSpec(memory_space=pltpu.SMEM)]
        + [pl.BlockSpec(memory_space=pl.ANY)] * 14,
        out_specs=[pl.BlockSpec(memory_space=pl.ANY)] * 3,
        scratch_shapes=[pltpu.VMEM((rows, features), half)] * 4
        + [pltpu.VMEM((features, rows), half)]
        + [
            pltpu.VMEM((rows, columns), half),
            pltpu.VMEM((layers, chunk, columns), half),
            pltpu.VMEM((layers, chunk, columns), half),
            pltpu.VMEM((layers, chunk, 128), full),
            pltpu.VMEM((rows, 128), full),
            pltpu.VMEM((rows, columns), half),
            pltpu.VMEM((rows, 128), full),
            pltpu.VMEM((rows, columns), full),
            pltpu.VMEM((PIECES, groups, rows, width), half),
            pltpu.VMEM((PIECES, groups, rows, width), half),
            pltpu.VMEM((PIECES, groups, rows, width), half),
            pltpu.VMEM((2, PIECES, groups, rows, width), half),
        ]
        + [swapped] * 4
        + [pltpu.VMEM((layers, chunk, width), full)]
        + [swapped] * 2
        + [
            pltpu.VMEM((rows, columns), half),
            pltpu.VMEM((rows, columns), full),
            pltpu.VMEM((PIECES, rows, width), half),
        ]
        + [dma((2, groups - 1, PIECES))] * 2
        + [dma((2, PIECES, groups))] * 2
        + [dma((2, groups - 1, PIECES))] * 2
        + [dma((PIECES, groups))] * 2
        + [dma((layers - 1, PIECES))] * 6
        + [dma((12 + groups,)), dma((3, PIECES))],
        compiler_params=pltpu.CompilerParams(
            collective_id=1, has_side_effects=True, vmem_limit_bytes=63 << 20
        ),
        cost_estimate=pl.CostEstimate(
            flops=10 * features * rows * columns, bytes_accessed=300_000_000, transcendentals=0
        ),
        name="back",
    )(
        exponents, *matrices, initial, full_first, upper_first, grads, solved, scales, own_scales,
        moments, master,
    )


def body(activations, factor_old, cross_old, gradients, moments, exponents, master):
    layers, groups = lax.axis_size("layer"), lax.axis_size("dp")
    row_count, features = factor_old.shape[1:]
    columns = gradients.shape[2]
    chunk = row_count // layers
    fresh_weight = (1.0 - FACTOR_DECAY) / (activations.shape[1] * groups)
    factor_new, cross_new, *rest = front(
        fresh_weight,
        activations[0],
        gradients[0].reshape(layers, chunk, columns),
        factor_old[0],
        cross_old[0],
    )
    *matrices, initial, full_first, upper_first, grad_swapped, initial_swapped, scales, own_scales = rest
    moments_new, master_new, replicas = back(
        exponents,
        matrices,
        initial.reshape(row_count, columns),
        full_first.reshape(groups, row_count, -1),
        upper_first.reshape(groups, row_count, -1),
        grad_swapped,
        initial_swapped,
        scales,
        own_scales,
        moments[0],
        master[0],
    )
    replicas = replicas.reshape(features, columns)
    return (factor_new[None], cross_new[None], moments_new[None], master_new[None], replicas[None])


def solution(mesh):
    return jax.shard_map(
        body,
        mesh=mesh,
        in_specs=(
            P("layer", "dp", None),
            P("layer", "dp", None),
            P("layer", "dp", None),
            P("layer", "dp", None),
            P("layer", "dp", None),
            P("layer", "dp"),
            P("layer", "dp", None),
        ),
        out_specs=(
            P("layer", "dp", None),
            P("layer", "dp", None),
            P("layer", "dp", None),
            P("layer", "dp", None),
            P("layer", None, None),
        ),
        check_vma=False,
    )
```

```python
import functools

import jax
import jax.numpy as jnp
from jax import lax
from jax.experimental import pallas as pl
from jax.experimental.pallas import tpu as pltpu
from jax.sharding import PartitionSpec as P

SCALE_BLOCK = 128


FACTOR_DECAY = 0.9
DAMPING = 0.5
MOMENTUM = 0.8
STEP_SIZE = 0.05

MESH = pl.DeviceIdType.MESH


def product(left, right):
    return jnp.dot(left, right, preferred_element_type=jnp.float32)


CHUNKS = 4


def column_of(row, eye):
    return jnp.sum(jnp.where(eye, jnp.broadcast_to(row, eye.shape), 0.0), axis=1, keepdims=True)


def identity(size):
    return lax.broadcasted_iota(jnp.int32, (size, size), 0) == lax.broadcasted_iota(
        jnp.int32, (size, size), 1
    )


def greet():
    barrier = pltpu.get_barrier_semaphore()
    total = 0
    for axis in ("layer", "dp"):
        count, mine = lax.axis_size(axis), lax.axis_index(axis)
        for step in range(1, count):
            pl.semaphore_signal(
                barrier, inc=1, device_id={axis: lax.rem(mine + step, count)}, device_id_type=MESH
            )
        total += count - 1
    pl.semaphore_wait(barrier, total)


def remote(source, target, send_sem, recv_sem, axis, step):
    count, mine = lax.axis_size(axis), lax.axis_index(axis)
    return pltpu.make_async_remote_copy(
        src_ref=source,
        dst_ref=target,
        send_sem=send_sem,
        recv_sem=recv_sem,
        device_id={axis: lax.rem(mine + step + count, count)},
        device_id_type=MESH,
    )


class Line:
    def __init__(self, axis, source, target, send_sem, recv_sem, pieces):
        self.axis, self.count, self.mine = axis, lax.axis_size(axis), lax.axis_index(axis)
        self.source, self.target, self.pieces = source, target, pieces
        self.send_sem, self.recv_sem = send_sem, recv_sem

    def copy(self, way, hop, piece):
        sign = 1 if way == 0 else -1
        block = jnp.clip(self.mine - sign * hop, 0, self.count - 1)
        landing = self.target(block, piece)
        return remote(
            self.source(piece) if hop == 0 else landing,
            landing,
            self.send_sem.at[way, hop, piece],
            self.recv_sem.at[way, hop, piece],
            self.axis,
            sign,
        )

    def has_next(self, way):
        return self.mine < self.count - 1 if way == 0 else self.mine > 0

    def has_block(self, way, hop):
        return self.mine >= hop if way == 0 else self.mine + hop <= self.count - 1

    def begin(self, pieces):
        for piece in pieces:
            for way in (0, 1):

                @pl.when(self.has_next(way))
                def _():
                    self.copy(way, 0, piece).start()

    def arrive(self, hop, pieces, then=None):
        for piece in pieces:
            for way in (0, 1):

                @pl.when(self.has_block(way, hop))
                def _():
                    self.copy(way, hop - 1, piece).wait_recv()
                    if hop < self.count - 1:

                        @pl.when(self.has_next(way))
                        def _():
                            self.copy(way, hop, piece).start()

                    if then is not None:
                        sign = 1 if way == 0 else -1
                        then(jnp.clip(self.mine - sign * hop, 0, self.count - 1), piece)

    def finish(self, pieces=None):
        for hop in range(self.count - 1):
            for piece in pieces or range(self.pieces):
                for way in (0, 1):

                    @pl.when(self.has_next(way) & self.has_block(way, hop))
                    def _():
                        self.copy(way, hop, piece).wait_send()


def front_kernel(
    fresh_weight,
    acts, grads, factor_old, cross_old,
    factor_out, cross_out, factor_high_out, factor_low_out, cross_high_out, cross_low_out, lent_out,
    initial_out, full_out, upper_out, grads_out, solved_out, scales_out, own_scales_out,
    tokens, upper, factor, cross, grads_in, solved, scaled,
    sums_away, sums_in, own_scales, scales, own_turned,
    factor_high, factor_low, cross_high, cross_low, lent,
    line_send, line_recv, lift_send, lift_recv, grad_send, grad_recv, sum_send, sum_recv,
    scale_send, scale_recv, start_send, start_recv, first_send, first_recv, rise_send, rise_recv, local_sem,
):
    layers, groups = lax.axis_size("layer"), lax.axis_size("dp")
    layer, group = lax.axis_index("layer"), lax.axis_index("dp")
    rows, features = factor.shape
    count = acts.shape[0]
    part = count // CHUNKS
    chunk = rows // layers
    columns = grads.shape[2]
    own = pl.ds(pl.multiple_of(group * rows, rows), rows)

    def span(piece):
        return pl.ds(piece * part, part)

    load_acts = pltpu.make_async_copy(acts, tokens.at[group], local_sem.at[0])
    load_factor = pltpu.make_async_copy(factor_old, factor, local_sem.at[1])
    load_cross = pltpu.make_async_copy(cross_old, cross, local_sem.at[2])
    load_grads = pltpu.make_async_copy(grads.at[layer], grads_in.at[layer], local_sem.at[3])
    load_acts.start()
    load_cross.start()
    load_factor.start()
    load_grads.start()
    greet()

    line = Line(
        "dp",
        lambda piece: acts.at[span(piece)],
        lambda block, piece: tokens.at[block, span(piece)],
        line_send,
        line_recv,
        CHUNKS,
    )

    def lift_copy(source, block, piece):
        return remote(
            source,
            upper.at[block, span(piece)],
            lift_send.at[block, piece],
            lift_recv.at[block, piece],
            "layer",
            -1,
        )

    def lift(block, piece):
        @pl.when(layer > 0)
        def _():
            lift_copy(tokens.at[block, span(piece)], block, piece).start()

    @pl.when(layer > 0)
    def _():
        for piece in range(CHUNKS):
            lift_copy(acts.at[span(piece)], group, piece).start()

    def grad_copy(step):
        peer = lax.rem(layer + step, layers)
        return remote(
            grads.at[peer], grads_in.at[layer], grad_send.at[step - 1], grad_recv.at[step - 1],
            "layer", step,
        )

    for step in range(layers - 1, 0, -1):
        grad_copy(step).start()
    line.begin(range(CHUNKS // 2))

    load_acts.wait()
    sums_away[...] = jnp.zeros_like(sums_away)
    for place in range(groups):
        wide = tokens[group, :, place * rows : (place + 1) * rows].astype(jnp.float32)
        sums_away[place, 0:1, :] = jnp.sum(wide * wide, axis=0, keepdims=True)
    load_cross.wait()
    load_factor.wait()
    eye = identity(rows)
    factor_diagonal = jnp.sum(jnp.where(eye, factor[:, own], 0.0), axis=1, keepdims=True)
    cross_diagonal = jnp.sum(jnp.where(eye, cross[:, own], 0.0), axis=1, keepdims=True)

    @pl.when(layer < layers - 1)
    def _():
        for piece in range(CHUNKS):
            lift_copy(acts.at[span(piece)], group, piece).wait_recv()
        for place in range(groups):
            cut = slice(place * rows, (place + 1) * rows)
            wide = tokens[group, :, cut].astype(jnp.float32)
            above = upper[group, :, cut].astype(jnp.float32)
            sums_away[place, 1:2, :] = jnp.sum(wide * above, axis=0, keepdims=True)

    @pl.when(layer == layers - 1)
    def _():
        upper[...] = jnp.zeros_like(upper)

    def sum_copy(step):
        peer = lax.rem(group + step, groups)
        return remote(
            sums_away.at[peer], sums_in.at[group], sum_send.at[step - 1], sum_recv.at[step - 1],
            "dp", step,
        )

    for step in range(groups - 1, 0, -1):
        sum_copy(step).start()
    line.begin(range(CHUNKS // 2, CHUNKS))
    sums_in[group] = sums_away[group]
    line.arrive(1, range(CHUNKS // 2))

    for step in range(groups - 1, 0, -1):
        sum_copy(step).wait_recv()
    sums = fresh_weight * jnp.sum(sums_in[...], axis=0)
    own_sum = column_of(sums[0:1], eye)
    next_sum = column_of(sums[1:2], eye)
    own_diagonal = FACTOR_DECAY * factor_diagonal + own_sum
    own_coupling = FACTOR_DECAY * cross_diagonal + next_sum
    lane = lax.broadcasted_iota(jnp.int32, (rows, 128), 1)
    own_scales[...] = jnp.where(
        lane == 0,
        DAMPING + own_diagonal,
        jnp.where(lane == 1, own_coupling, jnp.where(lane == 2, own_diagonal, next_sum)),
    )

    def scale_copy(step):
        peer = lax.rem(layer + step, layers)
        return remote(
            own_scales.at[pl.ds(pl.multiple_of(peer * chunk, chunk), chunk)],
            scales.at[layer], scale_send.at[step - 1], scale_recv.at[step - 1], "layer", step,
        )

    for step in range(layers - 1, 0, -1):
        scale_copy(step).start()
    scales[layer] = own_scales[pl.ds(pl.multiple_of(layer * chunk, chunk), chunk), :]
    line.arrive(1, range(CHUNKS // 2, CHUNKS))
    for way in (0, 1):

        @pl.when(line.has_block(way, 1))
        def _():
            for piece in range(CHUNKS):
                lift(jnp.clip(group - (1 if way == 0 else -1), 0, groups - 1), piece)

    load_grads.wait()
    for step in range(layers - 1, 0, -1):
        scale_copy(step).wait_recv()
        grad_copy(step).wait_recv()

    width = scaled.shape[2]

    def solve(tile, carry):
        cut = pl.ds(pl.multiple_of(tile * width, width), width)
        passed = None
        for place in range(layers):
            target = grads_in[place, :, cut].astype(jnp.float32)
            if place:
                target = target - passed
            value = target / scales[place, :, 0:1]
            scaled[place] = value
            passed = scales[place, :, 1:2] * value
        result = value
        solved[layers - 1, :, cut] = result.astype(jnp.bfloat16)
        for place in range(layers - 2, -1, -1):
            ratio = scales[place, :, 1:2] / scales[place, :, 0:1]
            result = scaled[place] - ratio * result
            solved[place, :, cut] = result.astype(jnp.bfloat16)
        return carry

    lax.fori_loop(0, columns // width, solve, 0)

    def start_copy(step):
        peer = lax.rem(layer + step, layers)
        return remote(
            solved.at[peer], initial_out.at[layer], start_send.at[step - 1],
            start_recv.at[step - 1], "layer", step,
        )

    for step in range(layers - 1, 0, -1):
        start_copy(step).start()
    stores = [
        pltpu.make_async_copy(solved.at[layer], initial_out.at[layer], local_sem.at[0]),
        pltpu.make_async_copy(grads_in, grads_out, local_sem.at[1]),
        pltpu.make_async_copy(solved, solved_out, local_sem.at[2]),
        pltpu.make_async_copy(scales, scales_out, local_sem.at[3]),
        pltpu.make_async_copy(own_scales, own_scales_out, local_sem.at[4]),
    ]
    for store in stores:
        store.start()

    for hop in range(2, groups - 1):
        line.arrive(hop, range(CHUNKS), lift)

    line.arrive(groups - 1, [0], lift)
    for step in range(1, layers):
        start_copy(step).wait_recv()
    stores[0].wait()

    piece_width = columns // PIECES
    begun = initial_out.at[:, :, 0:piece_width]
    first = Line(
        "dp",
        lambda piece: begun,
        lambda block, piece: full_out.at[block],
        first_send,
        first_recv,
        1,
    )

    def rise_copy(source, block):
        return remote(
            source, upper_out.at[block], rise_send.at[block], rise_recv.at[block], "layer", -1
        )

    def rise(block, piece):
        @pl.when(layer > 0)
        def _():
            rise_copy(full_out.at[block], block).start()

    first.begin([0])

    @pl.when(layer > 0)
    def _():
        rise_copy(begun, group).start()

    line.arrive(groups - 1, range(1, CHUNKS), lift)

    tile = 256
    every = count * groups

    def gather(ref, cut):
        return ref[:, :, cut].reshape(every, cut.size)

    own_turned[...] = gather(tokens, own).astype(jnp.float32).T.astype(jnp.bfloat16)

    def refresh_factor(place, carry):
        cut = pl.ds(pl.multiple_of(place * tile, tile), tile)
        value = product(own_turned[...], gather(tokens, cut))
        value = FACTOR_DECAY * factor[:, cut] + fresh_weight * value
        factor[:, cut] = value
        high = value.astype(jnp.bfloat16)
        factor_high[:, cut] = high
        factor_low[:, cut] = (value - high.astype(jnp.float32)).astype(jnp.bfloat16)
        return carry

    tiles = features // tile
    lax.fori_loop(0, tiles // 2, refresh_factor, 0)
    first.arrive(1, [0], rise)
    lax.fori_loop(tiles // 2, tiles, refresh_factor, 0)
    for hop in range(2, groups - 1):
        first.arrive(hop, [0], rise)
    more = [
        pltpu.make_async_copy(factor, factor_out, local_sem.at[10]),
        pltpu.make_async_copy(factor_high, factor_high_out, local_sem.at[5]),
        pltpu.make_async_copy(factor_low, factor_low_out, local_sem.at[6]),
    ]
    for store in more:
        store.start()
    stores += more

    @pl.when(layer < layers - 1)
    def _():
        for step in range(1, groups):
            block = lax.rem(group + step, groups)
            for piece in range(CHUNKS):
                lift_copy(acts.at[span(piece)], block, piece).wait_recv()

    def refresh_cross(place, carry):
        cut = pl.ds(pl.multiple_of(place * tile, tile), tile)
        value = product(own_turned[...], gather(upper, cut))
        value = FACTOR_DECAY * cross[:, cut] + fresh_weight * value
        cross[:, cut] = value
        high = value.astype(jnp.bfloat16)
        cross_high[:, cut] = high
        cross_low[:, cut] = (value - high.astype(jnp.float32)).astype(jnp.bfloat16)
        lent[cut, :] = value.T.astype(jnp.bfloat16)
        return carry

    lax.fori_loop(0, tiles, refresh_cross, 0)
    more = [
        pltpu.make_async_copy(cross, cross_out, local_sem.at[11]),
        pltpu.make_async_copy(cross_high, cross_high_out, local_sem.at[7]),
        pltpu.make_async_copy(cross_low, cross_low_out, local_sem.at[8]),
    ]
    for store in more:
        store.start()
    stores += more

    lent[own, :] = jnp.where(eye, 0.0, lent[own, :].astype(jnp.float32)).astype(jnp.bfloat16)
    last = pltpu.make_async_copy(lent, lent_out, local_sem.at[9])
    last.start()
    stores.append(last)

    first.arrive(groups - 1, [0], rise)

    @pl.when(layer < layers - 1)
    def _():
        for block in range(groups):
            rise_copy(begun, block).wait_recv()

    @pl.when(layer > 0)
    def _():
        for block in range(groups):
            rise_copy(begun, block).wait_send()

    for step in range(1, layers):
        start_copy(step).wait_send()
        grad_copy(step).wait_send()
        scale_copy(step).wait_send()
    for step in range(1, groups):
        sum_copy(step).wait_send()

    @pl.when(layer > 0)
    def _():
        for block in range(groups):
            for piece in range(CHUNKS):
                lift_copy(acts.at[span(piece)], block, piece).wait_send()

    line.finish()
    first.finish()
    for store in stores[1:]:
        store.wait()


def front(fresh_weight, acts, grads, factor_old, cross_old):
    layers, groups = lax.axis_size("layer"), lax.axis_size("dp")
    rows, features = factor_old.shape
    count = acts.shape[0]
    chunk, columns = grads.shape[1:]
    every = count * groups
    half, full = jnp.bfloat16, jnp.float32
    dma = pltpu.SemaphoreType.DMA
    shape = jax.ShapeDtypeStruct
    return pl.pallas_call(
        functools.partial(front_kernel, fresh_weight),
        out_shape=[shape((rows, features), full)] * 2
        + [shape((rows, features), half)] * 4
        + [shape((features, rows), half)]
        + [shape((layers, chunk, columns), half)]
        + [shape((groups, layers, chunk, columns // PIECES), half)] * 2
        + [shape((layers, chunk, columns), half)] * 2
        + [shape((layers, chunk, 128), full), shape((rows, 128), full)],
        in_specs=[pl.BlockSpec(memory_space=pl.ANY)] * 4,
        out_specs=[pl.BlockSpec(memory_space=pl.ANY)] * 14,
        scratch_shapes=[
            pltpu.VMEM((groups, count, features), half),
            pltpu.VMEM((groups, count, features), half),
            pltpu.VMEM((rows, features), full),
            pltpu.VMEM((rows, features), full),
            pltpu.VMEM((layers, chunk, columns), half),
            pltpu.VMEM((layers, chunk, columns), half),
            pltpu.VMEM((layers, chunk, 256), full),
            pltpu.VMEM((groups, 8, rows), full),
            pltpu.VMEM((groups, 8, rows), full),
            pltpu.VMEM((rows, 128), full),
            pltpu.VMEM((layers, chunk, 128), full),
            pltpu.VMEM((rows, every), half),
        ]
        + [pltpu.VMEM((rows, features), half)] * 4
        + [pltpu.VMEM((features, rows), half)]
        + [dma((2, groups - 1, CHUNKS))] * 2
        + [dma((groups, CHUNKS))] * 2
        + [dma((layers - 1,))] * 2
        + [dma((groups - 1,))] * 2
        + [dma((layers - 1,))] * 4
        + [dma((2, groups - 1, 1))] * 2
        + [dma((groups,))] * 2
        + [dma((12,))],
        compiler_params=pltpu.CompilerParams(
            collective_id=0, has_side_effects=True, vmem_limit_bytes=63 << 20
        ),
        cost_estimate=pl.CostEstimate(
            flops=6 * every * rows * features, bytes_accessed=200_000_000, transcendentals=0
        ),
        name="front",
    )(acts, grads, factor_old, cross_old)


PIECES = 4
ORDER = (
    "begin 3", "multiply 0", "lend 0", "meet 1", "begin 2", "away 0",
    "meet 3", "lend 1", "near 0", "carry 3", "lend 2", "meet 2",
    "join 0", "carry 1", "away 1", "end 1", "correct 0", "near 1",
    "carry 2", "away 2", "update 0", "join 1", "lend 3", "end 3",
    "multiply 1", "end 2", "multiply 2", "near 2", "correct 1", "multiply 3",
    "first 0", "update 1", "join 2", "middle 0", "away 3", "correct 2",
    "final 0", "update 2", "near 3", "first 1", "join 3", "first 2",
    "correct 3", "middle 1", "update 3", "final 1", "first 3", "final 2 3",
    "middle 2 3",
)


class Sums:
    def __init__(self, axis, source, target, send_sem, recv_sem):
        self.axis, self.count, self.mine = axis, lax.axis_size(axis), lax.axis_index(axis)
        self.source, self.target = source, target
        self.send_sem, self.recv_sem = send_sem, recv_sem

    def copy(self, way, piece, owner):
        return remote(
            self.source(piece, owner),
            self.target(way, piece, owner),
            self.send_sem.at[way, piece, owner],
            self.recv_sem.at[way, piece, owner],
            self.axis,
            1 if way == 0 else -1,
        )

    def has_before(self, way):
        return self.mine > 0 if way == 0 else self.mine < self.count - 1

    def begin(self, piece, add):
        for way in (0, 1):

            @pl.when(jnp.logical_not(self.has_before(way)))
            def _():
                for distance in range(self.count - 1, 0, -1):
                    place = distance if way == 0 else self.count - 1 - distance
                    add(way, piece, place, False)
                    self.copy(way, piece, place).start()

    def step(self, piece, distance, add):
        for way in (0, 1):
            owner = self.mine + (distance if way == 0 else -distance)

            @pl.when((owner >= 0) & (owner < self.count) & self.has_before(way))
            def _():
                place = jnp.clip(owner, 0, self.count - 1)
                self.copy(way, piece, place).wait_recv()
                add(way, piece, place, True)
                self.copy(way, piece, place).start()

    def close(self, piece):
        for way in (0, 1):

            @pl.when(self.has_before(way))
            def _():
                self.copy(way, piece, self.mine).wait_recv()

    def finish(self, pieces):
        for piece in range(pieces):
            for distance in range(1, self.count):
                for way in (0, 1):
                    owner = self.mine + (distance if way == 0 else -distance)

                    @pl.when((owner >= 0) & (owner < self.count))
                    def _():
                        self.copy(way, piece, jnp.clip(owner, 0, self.count - 1)).wait_send()


def back_kernel(
    exponents,
    factor_high_in, factor_low_in, cross_high_in, cross_low_in, lent_in,
    initial_in, full_in, upper_in, grads_in, solved_in, scales_in, own_scales_in, moments_in, master_in,
    moments_out, master_out, replicas_out,
    factor_high, factor_low, cross_high, cross_low, lent,
    initial, grads, solved, scales, own_scales, moments, powers, master,
    full, upper, sums, sums_in, away, lowered, away_in, lowered_in, scaled, fixed, fixed_in,
    moments_new, master_new, replicas,
    first_send, first_recv, sum_send, sum_recv, last_send, last_recv, lift_send, lift_recv,
    away_send, away_recv, lowered_send, lowered_recv, fixed_send, fixed_recv, load_sem, store_sem,
):
    layers, groups = lax.axis_size("layer"), lax.axis_size("dp")
    layer, group = lax.axis_index("layer"), lax.axis_index("dp")
    rows, columns = initial.shape
    chunk = rows // layers
    width = columns // PIECES
    features = rows * groups

    def cut(piece):
        return slice(piece * width, (piece + 1) * width)

    pairs = (
        (initial_in, initial),
        (factor_high_in, factor_high),
        (factor_low_in, factor_low),
        (cross_high_in, cross_high),
        (cross_low_in, cross_low),
        (lent_in, lent),
        (own_scales_in, own_scales),
        (grads_in, grads),
        (solved_in, solved),
        (scales_in, scales),
        (moments_in, moments),
        (master_in, master),
    )
    loads = [
        pltpu.make_async_copy(source, target, load_sem.at[place])
        for place, (source, target) in enumerate(pairs)
    ]
    for load in loads:
        load.start()
    greet()

    first = Line(
        "dp",
        lambda piece: initial_in.at[:, cut(piece)],
        lambda block, piece: full.at[piece, block],
        first_send,
        first_recv,
        PIECES,
    )
    last = Line(
        "dp",
        lambda piece: replicas.at[piece],
        lambda block, piece: replicas_out.at[block, :, cut(piece)],
        last_send,
        last_recv,
        PIECES,
    )

    def lift_copy(source, block, piece):
        return remote(
            source, upper.at[piece, block], lift_send.at[piece, block], lift_recv.at[piece, block],
            "layer", -1,
        )

    def lift(block, piece):
        @pl.when(layer > 0)
        def _():
            lift_copy(full.at[piece, block], block, piece).start()

    def begin(piece):
        first.begin([piece])

        @pl.when(layer > 0)
        def _():
            lift_copy(initial_in.at[:, cut(piece)], group, piece).start()

    begin(1)
    ready = [
        pltpu.make_async_copy(
            full_in.at[lax.rem(group + step, groups)],
            full.at[0, lax.rem(group + step, groups)],
            load_sem.at[len(pairs) + step],
        )
        for step in range(1, groups)
    ]
    ready_upper = pltpu.make_async_copy(upper_in, upper.at[0], load_sem.at[len(pairs)])
    for load in ready:
        load.start()

    @pl.when(layer < layers - 1)
    def _():
        ready_upper.start()

    @pl.when(layer == layers - 1)
    def _():
        upper[...] = jnp.zeros_like(upper)

    loads[0].wait()
    for piece in range(PIECES):
        full[piece, group] = initial[:, cut(piece)]

    def relay_copy(which, piece, step):
        source, target, send_sem, recv_sem = (
            (away, away_in, away_send, away_recv),
            (lowered, lowered_in, lowered_send, lowered_recv),
            (fixed, fixed_in, fixed_send, fixed_recv),
        )[which]
        peer = lax.rem(layer + step, layers)
        return remote(
            source.at[piece, peer], target.at[piece, layer],
            send_sem.at[step - 1, piece], recv_sem.at[step - 1, piece], "layer", step,
        )

    def multiply(piece):
        @pl.when(layer < layers - 1)
        def _():
            if piece == 0:
                ready_upper.wait()
            else:
                for block in range(groups):
                    lift_copy(full.at[piece, block], block, piece).wait_recv()

        def some(place, carry):
            part = pl.ds(pl.multiple_of(place * chunk * 2, chunk * 2), chunk * 2)
            mine = full[piece].reshape(features, width)
            theirs = upper[piece].reshape(features, width)
            value = product(factor_high[part, :], mine) + product(factor_low[part, :], mine)
            value = value - own_scales[part, 2:3] * full[piece, group, part, :].astype(jnp.float32)
            value = value + product(cross_high[part, :], theirs) + product(cross_low[part, :], theirs)
            value = value - own_scales[part, 1:2] * upper[piece, group, part, :].astype(jnp.float32)
            for side in range(2):
                inner = slice(side * chunk, (side + 1) * chunk)
                away[piece, 2 * place + side] = value[inner].astype(jnp.bfloat16)
            return carry

        lax.fori_loop(0, layers // 2, some, 0)
        for step in range(layers - 1, 0, -1):
            relay_copy(0, piece, step).start()
        away_in[piece, layer] = away[piece, layer]

    def block_of(place):
        return pl.ds(pl.multiple_of(place * rows, rows), rows)

    def add(way, piece, place, more):
        value = product(lent[block_of(place), :], initial[:, cut(piece)])
        if more:
            value = value + sums_in[way, piece, place].astype(jnp.float32)
        sums[piece, place] = value.astype(jnp.bfloat16)

    lower = Sums(
        "dp",
        lambda piece, owner: sums.at[piece, owner],
        lambda way, piece, owner: sums_in.at[way, piece, owner],
        sum_send,
        sum_recv,
    )

    def join(piece):
        lower.close(piece)
        value = product(lent[block_of(group), :], initial[:, cut(piece)])
        for way in (0, 1):
            value = value + sums_in[way, piece, group].astype(jnp.float32)
        for place in range(layers):
            part = value[place * chunk : (place + 1) * chunk]
            lowered[piece, place] = part.astype(jnp.bfloat16)
        for step in range(layers - 1, 0, -1):
            relay_copy(1, piece, step).start()
        lowered_in[piece, layer] = lowered[piece, layer]

    def correct(piece):
        for step in range(layers - 1, 0, -1):
            relay_copy(0, piece, step).wait_recv()
            relay_copy(1, piece, step).wait_recv()
        part = cut(piece)

        def wide(ref, place):
            return ref[place, :, part].astype(jnp.float32)

        passed = None
        for place in range(layers):
            target = wide(grads, place) - scales[place, :, 0:1] * wide(solved, place)
            if place < layers - 1:
                target = target - scales[place, :, 1:2] * wide(solved, place + 1)
            target = target - away_in[piece, place].astype(jnp.float32)
            if place:
                target = target - scales[place - 1, :, 1:2] * wide(solved, place - 1)
                target = target - lowered_in[piece, place - 1].astype(jnp.float32)
                target = target - passed
            value = target / scales[place, :, 0:1]
            scaled[place] = value
            passed = scales[place, :, 1:2] * value
        result = value
        fixed[piece, layers - 1] = result.astype(jnp.bfloat16)
        for place in range(layers - 2, -1, -1):
            ratio = scales[place, :, 1:2] / scales[place, :, 0:1]
            result = scaled[place] - ratio * result
            fixed[piece, place] = result.astype(jnp.bfloat16)
        for step in range(layers - 1, 0, -1):
            relay_copy(2, piece, step).start()
        fixed_in[piece, layer] = fixed[piece, layer]

    stores = []

    def update(piece):
        for step in range(layers - 1, 0, -1):
            relay_copy(2, piece, step).wait_recv()
        part = cut(piece)

        def some(place, carry):
            inner = pl.ds(pl.multiple_of(place * chunk, chunk), chunk)
            change = initial[inner, part].astype(jnp.float32) + fixed_in[piece, place].astype(
                jnp.float32
            )
            moment = MOMENTUM * moments[inner, part].astype(jnp.float32) * powers[inner, 0:1]
            moment = moment + (1.0 - MOMENTUM) * change
            moments_new[inner, part] = (moment * powers[inner, 1:2]).astype(jnp.bfloat16)
            weights = master[inner, part] - STEP_SIZE * moment
            master_new[inner, part] = weights
            replicas[piece, inner, :] = weights.astype(jnp.bfloat16)
            return carry

        lax.fori_loop(0, layers, some, 0)
        last.begin([piece])
        for place, (source, target) in enumerate(
            (
                (replicas.at[piece], replicas_out.at[group, :, part]),
                (master_new.at[:, part], master_out.at[:, part]),
                (moments_new.at[:, part], moments_out.at[:, part]),
            )
        ):
            stores.append(pltpu.make_async_copy(source, target, store_sem.at[place, piece]))
            stores[-1].start()

    far = groups - 1
    lane = lax.broadcasted_iota(jnp.int32, (SCALE_BLOCK, 128), 1)
    for place in range(rows // SCALE_BLOCK):
        power = jnp.full((SCALE_BLOCK, 128), exponents[0, place].astype(jnp.float32))
        powers[place * SCALE_BLOCK : (place + 1) * SCALE_BLOCK, :] = jnp.exp2(
            jnp.where(lane == 0, power, -power)
        )
    for way, end in ((0, 0), (1, groups - 1)):

        @pl.when(group == end)
        def _():
            for piece in range(PIECES):
                sums_in[way, piece, end] = jnp.zeros_like(sums_in[way, piece, end])

    for load in loads[1:] + ready:
        load.wait()
    tasks = dict(
        begin=begin,
        meet=lambda piece: first.arrive(1, [piece], lift),
        carry=lambda piece: [first.arrive(hop, [piece], lift) for hop in range(2, far)],
        end=lambda piece: first.arrive(far, [piece], lift),
        lend=lambda piece: lower.begin(piece, add),
        away=lambda piece: [lower.step(piece, distance, add) for distance in range(far - 1, 1, -1)],
        near=lambda piece: lower.step(piece, 1, add),
        multiply=multiply,
        join=join,
        correct=correct,
        update=update,
        first=lambda piece: last.arrive(1, [piece]),
        middle=lambda piece: [last.arrive(hop, [piece]) for hop in range(2, far)],
        final=lambda piece: last.arrive(far, [piece]),
    )
    for entry in ORDER:
        name, *pieces = entry.split()
        for piece in pieces:
            tasks[name](int(piece))

    for piece in range(PIECES):
        for step in range(1, layers):
            for which in range(3):
                relay_copy(which, piece, step).wait_send()

        if piece:

            @pl.when(layer > 0)
            def _():
                for block in range(groups):
                    lift_copy(full.at[piece, block], block, piece).wait_send()

    first.finish(range(1, PIECES))
    lower.finish(PIECES)
    last.finish()
    for store in stores:
        store.wait()


def back(exponents, matrices, initial, full_first, upper_first, grads, solved, scales, own_scales, moments, master):
    layers, groups = lax.axis_size("layer"), lax.axis_size("dp")
    rows, columns = initial.shape
    features = matrices[0].shape[1]
    chunk, width = rows // layers, columns // PIECES
    half, full = jnp.bfloat16, jnp.float32
    dma = pltpu.SemaphoreType.DMA
    shape = jax.ShapeDtypeStruct
    swapped = pltpu.VMEM((PIECES, layers, chunk, width), half)
    return pl.pallas_call(
        back_kernel,
        out_shape=[
            shape((rows, columns), half),
            shape((rows, columns), full),
            shape((groups, rows, columns), half),
        ],
        in_specs=[pl.BlockSpec(memory_space=pltpu.SMEM)]
        + [pl.BlockSpec(memory_space=pl.ANY)] * 14,
        out_specs=[pl.BlockSpec(memory_space=pl.ANY)] * 3,
        scratch_shapes=[pltpu.VMEM((rows, features), half)] * 4
        + [pltpu.VMEM((features, rows), half)]
        + [
            pltpu.VMEM((rows, columns), half),
            pltpu.VMEM((layers, chunk, columns), half),
            pltpu.VMEM((layers, chunk, columns), half),
            pltpu.VMEM((layers, chunk, 128), full),
            pltpu.VMEM((rows, 128), full),
            pltpu.VMEM((rows, columns), half),
            pltpu.VMEM((rows, 128), full),
            pltpu.VMEM((rows, columns), full),
            pltpu.VMEM((PIECES, groups, rows, width), half),
            pltpu.VMEM((PIECES, groups, rows, width), half),
            pltpu.VMEM((PIECES, groups, rows, width), half),
            pltpu.VMEM((2, PIECES, groups, rows, width), half),
        ]
        + [swapped] * 4
        + [pltpu.VMEM((layers, chunk, width), full)]
        + [swapped] * 2
        + [
            pltpu.VMEM((rows, columns), half),
            pltpu.VMEM((rows, columns), full),
            pltpu.VMEM((PIECES, rows, width), half),
        ]
        + [dma((2, groups - 1, PIECES))] * 2
        + [dma((2, PIECES, groups))] * 2
        + [dma((2, groups - 1, PIECES))] * 2
        + [dma((PIECES, groups))] * 2
        + [dma((layers - 1, PIECES))] * 6
        + [dma((12 + groups,)), dma((3, PIECES))],
        compiler_params=pltpu.CompilerParams(
            collective_id=1, has_side_effects=True, vmem_limit_bytes=58 << 20
        ),
        cost_estimate=pl.CostEstimate(
            flops=10 * features * rows * columns, bytes_accessed=300_000_000, transcendentals=0
        ),
        name="back",
    )(
        exponents, *matrices, initial, full_first, upper_first, grads, solved, scales, own_scales,
        moments, master,
    )


def body(activations, factor_old, cross_old, gradients, moments, exponents, master):
    layers, groups = lax.axis_size("layer"), lax.axis_size("dp")
    row_count, features = factor_old.shape[1:]
    columns = gradients.shape[2]
    chunk = row_count // layers
    fresh_weight = (1.0 - FACTOR_DECAY) / (activations.shape[1] * groups)
    factor_new, cross_new, *rest = front(
        fresh_weight,
        activations[0],
        gradients[0].reshape(layers, chunk, columns),
        factor_old[0],
        cross_old[0],
    )
    *matrices, initial, full_first, upper_first, grad_swapped, initial_swapped, scales, own_scales = rest
    moments_new, master_new, replicas = back(
        exponents,
        matrices,
        initial.reshape(row_count, columns),
        full_first.reshape(groups, row_count, -1),
        upper_first.reshape(groups, row_count, -1),
        grad_swapped,
        initial_swapped,
        scales,
        own_scales,
        moments[0],
        master[0],
    )
    replicas = replicas.reshape(features, columns)
    return (factor_new[None], cross_new[None], moments_new[None], master_new[None], replicas[None])


def solution(mesh):
    return jax.shard_map(
        body,
        mesh=mesh,
        in_specs=(
            P("layer", "dp", None),
            P("layer", "dp", None),
            P("layer", "dp", None),
            P("layer", "dp", None),
            P("layer", "dp", None),
            P("layer", "dp"),
            P("layer", "dp", None),
        ),
        out_specs=(
            P("layer", "dp", None),
            P("layer", "dp", None),
            P("layer", "dp", None),
            P("layer", "dp", None),
            P("layer", None, None),
        ),
        check_vma=False,
    )
```

```python
import functools

import jax
import jax.numpy as jnp
from jax import lax
from jax.experimental import pallas as pl
from jax.experimental.pallas import tpu as pltpu
from jax.sharding import PartitionSpec as P

SCALE_BLOCK = 128


FACTOR_DECAY = 0.9
DAMPING = 0.5
MOMENTUM = 0.8
STEP_SIZE = 0.05

MESH = pl.DeviceIdType.MESH


def product(left, right):
    return jnp.dot(left, right, preferred_element_type=jnp.float32)


CHUNKS = 4


def column_of(row, eye):
    return jnp.sum(jnp.where(eye, jnp.broadcast_to(row, eye.shape), 0.0), axis=1, keepdims=True)


def identity(size):
    return lax.broadcasted_iota(jnp.int32, (size, size), 0) == lax.broadcasted_iota(
        jnp.int32, (size, size), 1
    )


def greet():
    barrier = pltpu.get_barrier_semaphore()
    total = 0
    for axis in ("layer", "dp"):
        count, mine = lax.axis_size(axis), lax.axis_index(axis)
        for step in range(1, count):
            pl.semaphore_signal(
                barrier, inc=1, device_id={axis: lax.rem(mine + step, count)}, device_id_type=MESH
            )
        total += count - 1
    pl.semaphore_wait(barrier, total)


def remote(source, target, send_sem, recv_sem, axis, step):
    count, mine = lax.axis_size(axis), lax.axis_index(axis)
    return pltpu.make_async_remote_copy(
        src_ref=source,
        dst_ref=target,
        send_sem=send_sem,
        recv_sem=recv_sem,
        device_id={axis: lax.rem(mine + step + count, count)},
        device_id_type=MESH,
    )


class Line:
    def __init__(self, axis, source, target, send_sem, recv_sem, pieces):
        self.axis, self.count, self.mine = axis, lax.axis_size(axis), lax.axis_index(axis)
        self.source, self.target, self.pieces = source, target, pieces
        self.send_sem, self.recv_sem = send_sem, recv_sem
        self.given = {}

    def copy(self, way, hop, piece):
        sign = 1 if way == 0 else -1
        block = jnp.clip(self.mine - sign * hop, 0, self.count - 1)
        landing = self.target(block, piece)
        return remote(
            self.source(piece) if hop == 0 else landing,
            landing,
            self.send_sem.at[way, hop, piece],
            self.recv_sem.at[way, hop, piece],
            self.axis,
            sign,
        )

    def has_next(self, way):
        return self.mine < self.count - 1 if way == 0 else self.mine > 0

    def has_block(self, way, hop):
        return self.mine >= hop if way == 0 else self.mine + hop <= self.count - 1

    def begin(self, pieces):
        for piece in pieces:
            for way in (0, 1):

                @pl.when(self.has_next(way))
                def _():
                    self.copy(way, 0, piece).start()

    def arrive(self, hop, pieces, then=None):
        for piece in pieces:
            for way in (0, 1):

                @pl.when(self.has_block(way, hop))
                def _():
                    if hop == 1 and piece in self.given:
                        self.given[piece](way)
                    else:
                        self.copy(way, hop - 1, piece).wait_recv()
                    if hop < self.count - 1:

                        @pl.when(self.has_next(way))
                        def _():
                            self.copy(way, hop, piece).start()

                    if then is not None:
                        sign = 1 if way == 0 else -1
                        then(jnp.clip(self.mine - sign * hop, 0, self.count - 1), piece)

    def finish(self, pieces=None):
        for hop in range(self.count - 1):
            for piece in pieces or range(self.pieces):
                if hop == 0 and piece in self.given:
                    continue
                for way in (0, 1):

                    @pl.when(self.has_next(way) & self.has_block(way, hop))
                    def _():
                        self.copy(way, hop, piece).wait_send()


def front_kernel(
    fresh_weight,
    acts, grads, factor_old, cross_old,
    factor_out, cross_out, factor_high_out, factor_low_out, cross_high_out, cross_low_out, lent_out,
    initial_out, full_out, upper_out, next_out, grads_out, solved_out, scales_out, own_scales_out,
    tokens, upper, factor, cross, grads_in, solved, scaled,
    sums_away, sums_in, own_scales, scales, own_turned,
    factor_high, factor_low, cross_high, cross_low, lent,
    line_send, line_recv, lift_send, lift_recv, grad_send, grad_recv, sum_send, sum_recv,
    scale_send, scale_recv, start_send, start_recv, first_send, first_recv, rise_send, rise_recv, next_send, next_recv, local_sem,
):
    layers, groups = lax.axis_size("layer"), lax.axis_size("dp")
    layer, group = lax.axis_index("layer"), lax.axis_index("dp")
    rows, features = factor.shape
    count = acts.shape[0]
    part = count // CHUNKS
    chunk = rows // layers
    columns = grads.shape[2]
    own = pl.ds(pl.multiple_of(group * rows, rows), rows)

    def span(piece):
        return pl.ds(piece * part, part)

    load_acts = pltpu.make_async_copy(acts, tokens.at[group], local_sem.at[0])
    load_factor = pltpu.make_async_copy(factor_old, factor, local_sem.at[1])
    load_cross = pltpu.make_async_copy(cross_old, cross, local_sem.at[2])
    load_grads = pltpu.make_async_copy(grads.at[layer], grads_in.at[layer], local_sem.at[3])
    load_acts.start()
    load_cross.start()
    load_factor.start()
    load_grads.start()
    greet()

    line = Line(
        "dp",
        lambda piece: acts.at[span(piece)],
        lambda block, piece: tokens.at[block, span(piece)],
        line_send,
        line_recv,
        CHUNKS,
    )

    def lift_copy(source, block, piece):
        return remote(
            source,
            upper.at[block, span(piece)],
            lift_send.at[block, piece],
            lift_recv.at[block, piece],
            "layer",
            -1,
        )

    def lift(block, piece):
        @pl.when(layer > 0)
        def _():
            lift_copy(tokens.at[block, span(piece)], block, piece).start()

    @pl.when(layer > 0)
    def _():
        for piece in range(CHUNKS):
            lift_copy(acts.at[span(piece)], group, piece).start()

    def grad_copy(step):
        peer = lax.rem(layer + step, layers)
        return remote(
            grads.at[peer], grads_in.at[layer], grad_send.at[step - 1], grad_recv.at[step - 1],
            "layer", step,
        )

    for step in range(layers - 1, 0, -1):
        grad_copy(step).start()
    line.begin(range(CHUNKS // 2))

    load_acts.wait()
    sums_away[...] = jnp.zeros_like(sums_away)
    for place in range(groups):
        wide = tokens[group, :, place * rows : (place + 1) * rows].astype(jnp.float32)
        sums_away[place, 0:1, :] = jnp.sum(wide * wide, axis=0, keepdims=True)
    load_cross.wait()
    load_factor.wait()
    eye = identity(rows)
    factor_diagonal = jnp.sum(jnp.where(eye, factor[:, own], 0.0), axis=1, keepdims=True)
    cross_diagonal = jnp.sum(jnp.where(eye, cross[:, own], 0.0), axis=1, keepdims=True)

    @pl.when(layer < layers - 1)
    def _():
        for piece in range(CHUNKS):
            lift_copy(acts.at[span(piece)], group, piece).wait_recv()
        for place in range(groups):
            cut = slice(place * rows, (place + 1) * rows)
            wide = tokens[group, :, cut].astype(jnp.float32)
            above = upper[group, :, cut].astype(jnp.float32)
            sums_away[place, 1:2, :] = jnp.sum(wide * above, axis=0, keepdims=True)

    @pl.when(layer == layers - 1)
    def _():
        upper[...] = jnp.zeros_like(upper)

    def sum_copy(step):
        peer = lax.rem(group + step, groups)
        return remote(
            sums_away.at[peer], sums_in.at[group], sum_send.at[step - 1], sum_recv.at[step - 1],
            "dp", step,
        )

    for step in range(groups - 1, 0, -1):
        sum_copy(step).start()
    line.begin(range(CHUNKS // 2, CHUNKS))
    sums_in[group] = sums_away[group]
    line.arrive(1, range(CHUNKS // 2))

    for step in range(groups - 1, 0, -1):
        sum_copy(step).wait_recv()
    sums = fresh_weight * jnp.sum(sums_in[...], axis=0)
    own_sum = column_of(sums[0:1], eye)
    next_sum = column_of(sums[1:2], eye)
    own_diagonal = FACTOR_DECAY * factor_diagonal + own_sum
    own_coupling = FACTOR_DECAY * cross_diagonal + next_sum
    lane = lax.broadcasted_iota(jnp.int32, (rows, 128), 1)
    own_scales[...] = jnp.where(
        lane == 0,
        DAMPING + own_diagonal,
        jnp.where(lane == 1, own_coupling, jnp.where(lane == 2, own_diagonal, next_sum)),
    )

    def scale_copy(step):
        peer = lax.rem(layer + step, layers)
        return remote(
            own_scales.at[pl.ds(pl.multiple_of(peer * chunk, chunk), chunk)],
            scales.at[layer], scale_send.at[step - 1], scale_recv.at[step - 1], "layer", step,
        )

    for step in range(layers - 1, 0, -1):
        scale_copy(step).start()
    scales[layer] = own_scales[pl.ds(pl.multiple_of(layer * chunk, chunk), chunk), :]
    line.arrive(1, range(CHUNKS // 2, CHUNKS))
    for way in (0, 1):

        @pl.when(line.has_block(way, 1))
        def _():
            for piece in range(CHUNKS):
                lift(jnp.clip(group - (1 if way == 0 else -1), 0, groups - 1), piece)

    load_grads.wait()
    for step in range(layers - 1, 0, -1):
        scale_copy(step).wait_recv()
        grad_copy(step).wait_recv()

    width = scaled.shape[2]

    def solve(tile, carry):
        cut = pl.ds(pl.multiple_of(tile * width, width), width)
        passed = None
        for place in range(layers):
            target = grads_in[place, :, cut].astype(jnp.float32)
            if place:
                target = target - passed
            value = target / scales[place, :, 0:1]
            scaled[place] = value
            passed = scales[place, :, 1:2] * value
        result = value
        solved[layers - 1, :, cut] = result.astype(jnp.bfloat16)
        for place in range(layers - 2, -1, -1):
            ratio = scales[place, :, 1:2] / scales[place, :, 0:1]
            result = scaled[place] - ratio * result
            solved[place, :, cut] = result.astype(jnp.bfloat16)
        return carry

    lax.fori_loop(0, columns // width, solve, 0)

    def start_copy(step):
        peer = lax.rem(layer + step, layers)
        return remote(
            solved.at[peer], initial_out.at[layer], start_send.at[step - 1],
            start_recv.at[step - 1], "layer", step,
        )

    for step in range(layers - 1, 0, -1):
        start_copy(step).start()
    stores = [
        pltpu.make_async_copy(solved.at[layer], initial_out.at[layer], local_sem.at[0]),
        pltpu.make_async_copy(grads_in, grads_out, local_sem.at[1]),
        pltpu.make_async_copy(solved, solved_out, local_sem.at[2]),
        pltpu.make_async_copy(scales, scales_out, local_sem.at[3]),
        pltpu.make_async_copy(own_scales, own_scales_out, local_sem.at[4]),
    ]
    for store in stores:
        store.start()

    for hop in range(2, groups - 1):
        line.arrive(hop, range(CHUNKS), lift)

    line.arrive(groups - 1, [0], lift)
    for step in range(1, layers):
        start_copy(step).wait_recv()
    stores[0].wait()

    piece_width = columns // PIECES
    begun = initial_out.at[:, :, 0:piece_width]
    first = Line(
        "dp",
        lambda piece: begun,
        lambda block, piece: full_out.at[block],
        first_send,
        first_recv,
        1,
    )

    def rise_copy(source, block):
        return remote(
            source, upper_out.at[block], rise_send.at[block], rise_recv.at[block], "layer", -1
        )

    def rise(block, piece):
        @pl.when(layer > 0)
        def _():
            rise_copy(full_out.at[block], block).start()

    first.begin([0])

    @pl.when(layer > 0)
    def _():
        rise_copy(begun, group).start()

    line.arrive(groups - 1, range(1, CHUNKS), lift)

    tile = 256
    every = count * groups

    def gather(ref, cut):
        return ref[:, :, cut].reshape(every, cut.size)

    own_turned[...] = gather(tokens, own).astype(jnp.float32).T.astype(jnp.bfloat16)

    def refresh_factor(place, carry):
        cut = pl.ds(pl.multiple_of(place * tile, tile), tile)
        value = product(own_turned[...], gather(tokens, cut))
        value = FACTOR_DECAY * factor[:, cut] + fresh_weight * value
        factor[:, cut] = value
        high = value.astype(jnp.bfloat16)
        factor_high[:, cut] = high
        factor_low[:, cut] = (value - high.astype(jnp.float32)).astype(jnp.bfloat16)
        return carry

    tiles = features // tile
    lax.fori_loop(0, tiles // 2, refresh_factor, 0)
    first.arrive(1, [0], rise)
    lax.fori_loop(tiles // 2, tiles, refresh_factor, 0)
    for hop in range(2, groups - 1):
        first.arrive(hop, [0], rise)

    def next_copy(way):
        return remote(
            initial_out.at[:, :, piece_width : 2 * piece_width], next_out.at[way],
            next_send.at[way], next_recv.at[way], "dp", -1 if way else 1,
        )

    for way in (0, 1):

        @pl.when(first.has_next(way))
        def _():
            next_copy(way).start()

    more = [
        pltpu.make_async_copy(factor, factor_out, local_sem.at[10]),
        pltpu.make_async_copy(factor_high, factor_high_out, local_sem.at[5]),
        pltpu.make_async_copy(factor_low, factor_low_out, local_sem.at[6]),
    ]
    for store in more:
        store.start()
    stores += more

    @pl.when(layer < layers - 1)
    def _():
        for step in range(1, groups):
            block = lax.rem(group + step, groups)
            for piece in range(CHUNKS):
                lift_copy(acts.at[span(piece)], block, piece).wait_recv()

    def refresh_cross(place, carry):
        cut = pl.ds(pl.multiple_of(place * tile, tile), tile)
        value = product(own_turned[...], gather(upper, cut))
        value = FACTOR_DECAY * cross[:, cut] + fresh_weight * value
        cross[:, cut] = value
        high = value.astype(jnp.bfloat16)
        cross_high[:, cut] = high
        cross_low[:, cut] = (value - high.astype(jnp.float32)).astype(jnp.bfloat16)
        lent[cut, :] = value.T.astype(jnp.bfloat16)
        return carry

    lax.fori_loop(0, tiles, refresh_cross, 0)
    more = [
        pltpu.make_async_copy(cross, cross_out, local_sem.at[11]),
        pltpu.make_async_copy(cross_high, cross_high_out, local_sem.at[7]),
        pltpu.make_async_copy(cross_low, cross_low_out, local_sem.at[8]),
    ]
    for store in more:
        store.start()
    stores += more

    lent[own, :] = jnp.where(eye, 0.0, lent[own, :].astype(jnp.float32)).astype(jnp.bfloat16)
    last = pltpu.make_async_copy(lent, lent_out, local_sem.at[9])
    last.start()
    stores.append(last)

    first.arrive(groups - 1, [0], rise)

    @pl.when(layer < layers - 1)
    def _():
        for block in range(groups):
            rise_copy(begun, block).wait_recv()

    @pl.when(layer > 0)
    def _():
        for block in range(groups):
            rise_copy(begun, block).wait_send()

    for step in range(1, layers):
        start_copy(step).wait_send()
        grad_copy(step).wait_send()
        scale_copy(step).wait_send()
    for step in range(1, groups):
        sum_copy(step).wait_send()

    @pl.when(layer > 0)
    def _():
        for block in range(groups):
            for piece in range(CHUNKS):
                lift_copy(acts.at[span(piece)], block, piece).wait_send()

    for way in (0, 1):

        @pl.when(first.has_next(way))
        def _():
            next_copy(way).wait_send()

        @pl.when(first.has_block(way, 1))
        def _():
            next_copy(way).wait_recv()

    line.finish()
    first.finish()
    for store in stores[1:]:
        store.wait()


def front(fresh_weight, acts, grads, factor_old, cross_old):
    layers, groups = lax.axis_size("layer"), lax.axis_size("dp")
    rows, features = factor_old.shape
    count = acts.shape[0]
    chunk, columns = grads.shape[1:]
    every = count * groups
    half, full = jnp.bfloat16, jnp.float32
    dma = pltpu.SemaphoreType.DMA
    shape = jax.ShapeDtypeStruct
    return pl.pallas_call(
        functools.partial(front_kernel, fresh_weight),
        out_shape=[shape((rows, features), full)] * 2
        + [shape((rows, features), half)] * 4
        + [shape((features, rows), half)]
        + [shape((layers, chunk, columns), half)]
        + [shape((groups, layers, chunk, columns // PIECES), half)] * 2
        + [shape((2, layers, chunk, columns // PIECES), half)]
        + [shape((layers, chunk, columns), half)] * 2
        + [shape((layers, chunk, 128), full), shape((rows, 128), full)],
        in_specs=[pl.BlockSpec(memory_space=pl.ANY)] * 4,
        out_specs=[pl.BlockSpec(memory_space=pl.ANY)] * 15,
        scratch_shapes=[
            pltpu.VMEM((groups, count, features), half),
            pltpu.VMEM((groups, count, features), half),
            pltpu.VMEM((rows, features), full),
            pltpu.VMEM((rows, features), full),
            pltpu.VMEM((layers, chunk, columns), half),
            pltpu.VMEM((layers, chunk, columns), half),
            pltpu.VMEM((layers, chunk, 256), full),
            pltpu.VMEM((groups, 8, rows), full),
            pltpu.VMEM((groups, 8, rows), full),
            pltpu.VMEM((rows, 128), full),
            pltpu.VMEM((layers, chunk, 128), full),
            pltpu.VMEM((rows, every), half),
        ]
        + [pltpu.VMEM((rows, features), half)] * 4
        + [pltpu.VMEM((features, rows), half)]
        + [dma((2, groups - 1, CHUNKS))] * 2
        + [dma((groups, CHUNKS))] * 2
        + [dma((layers - 1,))] * 2
        + [dma((groups - 1,))] * 2
        + [dma((layers - 1,))] * 4
        + [dma((2, groups - 1, 1))] * 2
        + [dma((groups,))] * 2
        + [dma((2,))] * 2
        + [dma((12,))],
        compiler_params=pltpu.CompilerParams(
            collective_id=0, has_side_effects=True, vmem_limit_bytes=63 << 20
        ),
        cost_estimate=pl.CostEstimate(
            flops=6 * every * rows * features, bytes_accessed=200_000_000, transcendentals=0
        ),
        name="front",
    )(acts, grads, factor_old, cross_old)


PIECES = 4
ORDER = (
    "begin 2 3", "lend 0", "meet 1 2", "carry 1", "away 0", "meet 3",
    "near 0", "lend 1", "carry 2", "multiply 0", "end 1", "multiply 1",
    "carry 3", "away 1", "join 0", "near 1", "lend 2", "correct 0",
    "away 2", "join 1", "end 2", "update 0", "correct 1", "near 2",
    "lend 3", "multiply 2", "first 0", "join 2", "update 1", "middle 0",
    "correct 2", "away 3", "update 2", "end 3", "near 3", "multiply 3",
    "first 1", "join 3", "first 2", "middle 1", "correct 3", "update 3",
    "middle 2", "first 3", "final 3 1 0", "middle 3", "final 2",
)


class Sums:
    def __init__(self, axis, source, target, send_sem, recv_sem):
        self.axis, self.count, self.mine = axis, lax.axis_size(axis), lax.axis_index(axis)
        self.source, self.target = source, target
        self.send_sem, self.recv_sem = send_sem, recv_sem

    def copy(self, way, piece, owner):
        return remote(
            self.source(piece, owner),
            self.target(way, piece, owner),
            self.send_sem.at[way, piece, owner],
            self.recv_sem.at[way, piece, owner],
            self.axis,
            1 if way == 0 else -1,
        )

    def has_before(self, way):
        return self.mine > 0 if way == 0 else self.mine < self.count - 1

    def begin(self, piece, add):
        for way in (0, 1):

            @pl.when(jnp.logical_not(self.has_before(way)))
            def _():
                for distance in range(self.count - 1, 0, -1):
                    place = distance if way == 0 else self.count - 1 - distance
                    add(way, piece, place, False)
                    self.copy(way, piece, place).start()

    def step(self, piece, distance, add):
        for way in (0, 1):
            owner = self.mine + (distance if way == 0 else -distance)

            @pl.when((owner >= 0) & (owner < self.count) & self.has_before(way))
            def _():
                place = jnp.clip(owner, 0, self.count - 1)
                self.copy(way, piece, place).wait_recv()
                add(way, piece, place, True)
                self.copy(way, piece, place).start()

    def close(self, piece):
        for way in (0, 1):

            @pl.when(self.has_before(way))
            def _():
                self.copy(way, piece, self.mine).wait_recv()

    def finish(self, pieces):
        for piece in range(pieces):
            for distance in range(1, self.count):
                for way in (0, 1):
                    owner = self.mine + (distance if way == 0 else -distance)

                    @pl.when((owner >= 0) & (owner < self.count))
                    def _():
                        self.copy(way, piece, jnp.clip(owner, 0, self.count - 1)).wait_send()


def back_kernel(
    exponents,
    factor_high_in, factor_low_in, cross_high_in, cross_low_in, lent_in,
    initial_in, full_in, upper_in, next_in, grads_in, solved_in, scales_in, own_scales_in, moments_in, master_in,
    moments_out, master_out, replicas_out,
    factor_high, factor_low, cross_high, cross_low, lent,
    initial, grads, solved, scales, own_scales, moments, powers, master,
    full, upper, sums, sums_in, away, lowered, away_in, lowered_in, scaled, fixed, fixed_in,
    moments_new, master_new, replicas,
    first_send, first_recv, sum_send, sum_recv, last_send, last_recv, lift_send, lift_recv,
    away_send, away_recv, lowered_send, lowered_recv, fixed_send, fixed_recv, load_sem, store_sem,
):
    layers, groups = lax.axis_size("layer"), lax.axis_size("dp")
    layer, group = lax.axis_index("layer"), lax.axis_index("dp")
    rows, columns = initial.shape
    chunk = rows // layers
    width = columns // PIECES
    features = rows * groups

    def cut(piece):
        return slice(piece * width, (piece + 1) * width)

    pairs = (
        (initial_in, initial),
        (factor_high_in, factor_high),
        (factor_low_in, factor_low),
        (cross_high_in, cross_high),
        (cross_low_in, cross_low),
        (lent_in, lent),
        (own_scales_in, own_scales),
        (grads_in, grads),
        (solved_in, solved),
        (scales_in, scales),
        (moments_in, moments),
        (master_in, master),
    )
    loads = [
        pltpu.make_async_copy(source, target, load_sem.at[place])
        for place, (source, target) in enumerate(pairs)
    ]
    for load in loads:
        load.start()
    greet()

    first = Line(
        "dp",
        lambda piece: initial_in.at[:, cut(piece)],
        lambda block, piece: full.at[piece, block],
        first_send,
        first_recv,
        PIECES,
    )
    last = Line(
        "dp",
        lambda piece: replicas.at[piece],
        lambda block, piece: replicas_out.at[block, :, cut(piece)],
        last_send,
        last_recv,
        PIECES,
    )

    def lift_copy(source, block, piece):
        return remote(
            source, upper.at[piece, block], lift_send.at[piece, block], lift_recv.at[piece, block],
            "layer", -1,
        )

    def lift(block, piece):
        @pl.when(layer > 0)
        def _():
            lift_copy(full.at[piece, block], block, piece).start()

    def next_load(way):
        block = jnp.clip(group + (1 if way else -1), 0, groups - 1)
        return pltpu.make_async_copy(
            next_in.at[way], full.at[1, block], load_sem.at[len(pairs) + groups + way]
        )

    first.given = {1: lambda way: next_load(way).wait()}

    def begin(piece):
        if piece not in first.given:
            first.begin([piece])

        @pl.when(layer > 0)
        def _():
            lift_copy(initial_in.at[:, cut(piece)], group, piece).start()

    begin(1)
    for way in (0, 1):

        @pl.when(first.has_block(way, 1))
        def _():
            next_load(way).start()

    ready = [
        pltpu.make_async_copy(
            full_in.at[lax.rem(group + step, groups)],
            full.at[0, lax.rem(group + step, groups)],
            load_sem.at[len(pairs) + step],
        )
        for step in range(1, groups)
    ]
    ready_upper = pltpu.make_async_copy(upper_in, upper.at[0], load_sem.at[len(pairs)])
    for load in ready:
        load.start()

    @pl.when(layer < layers - 1)
    def _():
        ready_upper.start()

    @pl.when(layer == layers - 1)
    def _():
        upper[...] = jnp.zeros_like(upper)

    loads[0].wait()
    for piece in range(PIECES):
        full[piece, group] = initial[:, cut(piece)]

    def relay_copy(which, piece, step):
        source, target, send_sem, recv_sem = (
            (away, away_in, away_send, away_recv),
            (lowered, lowered_in, lowered_send, lowered_recv),
            (fixed, fixed_in, fixed_send, fixed_recv),
        )[which]
        peer = lax.rem(layer + step, layers)
        return remote(
            source.at[piece, peer], target.at[piece, layer],
            send_sem.at[step - 1, piece], recv_sem.at[step - 1, piece], "layer", step,
        )

    def multiply(piece):
        @pl.when(layer < layers - 1)
        def _():
            if piece == 0:
                ready_upper.wait()
            else:
                for block in range(groups):
                    lift_copy(full.at[piece, block], block, piece).wait_recv()

        def some(place, carry):
            part = pl.ds(pl.multiple_of(place * chunk * 2, chunk * 2), chunk * 2)
            mine = full[piece].reshape(features, width)
            theirs = upper[piece].reshape(features, width)
            value = product(factor_high[part, :], mine) + product(factor_low[part, :], mine)
            value = value - own_scales[part, 2:3] * full[piece, group, part, :].astype(jnp.float32)
            value = value + product(cross_high[part, :], theirs) + product(cross_low[part, :], theirs)
            value = value - own_scales[part, 1:2] * upper[piece, group, part, :].astype(jnp.float32)
            for side in range(2):
                inner = slice(side * chunk, (side + 1) * chunk)
                away[piece, 2 * place + side] = value[inner].astype(jnp.bfloat16)
            return carry

        lax.fori_loop(0, layers // 2, some, 0)
        for step in range(layers - 1, 0, -1):
            relay_copy(0, piece, step).start()
        away_in[piece, layer] = away[piece, layer]

    def block_of(place):
        return pl.ds(pl.multiple_of(place * rows, rows), rows)

    def add(way, piece, place, more):
        value = product(lent[block_of(place), :], initial[:, cut(piece)])
        if more:
            value = value + sums_in[way, piece, place].astype(jnp.float32)
        sums[piece, place] = value.astype(jnp.bfloat16)

    lower = Sums(
        "dp",
        lambda piece, owner: sums.at[piece, owner],
        lambda way, piece, owner: sums_in.at[way, piece, owner],
        sum_send,
        sum_recv,
    )

    def join(piece):
        lower.close(piece)
        value = product(lent[block_of(group), :], initial[:, cut(piece)])
        for way in (0, 1):
            value = value + sums_in[way, piece, group].astype(jnp.float32)
        for place in range(layers):
            part = value[place * chunk : (place + 1) * chunk]
            lowered[piece, place] = part.astype(jnp.bfloat16)
        for step in range(layers - 1, 0, -1):
            relay_copy(1, piece, step).start()
        lowered_in[piece, layer] = lowered[piece, layer]

    def correct(piece):
        for step in range(layers - 1, 0, -1):
            relay_copy(0, piece, step).wait_recv()
            relay_copy(1, piece, step).wait_recv()
        part = cut(piece)

        def wide(ref, place):
            return ref[place, :, part].astype(jnp.float32)

        passed = None
        for place in range(layers):
            target = wide(grads, place) - scales[place, :, 0:1] * wide(solved, place)
            if place < layers - 1:
                target = target - scales[place, :, 1:2] * wide(solved, place + 1)
            target = target - away_in[piece, place].astype(jnp.float32)
            if place:
                target = target - scales[place - 1, :, 1:2] * wide(solved, place - 1)
                target = target - lowered_in[piece, place - 1].astype(jnp.float32)
                target = target - passed
            value = target / scales[place, :, 0:1]
            scaled[place] = value
            passed = scales[place, :, 1:2] * value
        result = value
        fixed[piece, layers - 1] = result.astype(jnp.bfloat16)
        for place in range(layers - 2, -1, -1):
            ratio = scales[place, :, 1:2] / scales[place, :, 0:1]
            result = scaled[place] - ratio * result
            fixed[piece, place] = result.astype(jnp.bfloat16)
        for step in range(layers - 1, 0, -1):
            relay_copy(2, piece, step).start()
        fixed_in[piece, layer] = fixed[piece, layer]

    stores = []

    def update(piece):
        for step in range(layers - 1, 0, -1):
            relay_copy(2, piece, step).wait_recv()
        part = cut(piece)

        def some(place, carry):
            inner = pl.ds(pl.multiple_of(place * chunk, chunk), chunk)
            change = initial[inner, part].astype(jnp.float32) + fixed_in[piece, place].astype(
                jnp.float32
            )
            moment = MOMENTUM * moments[inner, part].astype(jnp.float32) * powers[inner, 0:1]
            moment = moment + (1.0 - MOMENTUM) * change
            moments_new[inner, part] = (moment * powers[inner, 1:2]).astype(jnp.bfloat16)
            weights = master[inner, part] - STEP_SIZE * moment
            master_new[inner, part] = weights
            replicas[piece, inner, :] = weights.astype(jnp.bfloat16)
            return carry

        lax.fori_loop(0, layers, some, 0)
        last.begin([piece])
        for place, (source, target) in enumerate(
            (
                (replicas.at[piece], replicas_out.at[group, :, part]),
                (master_new.at[:, part], master_out.at[:, part]),
                (moments_new.at[:, part], moments_out.at[:, part]),
            )
        ):
            stores.append(pltpu.make_async_copy(source, target, store_sem.at[place, piece]))
            stores[-1].start()

    far = groups - 1
    lane = lax.broadcasted_iota(jnp.int32, (SCALE_BLOCK, 128), 1)
    for place in range(rows // SCALE_BLOCK):
        power = jnp.full((SCALE_BLOCK, 128), exponents[0, place].astype(jnp.float32))
        powers[place * SCALE_BLOCK : (place + 1) * SCALE_BLOCK, :] = jnp.exp2(
            jnp.where(lane == 0, power, -power)
        )
    for way, end in ((0, 0), (1, groups - 1)):

        @pl.when(group == end)
        def _():
            for piece in range(PIECES):
                sums_in[way, piece, end] = jnp.zeros_like(sums_in[way, piece, end])

    for load in loads[1:] + ready:
        load.wait()
    tasks = dict(
        begin=begin,
        meet=lambda piece: first.arrive(1, [piece], lift),
        carry=lambda piece: [first.arrive(hop, [piece], lift) for hop in range(2, far)],
        end=lambda piece: first.arrive(far, [piece], lift),
        lend=lambda piece: lower.begin(piece, add),
        away=lambda piece: [lower.step(piece, distance, add) for distance in range(far - 1, 1, -1)],
        near=lambda piece: lower.step(piece, 1, add),
        multiply=multiply,
        join=join,
        correct=correct,
        update=update,
        first=lambda piece: last.arrive(1, [piece]),
        middle=lambda piece: [last.arrive(hop, [piece]) for hop in range(2, far)],
        final=lambda piece: last.arrive(far, [piece]),
    )
    for entry in ORDER:
        name, *pieces = entry.split()
        for piece in pieces:
            tasks[name](int(piece))

    for piece in range(PIECES):
        for step in range(1, layers):
            for which in range(3):
                relay_copy(which, piece, step).wait_send()

        if piece:

            @pl.when(layer > 0)
            def _():
                for block in range(groups):
                    lift_copy(full.at[piece, block], block, piece).wait_send()

    first.finish(range(1, PIECES))
    lower.finish(PIECES)
    last.finish()
    for store in stores:
        store.wait()


def back(exponents, matrices, initial, full_first, upper_first, next_first, grads, solved, scales, own_scales, moments, master):
    layers, groups = lax.axis_size("layer"), lax.axis_size("dp")
    rows, columns = initial.shape
    features = matrices[0].shape[1]
    chunk, width = rows // layers, columns // PIECES
    half, full = jnp.bfloat16, jnp.float32
    dma = pltpu.SemaphoreType.DMA
    shape = jax.ShapeDtypeStruct
    swapped = pltpu.VMEM((PIECES, layers, chunk, width), half)
    return pl.pallas_call(
        back_kernel,
        out_shape=[
            shape((rows, columns), half),
            shape((rows, columns), full),
            shape((groups, rows, columns), half),
        ],
        in_specs=[pl.BlockSpec(memory_space=pltpu.SMEM)]
        + [pl.BlockSpec(memory_space=pl.ANY)] * 15,
        out_specs=[pl.BlockSpec(memory_space=pl.ANY)] * 3,
        scratch_shapes=[pltpu.VMEM((rows, features), half)] * 4
        + [pltpu.VMEM((features, rows), half)]
        + [
            pltpu.VMEM((rows, columns), half),
            pltpu.VMEM((layers, chunk, columns), half),
            pltpu.VMEM((layers, chunk, columns), half),
            pltpu.VMEM((layers, chunk, 128), full),
            pltpu.VMEM((rows, 128), full),
            pltpu.VMEM((rows, columns), half),
            pltpu.VMEM((rows, 128), full),
            pltpu.VMEM((rows, columns), full),
            pltpu.VMEM((PIECES, groups, rows, width), half),
            pltpu.VMEM((PIECES, groups, rows, width), half),
            pltpu.VMEM((PIECES, groups, rows, width), half),
            pltpu.VMEM((2, PIECES, groups, rows, width), half),
        ]
        + [swapped] * 4
        + [pltpu.VMEM((layers, chunk, width), full)]
        + [swapped] * 2
        + [
            pltpu.VMEM((rows, columns), half),
            pltpu.VMEM((rows, columns), full),
            pltpu.VMEM((PIECES, rows, width), half),
        ]
        + [dma((2, groups - 1, PIECES))] * 2
        + [dma((2, PIECES, groups))] * 2
        + [dma((2, groups - 1, PIECES))] * 2
        + [dma((PIECES, groups))] * 2
        + [dma((layers - 1, PIECES))] * 6
        + [dma((14 + groups,)), dma((3, PIECES))],
        compiler_params=pltpu.CompilerParams(
            collective_id=1, has_side_effects=True, vmem_limit_bytes=58 << 20
        ),
        cost_estimate=pl.CostEstimate(
            flops=10 * features * rows * columns, bytes_accessed=300_000_000, transcendentals=0
        ),
        name="back",
    )(
        exponents, *matrices, initial, full_first, upper_first, next_first, grads, solved, scales, own_scales,
        moments, master,
    )


def body(activations, factor_old, cross_old, gradients, moments, exponents, master):
    layers, groups = lax.axis_size("layer"), lax.axis_size("dp")
    row_count, features = factor_old.shape[1:]
    columns = gradients.shape[2]
    chunk = row_count // layers
    fresh_weight = (1.0 - FACTOR_DECAY) / (activations.shape[1] * groups)
    factor_new, cross_new, *rest = front(
        fresh_weight,
        activations[0],
        gradients[0].reshape(layers, chunk, columns),
        factor_old[0],
        cross_old[0],
    )
    *matrices, initial, full_first, upper_first, next_first, grad_swapped, initial_swapped, scales, own_scales = rest
    moments_new, master_new, replicas = back(
        exponents,
        matrices,
        initial.reshape(row_count, columns),
        full_first.reshape(groups, row_count, -1),
        upper_first.reshape(groups, row_count, -1),
        next_first.reshape(2, row_count, -1),
        grad_swapped,
        initial_swapped,
        scales,
        own_scales,
        moments[0],
        master[0],
    )
    replicas = replicas.reshape(features, columns)
    return (factor_new[None], cross_new[None], moments_new[None], master_new[None], replicas[None])


def solution(mesh):
    return jax.shard_map(
        body,
        mesh=mesh,
        in_specs=(
            P("layer", "dp", None),
            P("layer", "dp", None),
            P("layer", "dp", None),
            P("layer", "dp", None),
            P("layer", "dp", None),
            P("layer", "dp"),
            P("layer", "dp", None),
        ),
        out_specs=(
            P("layer", "dp", None),
            P("layer", "dp", None),
            P("layer", "dp", None),
            P("layer", "dp", None),
            P("layer", None, None),
        ),
        check_vma=False,
    )
```

```python
import functools

import jax
import jax.numpy as jnp
from jax import lax
from jax.experimental import pallas as pl
from jax.experimental.pallas import tpu as pltpu
from jax.sharding import PartitionSpec as P

SCALE_BLOCK = 128


FACTOR_DECAY = 0.9
DAMPING = 0.5
MOMENTUM = 0.8
STEP_SIZE = 0.05

MESH = pl.DeviceIdType.MESH


def product(left, right):
    return jnp.dot(left, right, preferred_element_type=jnp.float32)


CHUNKS = 4


def column_of(row, eye):
    return jnp.sum(jnp.where(eye, jnp.broadcast_to(row, eye.shape), 0.0), axis=1, keepdims=True)


def identity(size):
    return lax.broadcasted_iota(jnp.int32, (size, size), 0) == lax.broadcasted_iota(
        jnp.int32, (size, size), 1
    )


def greet():
    barrier = pltpu.get_barrier_semaphore()
    total = 0
    for axis in ("layer", "dp"):
        count, mine = lax.axis_size(axis), lax.axis_index(axis)
        for step in range(1, count):
            pl.semaphore_signal(
                barrier, inc=1, device_id={axis: lax.rem(mine + step, count)}, device_id_type=MESH
            )
        total += count - 1
    pl.semaphore_wait(barrier, total)


def remote(source, target, send_sem, recv_sem, axis, step):
    count, mine = lax.axis_size(axis), lax.axis_index(axis)
    return pltpu.make_async_remote_copy(
        src_ref=source,
        dst_ref=target,
        send_sem=send_sem,
        recv_sem=recv_sem,
        device_id={axis: lax.rem(mine + step + count, count)},
        device_id_type=MESH,
    )


class Line:
    def __init__(self, axis, source, target, send_sem, recv_sem, pieces):
        self.axis, self.count, self.mine = axis, lax.axis_size(axis), lax.axis_index(axis)
        self.source, self.target, self.pieces = source, target, pieces
        self.send_sem, self.recv_sem = send_sem, recv_sem
        self.given = {}

    def copy(self, way, hop, piece):
        sign = 1 if way == 0 else -1
        block = jnp.clip(self.mine - sign * hop, 0, self.count - 1)
        landing = self.target(block, piece)
        return remote(
            self.source(piece) if hop == 0 else landing,
            landing,
            self.send_sem.at[way, hop, piece],
            self.recv_sem.at[way, hop, piece],
            self.axis,
            sign,
        )

    def has_next(self, way):
        return self.mine < self.count - 1 if way == 0 else self.mine > 0

    def has_block(self, way, hop):
        return self.mine >= hop if way == 0 else self.mine + hop <= self.count - 1

    def begin(self, pieces):
        for piece in pieces:
            for way in (0, 1):

                @pl.when(self.has_next(way))
                def _():
                    self.copy(way, 0, piece).start()

    def arrive(self, hop, pieces, then=None):
        for piece in pieces:
            for way in (0, 1):

                @pl.when(self.has_block(way, hop))
                def _():
                    if hop == 1 and piece in self.given:
                        self.given[piece](way)
                    else:
                        self.copy(way, hop - 1, piece).wait_recv()
                    if hop < self.count - 1:

                        @pl.when(self.has_next(way))
                        def _():
                            self.copy(way, hop, piece).start()

                    if then is not None:
                        sign = 1 if way == 0 else -1
                        then(jnp.clip(self.mine - sign * hop, 0, self.count - 1), piece)

    def finish(self, pieces=None):
        for hop in range(self.count - 1):
            for piece in pieces or range(self.pieces):
                if hop == 0 and piece in self.given:
                    continue
                for way in (0, 1):

                    @pl.when(self.has_next(way) & self.has_block(way, hop))
                    def _():
                        self.copy(way, hop, piece).wait_send()


def front_kernel(
    fresh_weight,
    acts, grads, factor_old, cross_old,
    factor_out, cross_out, factor_high_out, factor_low_out, cross_high_out, cross_low_out, lent_out,
    initial_out, full_out, upper_out, next_out, grads_out, solved_out, scales_out, own_scales_out,
    tokens, upper, factor, cross, grads_in, solved, scaled,
    sums_away, sums_in, own_scales, scales, own_turned,
    factor_high, factor_low, cross_high, cross_low, lent,
    line_send, line_recv, lift_send, lift_recv, grad_send, grad_recv, sum_send, sum_recv,
    scale_send, scale_recv, start_send, start_recv, first_send, first_recv, rise_send, rise_recv, next_send, next_recv, local_sem,
):
    layers, groups = lax.axis_size("layer"), lax.axis_size("dp")
    layer, group = lax.axis_index("layer"), lax.axis_index("dp")
    rows, features = factor.shape
    count = acts.shape[0]
    part = count // CHUNKS
    chunk = rows // layers
    columns = grads.shape[2]
    own = pl.ds(pl.multiple_of(group * rows, rows), rows)

    def span(piece):
        return pl.ds(piece * part, part)

    load_acts = pltpu.make_async_copy(acts, tokens.at[group], local_sem.at[0])
    load_factor = pltpu.make_async_copy(factor_old, factor, local_sem.at[1])
    load_cross = pltpu.make_async_copy(cross_old, cross, local_sem.at[2])
    load_grads = pltpu.make_async_copy(grads.at[layer], grads_in.at[layer], local_sem.at[3])
    load_acts.start()
    load_cross.start()
    load_factor.start()
    load_grads.start()
    greet()

    line = Line(
        "dp",
        lambda piece: acts.at[span(piece)],
        lambda block, piece: tokens.at[block, span(piece)],
        line_send,
        line_recv,
        CHUNKS,
    )

    def lift_copy(source, block, piece):
        return remote(
            source,
            upper.at[block, span(piece)],
            lift_send.at[block, piece],
            lift_recv.at[block, piece],
            "layer",
            -1,
        )

    def lift(block, piece):
        @pl.when(layer > 0)
        def _():
            lift_copy(tokens.at[block, span(piece)], block, piece).start()

    @pl.when(layer > 0)
    def _():
        for piece in range(CHUNKS):
            lift_copy(acts.at[span(piece)], group, piece).start()

    def grad_copy(step):
        peer = lax.rem(layer + step, layers)
        return remote(
            grads.at[peer], grads_in.at[layer], grad_send.at[step - 1], grad_recv.at[step - 1],
            "layer", step,
        )

    for step in range(layers - 1, 0, -1):
        grad_copy(step).start()
    line.begin(range(CHUNKS // 2))

    load_acts.wait()
    sums_away[...] = jnp.zeros_like(sums_away)
    for place in range(groups):
        wide = tokens[group, :, place * rows : (place + 1) * rows].astype(jnp.float32)
        sums_away[place, 0:1, :] = jnp.sum(wide * wide, axis=0, keepdims=True)
    load_cross.wait()
    load_factor.wait()
    eye = identity(rows)
    factor_diagonal = jnp.sum(jnp.where(eye, factor[:, own], 0.0), axis=1, keepdims=True)
    cross_diagonal = jnp.sum(jnp.where(eye, cross[:, own], 0.0), axis=1, keepdims=True)

    @pl.when(layer < layers - 1)
    def _():
        for piece in range(CHUNKS):
            lift_copy(acts.at[span(piece)], group, piece).wait_recv()
        for place in range(groups):
            cut = slice(place * rows, (place + 1) * rows)
            wide = tokens[group, :, cut].astype(jnp.float32)
            above = upper[group, :, cut].astype(jnp.float32)
            sums_away[place, 1:2, :] = jnp.sum(wide * above, axis=0, keepdims=True)

    @pl.when(layer == layers - 1)
    def _():
        upper[...] = jnp.zeros_like(upper)

    def sum_copy(step):
        peer = lax.rem(group + step, groups)
        return remote(
            sums_away.at[peer], sums_in.at[group], sum_send.at[step - 1], sum_recv.at[step - 1],
            "dp", step,
        )

    for step in range(groups - 1, 0, -1):
        sum_copy(step).start()
    line.begin(range(CHUNKS // 2, CHUNKS))
    sums_in[group] = sums_away[group]
    line.arrive(1, range(CHUNKS // 2))

    for step in range(groups - 1, 0, -1):
        sum_copy(step).wait_recv()
    sums = fresh_weight * jnp.sum(sums_in[...], axis=0)
    own_sum = column_of(sums[0:1], eye)
    next_sum = column_of(sums[1:2], eye)
    own_diagonal = FACTOR_DECAY * factor_diagonal + own_sum
    own_coupling = FACTOR_DECAY * cross_diagonal + next_sum
    lane = lax.broadcasted_iota(jnp.int32, (rows, 128), 1)
    own_scales[...] = jnp.where(
        lane == 0,
        DAMPING + own_diagonal,
        jnp.where(lane == 1, own_coupling, jnp.where(lane == 2, own_diagonal, next_sum)),
    )

    def scale_copy(step):
        peer = lax.rem(layer + step, layers)
        return remote(
            own_scales.at[pl.ds(pl.multiple_of(peer * chunk, chunk), chunk)],
            scales.at[layer], scale_send.at[step - 1], scale_recv.at[step - 1], "layer", step,
        )

    for step in range(layers - 1, 0, -1):
        scale_copy(step).start()
    scales[layer] = own_scales[pl.ds(pl.multiple_of(layer * chunk, chunk), chunk), :]
    line.arrive(1, range(CHUNKS // 2, CHUNKS))
    for way in (0, 1):

        @pl.when(line.has_block(way, 1))
        def _():
            for piece in range(CHUNKS):
                lift(jnp.clip(group - (1 if way == 0 else -1), 0, groups - 1), piece)

    load_grads.wait()
    for step in range(layers - 1, 0, -1):
        scale_copy(step).wait_recv()
        grad_copy(step).wait_recv()

    width = scaled.shape[2]

    def solve(tile, carry):
        cut = pl.ds(pl.multiple_of(tile * width, width), width)
        passed = None
        for place in range(layers):
            target = grads_in[place, :, cut].astype(jnp.float32)
            if place:
                target = target - passed
            value = target / scales[place, :, 0:1]
            scaled[place] = value
            passed = scales[place, :, 1:2] * value
        result = value
        solved[layers - 1, :, cut] = result.astype(jnp.bfloat16)
        for place in range(layers - 2, -1, -1):
            ratio = scales[place, :, 1:2] / scales[place, :, 0:1]
            result = scaled[place] - ratio * result
            solved[place, :, cut] = result.astype(jnp.bfloat16)
        return carry

    lax.fori_loop(0, columns // width, solve, 0)

    def start_copy(step):
        peer = lax.rem(layer + step, layers)
        return remote(
            solved.at[peer], initial_out.at[layer], start_send.at[step - 1],
            start_recv.at[step - 1], "layer", step,
        )

    for step in range(layers - 1, 0, -1):
        start_copy(step).start()
    stores = [
        pltpu.make_async_copy(solved.at[layer], initial_out.at[layer], local_sem.at[0]),
        pltpu.make_async_copy(grads_in, grads_out, local_sem.at[1]),
        pltpu.make_async_copy(solved, solved_out, local_sem.at[2]),
        pltpu.make_async_copy(scales, scales_out, local_sem.at[3]),
        pltpu.make_async_copy(own_scales, own_scales_out, local_sem.at[4]),
    ]
    for store in stores:
        store.start()

    for hop in range(2, groups - 1):
        line.arrive(hop, range(CHUNKS), lift)

    line.arrive(groups - 1, [0], lift)
    for step in range(1, layers):
        start_copy(step).wait_recv()
    stores[0].wait()

    piece_width = columns // PIECES
    begun = initial_out.at[:, :, 0:piece_width]
    first = Line(
        "dp",
        lambda piece: begun,
        lambda block, piece: full_out.at[block],
        first_send,
        first_recv,
        1,
    )

    def rise_copy(source, block):
        return remote(
            source, upper_out.at[block], rise_send.at[block], rise_recv.at[block], "layer", -1
        )

    def rise(block, piece):
        @pl.when(layer > 0)
        def _():
            rise_copy(full_out.at[block], block).start()

    first.begin([0])

    @pl.when(layer > 0)
    def _():
        rise_copy(begun, group).start()

    line.arrive(groups - 1, range(1, CHUNKS), lift)

    tile = 256
    every = count * groups

    def gather(ref, cut):
        return ref[:, :, cut].reshape(every, cut.size)

    own_turned[...] = gather(tokens, own).astype(jnp.float32).T.astype(jnp.bfloat16)

    def refresh_factor(place, carry):
        cut = pl.ds(pl.multiple_of(place * tile, tile), tile)
        value = product(own_turned[...], gather(tokens, cut))
        value = FACTOR_DECAY * factor[:, cut] + fresh_weight * value
        factor[:, cut] = value
        high = value.astype(jnp.bfloat16)
        factor_high[:, cut] = high
        factor_low[:, cut] = (value - high.astype(jnp.float32)).astype(jnp.bfloat16)
        return carry

    tiles = features // tile
    lax.fori_loop(0, tiles // 2, refresh_factor, 0)
    first.arrive(1, [0], rise)
    lax.fori_loop(tiles // 2, tiles, refresh_factor, 0)
    for hop in range(2, groups - 1):
        first.arrive(hop, [0], rise)

    def next_copy(way):
        return remote(
            initial_out.at[:, :, piece_width : 2 * piece_width], next_out.at[way],
            next_send.at[way], next_recv.at[way], "dp", -1 if way else 1,
        )

    for way in (0, 1):

        @pl.when(first.has_next(way))
        def _():
            next_copy(way).start()

    more = [
        pltpu.make_async_copy(factor, factor_out, local_sem.at[10]),
        pltpu.make_async_copy(factor_high, factor_high_out, local_sem.at[5]),
        pltpu.make_async_copy(factor_low, factor_low_out, local_sem.at[6]),
    ]
    for store in more:
        store.start()
    stores += more

    @pl.when(layer < layers - 1)
    def _():
        for step in range(1, groups):
            block = lax.rem(group + step, groups)
            for piece in range(CHUNKS):
                lift_copy(acts.at[span(piece)], block, piece).wait_recv()

    def refresh_cross(place, carry):
        cut = pl.ds(pl.multiple_of(place * tile, tile), tile)
        value = product(own_turned[...], gather(upper, cut))
        value = FACTOR_DECAY * cross[:, cut] + fresh_weight * value
        cross[:, cut] = value
        high = value.astype(jnp.bfloat16)
        cross_high[:, cut] = high
        cross_low[:, cut] = (value - high.astype(jnp.float32)).astype(jnp.bfloat16)
        lent[cut, :] = value.T.astype(jnp.bfloat16)
        return carry

    lax.fori_loop(0, tiles, refresh_cross, 0)
    more = [
        pltpu.make_async_copy(cross, cross_out, local_sem.at[11]),
        pltpu.make_async_copy(cross_high, cross_high_out, local_sem.at[7]),
        pltpu.make_async_copy(cross_low, cross_low_out, local_sem.at[8]),
    ]
    for store in more:
        store.start()
    stores += more

    lent[own, :] = jnp.where(eye, 0.0, lent[own, :].astype(jnp.float32)).astype(jnp.bfloat16)
    last = pltpu.make_async_copy(lent, lent_out, local_sem.at[9])
    last.start()
    stores.append(last)

    first.arrive(groups - 1, [0], rise)

    @pl.when(layer < layers - 1)
    def _():
        for block in range(groups):
            rise_copy(begun, block).wait_recv()

    @pl.when(layer > 0)
    def _():
        for block in range(groups):
            rise_copy(begun, block).wait_send()

    for step in range(1, layers):
        start_copy(step).wait_send()
        grad_copy(step).wait_send()
        scale_copy(step).wait_send()
    for step in range(1, groups):
        sum_copy(step).wait_send()

    @pl.when(layer > 0)
    def _():
        for block in range(groups):
            for piece in range(CHUNKS):
                lift_copy(acts.at[span(piece)], block, piece).wait_send()

    for way in (0, 1):

        @pl.when(first.has_next(way))
        def _():
            next_copy(way).wait_send()

        @pl.when(first.has_block(way, 1))
        def _():
            next_copy(way).wait_recv()

    line.finish()
    first.finish()
    for store in stores[1:]:
        store.wait()


def front(fresh_weight, acts, grads, factor_old, cross_old):
    layers, groups = lax.axis_size("layer"), lax.axis_size("dp")
    rows, features = factor_old.shape
    count = acts.shape[0]
    chunk, columns = grads.shape[1:]
    every = count * groups
    half, full = jnp.bfloat16, jnp.float32
    dma = pltpu.SemaphoreType.DMA
    shape = jax.ShapeDtypeStruct
    return pl.pallas_call(
        functools.partial(front_kernel, fresh_weight),
        out_shape=[shape((rows, features), full)] * 2
        + [shape((rows, features), half)] * 4
        + [shape((features, rows), half)]
        + [shape((layers, chunk, columns), half)]
        + [shape((groups, layers, chunk, columns // PIECES), half)] * 2
        + [shape((2, layers, chunk, columns // PIECES), half)]
        + [shape((layers, chunk, columns), half)] * 2
        + [shape((layers, chunk, 128), full), shape((rows, 128), full)],
        in_specs=[pl.BlockSpec(memory_space=pl.ANY)] * 4,
        out_specs=[pl.BlockSpec(memory_space=pl.ANY)] * 15,
        scratch_shapes=[
            pltpu.VMEM((groups, count, features), half),
            pltpu.VMEM((groups, count, features), half),
            pltpu.VMEM((rows, features), full),
            pltpu.VMEM((rows, features), full),
            pltpu.VMEM((layers, chunk, columns), half),
            pltpu.VMEM((layers, chunk, columns), half),
            pltpu.VMEM((layers, chunk, 256), full),
            pltpu.VMEM((groups, 8, rows), full),
            pltpu.VMEM((groups, 8, rows), full),
            pltpu.VMEM((rows, 128), full),
            pltpu.VMEM((layers, chunk, 128), full),
            pltpu.VMEM((rows, every), half),
        ]
        + [pltpu.VMEM((rows, features), half)] * 4
        + [pltpu.VMEM((features, rows), half)]
        + [dma((2, groups - 1, CHUNKS))] * 2
        + [dma((groups, CHUNKS))] * 2
        + [dma((layers - 1,))] * 2
        + [dma((groups - 1,))] * 2
        + [dma((layers - 1,))] * 4
        + [dma((2, groups - 1, 1))] * 2
        + [dma((groups,))] * 2
        + [dma((2,))] * 2
        + [dma((12,))],
        compiler_params=pltpu.CompilerParams(
            collective_id=0, has_side_effects=True, vmem_limit_bytes=63 << 20
        ),
        cost_estimate=pl.CostEstimate(
            flops=6 * every * rows * features, bytes_accessed=200_000_000, transcendentals=0
        ),
        name="front",
    )(acts, grads, factor_old, cross_old)


PIECES = 4
ORDER = (
    "begin 2 3", "lend 0", "meet 1 2", "carry 1", "away 0", "meet 3",
    "near 0", "lend 1", "carry 2", "multiply 0", "end 1", "multiply 1",
    "carry 3", "away 1", "join 0", "near 1", "lend 2", "correct 0",
    "away 2", "join 1", "end 2", "update 0", "correct 1", "near 2",
    "lend 3", "multiply 2", "first 0", "join 2", "update 1", "middle 0",
    "correct 2", "away 3", "update 2", "end 3", "near 3", "multiply 3",
    "first 1", "join 3", "first 2", "middle 1", "correct 3", "update 3",
    "middle 2", "first 3", "final 3 1 0", "middle 3", "final 2",
)


class Sums:
    def __init__(self, axis, source, target, send_sem, recv_sem):
        self.axis, self.count, self.mine = axis, lax.axis_size(axis), lax.axis_index(axis)
        self.source, self.target = source, target
        self.send_sem, self.recv_sem = send_sem, recv_sem

    def copy(self, way, piece, owner):
        return remote(
            self.source(piece, owner),
            self.target(way, piece, owner),
            self.send_sem.at[way, piece, owner],
            self.recv_sem.at[way, piece, owner],
            self.axis,
            1 if way == 0 else -1,
        )

    def has_before(self, way):
        return self.mine > 0 if way == 0 else self.mine < self.count - 1

    def begin(self, piece, add):
        for way in (0, 1):

            @pl.when(jnp.logical_not(self.has_before(way)))
            def _():
                for distance in range(self.count - 1, 0, -1):
                    place = distance if way == 0 else self.count - 1 - distance
                    add(way, piece, place, False)
                    self.copy(way, piece, place).start()

    def step(self, piece, distance, add):
        for way in (0, 1):
            owner = self.mine + (distance if way == 0 else -distance)

            @pl.when((owner >= 0) & (owner < self.count) & self.has_before(way))
            def _():
                place = jnp.clip(owner, 0, self.count - 1)
                self.copy(way, piece, place).wait_recv()
                add(way, piece, place, True)
                self.copy(way, piece, place).start()

    def close(self, piece):
        for way in (0, 1):

            @pl.when(self.has_before(way))
            def _():
                self.copy(way, piece, self.mine).wait_recv()

    def finish(self, pieces):
        for piece in range(pieces):
            for distance in range(1, self.count):
                for way in (0, 1):
                    owner = self.mine + (distance if way == 0 else -distance)

                    @pl.when((owner >= 0) & (owner < self.count))
                    def _():
                        self.copy(way, piece, jnp.clip(owner, 0, self.count - 1)).wait_send()


def back_kernel(
    exponents,
    factor_high_in, factor_low_in, cross_high_in, cross_low_in, lent_in,
    initial_in, full_in, upper_in, next_in, grads_in, solved_in, scales_in, own_scales_in, moments_in, master_in,
    moments_out, master_out, replicas_out,
    factor_high, factor_low, cross_high, cross_low, lent,
    initial, grads, solved, scales, own_scales, moments, powers, master,
    full, upper, sums, sums_in, away, lowered, away_in, lowered_in, scaled, fixed, fixed_in,
    moments_new, master_new, replicas,
    first_send, first_recv, sum_send, sum_recv, last_send, last_recv, lift_send, lift_recv,
    away_send, away_recv, lowered_send, lowered_recv, fixed_send, fixed_recv, load_sem, store_sem,
):
    layers, groups = lax.axis_size("layer"), lax.axis_size("dp")
    layer, group = lax.axis_index("layer"), lax.axis_index("dp")
    rows, columns = initial.shape
    chunk = rows // layers
    width = columns // PIECES
    features = rows * groups

    def cut(piece):
        return slice(piece * width, (piece + 1) * width)

    pairs = (
        (initial_in, initial),
        (factor_high_in, factor_high),
        (factor_low_in, factor_low),
        (cross_high_in, cross_high),
        (cross_low_in, cross_low),
        (lent_in, lent),
        (own_scales_in, own_scales),
        (grads_in, grads),
        (solved_in, solved),
        (scales_in, scales),
        (moments_in, moments),
        (master_in, master),
    )
    loads = [
        pltpu.make_async_copy(source, target, load_sem.at[place])
        for place, (source, target) in enumerate(pairs)
    ]
    for load in loads[:7]:
        load.start()
    greet()

    first = Line(
        "dp",
        lambda piece: initial_in.at[:, cut(piece)],
        lambda block, piece: full.at[piece, block],
        first_send,
        first_recv,
        PIECES,
    )
    last = Line(
        "dp",
        lambda piece: replicas.at[piece],
        lambda block, piece: replicas_out.at[block, :, cut(piece)],
        last_send,
        last_recv,
        PIECES,
    )

    def lift_copy(source, block, piece):
        return remote(
            source, upper.at[piece, block], lift_send.at[piece, block], lift_recv.at[piece, block],
            "layer", -1,
        )

    def lift(block, piece):
        @pl.when(layer > 0)
        def _():
            lift_copy(full.at[piece, block], block, piece).start()

    def next_load(way):
        block = jnp.clip(group + (1 if way else -1), 0, groups - 1)
        return pltpu.make_async_copy(
            next_in.at[way], full.at[1, block], load_sem.at[len(pairs) + groups + way]
        )

    first.given = {1: lambda way: next_load(way).wait()}

    def begin(piece):
        if piece not in first.given:
            first.begin([piece])

        @pl.when(layer > 0)
        def _():
            lift_copy(initial_in.at[:, cut(piece)], group, piece).start()

    begin(1)
    for way in (0, 1):

        @pl.when(first.has_block(way, 1))
        def _():
            next_load(way).start()

    ready = [
        pltpu.make_async_copy(
            full_in.at[lax.rem(group + step, groups)],
            full.at[0, lax.rem(group + step, groups)],
            load_sem.at[len(pairs) + step],
        )
        for step in range(1, groups)
    ]
    ready_upper = pltpu.make_async_copy(upper_in, upper.at[0], load_sem.at[len(pairs)])
    for load in ready + loads[7:]:
        load.start()

    @pl.when(layer < layers - 1)
    def _():
        ready_upper.start()

    @pl.when(layer == layers - 1)
    def _():
        upper[...] = jnp.zeros_like(upper)

    loads[0].wait()
    for piece in range(PIECES):
        full[piece, group] = initial[:, cut(piece)]

    def relay_copy(which, piece, step):
        source, target, send_sem, recv_sem = (
            (away, away_in, away_send, away_recv),
            (lowered, lowered_in, lowered_send, lowered_recv),
            (fixed, fixed_in, fixed_send, fixed_recv),
        )[which]
        peer = lax.rem(layer + step, layers)
        return remote(
            source.at[piece, peer], target.at[piece, layer],
            send_sem.at[step - 1, piece], recv_sem.at[step - 1, piece], "layer", step,
        )

    def multiply(piece):
        @pl.when(layer < layers - 1)
        def _():
            if piece == 0:
                ready_upper.wait()
            else:
                for block in range(groups):
                    lift_copy(full.at[piece, block], block, piece).wait_recv()

        def some(place, carry):
            part = pl.ds(pl.multiple_of(place * chunk * 2, chunk * 2), chunk * 2)
            mine = full[piece].reshape(features, width)
            theirs = upper[piece].reshape(features, width)
            value = product(factor_high[part, :], mine) + product(factor_low[part, :], mine)
            value = value - own_scales[part, 2:3] * full[piece, group, part, :].astype(jnp.float32)
            value = value + product(cross_high[part, :], theirs) + product(cross_low[part, :], theirs)
            value = value - own_scales[part, 1:2] * upper[piece, group, part, :].astype(jnp.float32)
            for side in range(2):
                inner = slice(side * chunk, (side + 1) * chunk)
                away[piece, 2 * place + side] = value[inner].astype(jnp.bfloat16)
            return carry

        lax.fori_loop(0, layers // 2, some, 0)
        for step in range(layers - 1, 0, -1):
            relay_copy(0, piece, step).start()
        away_in[piece, layer] = away[piece, layer]

    def block_of(place):
        return pl.ds(pl.multiple_of(place * rows, rows), rows)

    def add(way, piece, place, more):
        value = product(lent[block_of(place), :], initial[:, cut(piece)])
        if more:
            value = value + sums_in[way, piece, place].astype(jnp.float32)
        sums[piece, place] = value.astype(jnp.bfloat16)

    lower = Sums(
        "dp",
        lambda piece, owner: sums.at[piece, owner],
        lambda way, piece, owner: sums_in.at[way, piece, owner],
        sum_send,
        sum_recv,
    )

    def join(piece):
        lower.close(piece)
        value = product(lent[block_of(group), :], initial[:, cut(piece)])
        for way in (0, 1):
            value = value + sums_in[way, piece, group].astype(jnp.float32)
        for place in range(layers):
            part = value[place * chunk : (place + 1) * chunk]
            lowered[piece, place] = part.astype(jnp.bfloat16)
        for step in range(layers - 1, 0, -1):
            relay_copy(1, piece, step).start()
        lowered_in[piece, layer] = lowered[piece, layer]

    def correct(piece):
        for step in range(layers - 1, 0, -1):
            relay_copy(0, piece, step).wait_recv()
            relay_copy(1, piece, step).wait_recv()
        part = cut(piece)

        def wide(ref, place):
            return ref[place, :, part].astype(jnp.float32)

        passed = None
        for place in range(layers):
            target = wide(grads, place) - scales[place, :, 0:1] * wide(solved, place)
            if place < layers - 1:
                target = target - scales[place, :, 1:2] * wide(solved, place + 1)
            target = target - away_in[piece, place].astype(jnp.float32)
            if place:
                target = target - scales[place - 1, :, 1:2] * wide(solved, place - 1)
                target = target - lowered_in[piece, place - 1].astype(jnp.float32)
                target = target - passed
            value = target / scales[place, :, 0:1]
            scaled[place] = value
            passed = scales[place, :, 1:2] * value
        result = value
        fixed[piece, layers - 1] = result.astype(jnp.bfloat16)
        for place in range(layers - 2, -1, -1):
            ratio = scales[place, :, 1:2] / scales[place, :, 0:1]
            result = scaled[place] - ratio * result
            fixed[piece, place] = result.astype(jnp.bfloat16)
        for step in range(layers - 1, 0, -1):
            relay_copy(2, piece, step).start()
        fixed_in[piece, layer] = fixed[piece, layer]

    stores = []

    def update(piece):
        for step in range(layers - 1, 0, -1):
            relay_copy(2, piece, step).wait_recv()
        part = cut(piece)

        def some(place, carry):
            inner = pl.ds(pl.multiple_of(place * chunk, chunk), chunk)
            change = initial[inner, part].astype(jnp.float32) + fixed_in[piece, place].astype(
                jnp.float32
            )
            moment = MOMENTUM * moments[inner, part].astype(jnp.float32) * powers[inner, 0:1]
            moment = moment + (1.0 - MOMENTUM) * change
            moments_new[inner, part] = (moment * powers[inner, 1:2]).astype(jnp.bfloat16)
            weights = master[inner, part] - STEP_SIZE * moment
            master_new[inner, part] = weights
            replicas[piece, inner, :] = weights.astype(jnp.bfloat16)
            return carry

        lax.fori_loop(0, layers, some, 0)
        last.begin([piece])
        for place, (source, target) in enumerate(
            (
                (replicas.at[piece], replicas_out.at[group, :, part]),
                (master_new.at[:, part], master_out.at[:, part]),
                (moments_new.at[:, part], moments_out.at[:, part]),
            )
        ):
            stores.append(pltpu.make_async_copy(source, target, store_sem.at[place, piece]))
            stores[-1].start()

    far = groups - 1
    lane = lax.broadcasted_iota(jnp.int32, (SCALE_BLOCK, 128), 1)
    for place in range(rows // SCALE_BLOCK):
        power = jnp.full((SCALE_BLOCK, 128), exponents[0, place].astype(jnp.float32))
        powers[place * SCALE_BLOCK : (place + 1) * SCALE_BLOCK, :] = jnp.exp2(
            jnp.where(lane == 0, power, -power)
        )
    for way, end in ((0, 0), (1, groups - 1)):

        @pl.when(group == end)
        def _():
            for piece in range(PIECES):
                sums_in[way, piece, end] = jnp.zeros_like(sums_in[way, piece, end])

    for load in loads[1:7] + ready:
        load.wait()
    tasks = dict(
        begin=begin,
        meet=lambda piece: first.arrive(1, [piece], lift),
        carry=lambda piece: [first.arrive(hop, [piece], lift) for hop in range(2, far)],
        end=lambda piece: first.arrive(far, [piece], lift),
        lend=lambda piece: lower.begin(piece, add),
        away=lambda piece: [lower.step(piece, distance, add) for distance in range(far - 1, 1, -1)],
        near=lambda piece: lower.step(piece, 1, add),
        multiply=multiply,
        join=join,
        correct=correct,
        update=update,
        first=lambda piece: last.arrive(1, [piece]),
        middle=lambda piece: [last.arrive(hop, [piece]) for hop in range(2, far)],
        final=lambda piece: last.arrive(far, [piece]),
    )
    for entry in ORDER:
        name, *pieces = entry.split()
        if entry == "correct 0":
            for load in loads[7:]:
                load.wait()
        for piece in pieces:
            tasks[name](int(piece))

    for piece in range(PIECES):
        for step in range(1, layers):
            for which in range(3):
                relay_copy(which, piece, step).wait_send()

        if piece:

            @pl.when(layer > 0)
            def _():
                for block in range(groups):
                    lift_copy(full.at[piece, block], block, piece).wait_send()

    first.finish(range(1, PIECES))
    lower.finish(PIECES)
    last.finish()
    for store in stores:
        store.wait()


def back(exponents, matrices, initial, full_first, upper_first, next_first, grads, solved, scales, own_scales, moments, master):
    layers, groups = lax.axis_size("layer"), lax.axis_size("dp")
    rows, columns = initial.shape
    features = matrices[0].shape[1]
    chunk, width = rows // layers, columns // PIECES
    half, full = jnp.bfloat16, jnp.float32
    dma = pltpu.SemaphoreType.DMA
    shape = jax.ShapeDtypeStruct
    swapped = pltpu.VMEM((PIECES, layers, chunk, width), half)
    return pl.pallas_call(
        back_kernel,
        out_shape=[
            shape((rows, columns), half),
            shape((rows, columns), full),
            shape((groups, rows, columns), half),
        ],
        in_specs=[pl.BlockSpec(memory_space=pltpu.SMEM)]
        + [pl.BlockSpec(memory_space=pl.ANY)] * 15,
        out_specs=[pl.BlockSpec(memory_space=pl.ANY)] * 3,
        scratch_shapes=[pltpu.VMEM((rows, features), half)] * 4
        + [pltpu.VMEM((features, rows), half)]
        + [
            pltpu.VMEM((rows, columns), half),
            pltpu.VMEM((layers, chunk, columns), half),
            pltpu.VMEM((layers, chunk, columns), half),
            pltpu.VMEM((layers, chunk, 128), full),
            pltpu.VMEM((rows, 128), full),
            pltpu.VMEM((rows, columns), half),
            pltpu.VMEM((rows, 128), full),
            pltpu.VMEM((rows, columns), full),
            pltpu.VMEM((PIECES, groups, rows, width), half),
            pltpu.VMEM((PIECES, groups, rows, width), half),
            pltpu.VMEM((PIECES, groups, rows, width), half),
            pltpu.VMEM((2, PIECES, groups, rows, width), half),
        ]
        + [swapped] * 4
        + [pltpu.VMEM((layers, chunk, width), full)]
        + [swapped] * 2
        + [
            pltpu.VMEM((rows, columns), half),
            pltpu.VMEM((rows, columns), full),
            pltpu.VMEM((PIECES, rows, width), half),
        ]
        + [dma((2, groups - 1, PIECES))] * 2
        + [dma((2, PIECES, groups))] * 2
        + [dma((2, groups - 1, PIECES))] * 2
        + [dma((PIECES, groups))] * 2
        + [dma((layers - 1, PIECES))] * 6
        + [dma((14 + groups,)), dma((3, PIECES))],
        compiler_params=pltpu.CompilerParams(
            collective_id=1, has_side_effects=True, vmem_limit_bytes=58 << 20
        ),
        cost_estimate=pl.CostEstimate(
            flops=10 * features * rows * columns, bytes_accessed=300_000_000, transcendentals=0
        ),
        name="back",
    )(
        exponents, *matrices, initial, full_first, upper_first, next_first, grads, solved, scales, own_scales,
        moments, master,
    )


def body(activations, factor_old, cross_old, gradients, moments, exponents, master):
    layers, groups = lax.axis_size("layer"), lax.axis_size("dp")
    row_count, features = factor_old.shape[1:]
    columns = gradients.shape[2]
    chunk = row_count // layers
    fresh_weight = (1.0 - FACTOR_DECAY) / (activations.shape[1] * groups)
    factor_new, cross_new, *rest = front(
        fresh_weight,
        activations[0],
        gradients[0].reshape(layers, chunk, columns),
        factor_old[0],
        cross_old[0],
    )
    *matrices, initial, full_first, upper_first, next_first, grad_swapped, initial_swapped, scales, own_scales = rest
    moments_new, master_new, replicas = back(
        exponents,
        matrices,
        initial.reshape(row_count, columns),
        full_first.reshape(groups, row_count, -1),
        upper_first.reshape(groups, row_count, -1),
        next_first.reshape(2, row_count, -1),
        grad_swapped,
        initial_swapped,
        scales,
        own_scales,
        moments[0],
        master[0],
    )
    replicas = replicas.reshape(features, columns)
    return (factor_new[None], cross_new[None], moments_new[None], master_new[None], replicas[None])


def solution(mesh):
    return jax.shard_map(
        body,
        mesh=mesh,
        in_specs=(
            P("layer", "dp", None),
            P("layer", "dp", None),
            P("layer", "dp", None),
            P("layer", "dp", None),
            P("layer", "dp", None),
            P("layer", "dp"),
            P("layer", "dp", None),
        ),
        out_specs=(
            P("layer", "dp", None),
            P("layer", "dp", None),
            P("layer", "dp", None),
            P("layer", "dp", None),
            P("layer", None, None),
        ),
        check_vma=False,
    )
```
